32 devices in a mesh: dp: 4 (over z), seq: 8 (over y, x, core).
Axes of the slice: x: 2, y: 2, z: 4, core: 2. Of those that a mesh axis runs over, the one named last changes fastest.
Arguments:
- hidden_in: bfloat16 [4, 2048, 1024], P('dp', 'seq'), may hold values from -6 to 6
- out_cotangent: bfloat16 [4, 2048, 1024], P('dp', 'seq'), may hold values from -6 to 6
- norm_gain: float32 [1024], P(('dp', 'seq')), may hold values from 0.5 to 1.5
- norm_shift: float32 [1024], P(('dp', 'seq')), may hold values from -1.75 to 1.75
- attend_in: float32 [1024, 3072], P(('dp', 'seq')), may hold values from -0.1875 to 0.1875
- attend_out: float32 [1024, 1024], P(('dp', 'seq')), may hold values from -0.75 to 0.75
- expand_weight: float32 [1024, 4096], P(('dp', 'seq')), may hold values from -0.1875 to 0.1875
- expand_bias: float32 [4096], P(('dp', 'seq')), may hold values from -1.75 to 1.75
- reduce_weight: float32 [4096, 1024], P(('dp', 'seq')), may hold values from -0.09375 to 0.09375
- reduce_bias: float32 [1024], P(('dp', 'seq')), may hold values from -1.75 to 1.75
- gain_moment: float32 [1024], P(('dp', 'seq')), may hold values from -24 to 24
- shift_moment: float32 [1024], P(('dp', 'seq')), may hold values from -24 to 24
- inward_moment: float32 [1024, 3072], P(('dp', 'seq')), may hold values from -24 to 24
- outward_moment: float32 [1024, 1024], P(('dp', 'seq')), may hold values from -24 to 24
- expand_moment: float32 [1024, 4096], P(('dp', 'seq')), may hold values from -24 to 24
- expbias_moment: float32 [4096], P(('dp', 'seq')), may hold values from -24 to 24
- reduce_moment: float32 [4096, 1024], P(('dp', 'seq')), may hold values from -24 to 24
- redbias_moment: float32 [1024], P(('dp', 'seq')), may hold values from -24 to 24
- learn_rate: float32 [1], replicated, may hold values from 0.01 to 0.04
- decay_rate: float32 [1], replicated, may hold values from 0.05 to 0.2
Outputs:
- hidden_out: bfloat16 [4, 2048, 1024], P('dp', 'seq')
- hidden_grad: bfloat16 [4, 2048, 1024], P('dp', 'seq')
- gain_momentum: float32 [1024], P(('dp', 'seq'))
- shift_momentum: float32 [1024], P(('dp', 'seq'))
- inward_momentum: float32 [1024, 3072], P(('dp', 'seq'))
- outward_momentum: float32 [1024, 1024], P(('dp', 'seq'))
- expand_momentum: float32 [1024, 4096], P(('dp', 'seq'))
- expbias_momentum: float32 [4096], P(('dp', 'seq'))
- reduce_momentum: float32 [4096, 1024], P(('dp', 'seq'))
- redbias_momentum: float32 [1024], P(('dp', 'seq'))
- updated_gain: float32 [1024], P(('dp', 'seq'))
- updated_shift: float32 [1024], P(('dp', 'seq'))
- updated_in: float32 [1024, 3072], P(('dp', 'seq'))
- updated_out: float32 [1024, 1024], P(('dp', 'seq'))
- updated_expand: float32 [1024, 4096], P(('dp', 'seq'))
- updated_expbias: float32 [4096], P(('dp', 'seq'))
- updated_reduce: float32 [4096, 1024], P(('dp', 'seq'))
- updated_redbias: float32 [1024], P(('dp', 'seq'))
The draws below stay inside these ranges and needn't reach their ends.
All inputs are finite; a program needn't handle non-finite values.
Results may differ from the reference program's by a relative error of at most 0.011.
Values may be sent and summed in bfloat16 or wider, within the bound.
A program may use at most 320 MiB of HBM per device.

```python
import math
import jax
import jax.numpy as jnp
from jax import lax

D = 1024
H = 16
HD = 64
ROT = 32
FF = 4096
SEQ_LEN = 2048
SEQS = 4


def block_levels(stream_key, extent, pieces, least, largest):
    level, own = 1.0, jax.random.fold_in(stream_key, 6)
    for axis_at, blocks in pieces:
        heights = jnp.exp(jax.random.uniform(jax.random.fold_in(own, axis_at), (blocks,), jnp.float32, least / len(pieces), largest / len(pieces)))
        level = level * jnp.repeat(heights, extent[axis_at] // blocks).reshape([-1 if axis == axis_at else 1 for axis in range(len(extent))])
    return level


def noise(key, shape, scale, most, shards=(), kind=jnp.bfloat16):
    drawn = jax.random.normal(key, shape, jnp.float32) * scale
    if len(shards) > 0:
        drawn = block_levels(key, shape, shards, -0.22, 0.18) * drawn
    return jnp.clip(drawn, min=-most, max=most).astype(kind)


def setup_inputs(seed: int = 0) -> dict:
    keys = jax.random.split(jax.random.key(seed), 21)
    return {
        "hidden_in": noise(keys[0], (SEQS, SEQ_LEN, D), 1.0, 6.0, ((0, 4), (1, 8))),
        "out_cotangent": noise(keys[1], (SEQS, SEQ_LEN, D), 1.0, 6.0, ((0, 4), (1, 8))),
        "norm_gain": jnp.clip(1.0 + 0.1 * jax.random.normal(keys[2], (D,), jnp.float32), 0.5, 1.5),
        "norm_shift": noise(keys[3], (D,), 0.3, 1.75, ((0, 32),), jnp.float32),
        "attend_in": noise(keys[4], (D, 3 * D), D ** -0.5, 0.1875, ((0, 32),), jnp.float32),
        "attend_out": noise(keys[5], (D, D), (D // 16) ** -0.5, 0.75, ((0, 32),), jnp.float32),
        "expand_weight": noise(keys[6], (D, FF), D ** -0.5, 0.1875, ((0, 32),), jnp.float32),
        "expand_bias": noise(keys[7], (FF,), 0.3, 1.75, ((0, 32),), jnp.float32),
        "reduce_weight": noise(keys[8], (FF, D), FF ** -0.5, 0.09375, ((0, 32),), jnp.float32),
        "reduce_bias": noise(keys[9], (D,), 0.3, 1.75, ((0, 32),), jnp.float32),
        "gain_moment": noise(keys[10], (D,), 4.0, 24.0, ((0, 32),), jnp.float32),
        "shift_moment": noise(keys[11], (D,), 4.0, 24.0, ((0, 32),), jnp.float32),
        "inward_moment": noise(keys[12], (D, 3 * D), 4.0, 24.0, ((0, 32),), jnp.float32),
        "outward_moment": noise(keys[13], (D, D), 4.0, 24.0, ((0, 32),), jnp.float32),
        "expand_moment": noise(keys[14], (D, FF), 4.0, 24.0, ((0, 32),), jnp.float32),
        "expbias_moment": noise(keys[15], (FF,), 4.0, 24.0, ((0, 32),), jnp.float32),
        "reduce_moment": noise(keys[16], (FF, D), 4.0, 24.0, ((0, 32),), jnp.float32),
        "redbias_moment": noise(keys[17], (D,), 4.0, 24.0, ((0, 32),), jnp.float32),
        "learn_rate": jnp.clip(jnp.exp(jax.random.uniform(keys[18], (1,), jnp.float32, math.log(0.01), math.log(0.04))), 0.01, 0.04),
        "decay_rate": jnp.clip(jax.random.uniform(keys[19], (1,), jnp.float32, 0.05, 0.2), 0.05, 0.2),
    }


@jax.custom_vjp
def low(v):
    return lax.optimization_barrier(v.astype(jnp.bfloat16)).astype(jnp.float32)

@jax.custom_vjp
def low_back(v):
    return v

def low_keep(v):
    return (low(v), None)

def low_pass(kept, grad):
    return (grad,)

def back_keep(v):
    return (v, None)

def back_low(kept, grad):
    return (low(grad),)
low.defvjp(low_keep, low_pass)
low_back.defvjp(back_keep, back_low)
highest = lax.Precision.HIGHEST
epsilon = 1e-05
masked_score = -1e+30

def rotary(block, positions, direction):
    half_rot = ROT // 2
    frequency = 10000.0 ** (-2.0 * jnp.arange(half_rot, dtype=jnp.float32) / ROT)
    angles = direction * positions[:, None] * frequency[None, :]
    cosine = jnp.cos(angles)[:, None, :]
    sine_part = jnp.sin(angles)[:, None, :]
    first_half = block[..., :half_rot]
    second = block[..., half_rot:ROT]
    return jnp.concatenate([first_half * cosine - second * sine_part, second * cosine + first_half * sine_part, block[..., ROT:]], axis=-1)

def block_forward(inputs, norm_gain, norm_shift, attend_in, attend_out, expand_weight, expand_bias, reduce_weight, reduce_bias):
    seq_len = inputs.shape[0]
    row_mean = lax.optimization_barrier(jnp.mean(inputs, axis=-1, keepdims=True))
    centred = inputs - row_mean
    row_var = lax.optimization_barrier(jnp.mean(centred * centred, axis=-1, keepdims=True))
    normed = low(centred * lax.rsqrt(row_var + epsilon) * low(norm_gain) + low(norm_shift))
    joined = low_back(jnp.dot(normed, low(attend_in), precision=highest))
    positions = jnp.arange(seq_len, dtype=jnp.float32)
    query = low(rotary(joined[:, :D].reshape(seq_len, H, HD), positions, 1.0))
    keyed = low(rotary(joined[:, D:2 * D].reshape(seq_len, H, HD), positions, 1.0))
    valued = low(joined[:, 2 * D:].reshape(seq_len, H, HD))
    scores = low_back(jnp.einsum('qhd,khd->hqk', query, keyed, precision=highest) * HD ** (-0.5))
    causal = jnp.arange(seq_len)[None, :] <= jnp.arange(seq_len)[:, None]
    scores = jnp.where(causal[None], scores, masked_score)
    weights = low(jax.nn.softmax(scores, axis=-1))
    attended = jnp.einsum('hqk,khd->qhd', weights, valued, precision=highest).reshape(seq_len, D)
    attended = low(low_back(attended))
    expanded = low_back(jnp.dot(normed, low(expand_weight), precision=highest) + low(expand_bias))
    activated = low(jax.nn.gelu(expanded, approximate=True))
    branch_attn = jnp.dot(attended, low(attend_out), precision=highest)
    branch_mlp = jnp.dot(activated, low(reduce_weight), precision=highest) + low(reduce_bias)
    return inputs + branch_attn + branch_mlp

def reference(hidden_in, out_cotangent, norm_gain, norm_shift, attend_in, attend_out, expand_weight, expand_bias, reduce_weight, reduce_bias, gain_moment, shift_moment, inward_moment, outward_moment, expand_moment, expbias_moment, reduce_moment, redbias_moment, learn_rate, decay_rate):
    params = (norm_gain, norm_shift, attend_in, attend_out, expand_weight, expand_bias, reduce_weight, reduce_bias)
    moments = (gain_moment, shift_moment, inward_moment, outward_moment, expand_moment, expbias_moment, reduce_moment, redbias_moment)

    def one_sequence(running, operands):
        sequence, cotangent = operands
        outputs, pullback = jax.vjp(block_forward, sequence.astype(jnp.float32), norm_gain, norm_shift, attend_in, attend_out, expand_weight, expand_bias, reduce_weight, reduce_bias)
        gradients = pullback(cotangent.astype(jnp.float32))
        summed = tuple((earlier + addend for earlier, addend in zip(running, gradients[1:])))
        return (summed, (outputs.astype(jnp.bfloat16), gradients[0].astype(jnp.bfloat16)))
    initial = tuple((jnp.zeros_like(weight_now) for weight_now in params))
    totals, (hidden_out, hidden_grad) = lax.scan(one_sequence, initial, (hidden_in, out_cotangent))
    step_rate = learn_rate[0]
    decay_now = decay_rate[0]
    momenta = [0.5 * moment + 0.5 * (summed_grad / SEQS) for moment, summed_grad in zip(moments, totals)]
    updated = [(1.0 - decay_now) * weight_now - step_rate * momentum for weight_now, momentum in zip(params, momenta)]
    return (hidden_out, hidden_grad, momenta[0], momenta[1], momenta[2], momenta[3], momenta[4], momenta[5], momenta[6], momenta[7], updated[0], updated[1], updated[2], updated[3], updated[4], updated[5], updated[6], updated[7])
```

```python
import jax
import jax.numpy as jnp
import numpy as np
from jax import lax
from jax.experimental import pallas as pl
from jax.experimental.pallas import tpu as pltpu
from jax.sharding import PartitionSpec as P

D = 1024
H = 16
HD = 64
ROT = 32


epsilon = 1e-05
masked_score = -1e30


def rotary(block, positions, direction):
    half_rot = ROT // 2
    frequency = 10000.0 ** (-2.0 * jnp.arange(half_rot, dtype=jnp.float32) / ROT)
    angles = direction * positions[:, None] * frequency[None, :]
    cosine = jnp.cos(angles)[:, None, :]
    sine_part = jnp.sin(angles)[:, None, :]
    first_half = block[..., :half_rot]
    second = block[..., half_rot:ROT]
    return jnp.concatenate(
        [
            first_half * cosine - second * sine_part,
            second * cosine + first_half * sine_part,
            block[..., ROT:],
        ],
        axis=-1,
    )


def gelu_tanh(values):
    return jax.nn.gelu(values, approximate=True)


def gelu_back(expanded, upstream):
    unused_out, pullback = jax.vjp(gelu_tanh, expanded)
    return pullback(upstream)[0]


def heads_of(rows):
    return rows.reshape(rows.shape[0], H, HD)


def scores_of(query_rows, key_rows):
    score_scale = HD ** (-0.5)
    return (
        jnp.einsum(
            "qhd,khd->hqk",
            heads_of(query_rows),
            heads_of(key_rows),
            preferred_element_type=jnp.float32,
        )
        * score_scale
    )


def shards(
    hidden_in,
    out_cotangent,
    norm_gain,
    norm_shift,
    attend_in,
    attend_out,
    expand_weight,
    expand_bias,
    reduce_weight,
    reduce_bias,
    gain_moment,
    shift_moment,
    inward_moment,
    outward_moment,
    expand_moment,
    expbias_moment,
    reduce_moment,
    redbias_moment,
    learn_rate,
    decay_rate,
):
    score_scale = HD ** (-0.5)
    gain_low, shift_low, inward_mat, outward_mat, expand_mat, expand_vec, reduce_mat, reduce_vec = (
        lax.all_gather(norm_gain.astype(jnp.bfloat16), ("dp", "seq"), axis=0, tiled=True),
        lax.all_gather(norm_shift.astype(jnp.bfloat16), ("dp", "seq"), axis=0, tiled=True),
        lax.all_gather(attend_in.astype(jnp.bfloat16), ("dp", "seq"), axis=0, tiled=True),
        lax.all_gather(attend_out.astype(jnp.bfloat16), ("dp", "seq"), axis=0, tiled=True),
        lax.all_gather(expand_weight.astype(jnp.bfloat16), ("dp", "seq"), axis=0, tiled=True),
        lax.all_gather(expand_bias.astype(jnp.bfloat16), ("dp", "seq"), axis=0, tiled=True),
        lax.all_gather(reduce_weight.astype(jnp.bfloat16), ("dp", "seq"), axis=0, tiled=True),
        lax.all_gather(reduce_bias.astype(jnp.bfloat16), ("dp", "seq"), axis=0, tiled=True),
    )
    seq_count, block_len, model_width = hidden_in.shape
    row_count = seq_count * block_len
    full_len = block_len * lax.axis_size("seq")
    seq_start = lax.axis_index("seq") * block_len
    query_index = seq_start + jnp.arange(block_len, dtype=jnp.int32)
    key_index = jnp.arange(full_len, dtype=jnp.int32)
    causal = key_index[None, :] <= query_index[:, None]
    positions = query_index.astype(jnp.float32)
    inputs = hidden_in.astype(jnp.float32).reshape(row_count, model_width)
    row_mean = jnp.mean(inputs, axis=-1, keepdims=True)
    centred = inputs - row_mean
    row_var = jnp.mean(centred * centred, axis=-1, keepdims=True)
    inverse = lax.rsqrt(row_var + epsilon)
    unit_rows = centred * inverse
    gain_full = gain_low.astype(jnp.float32)
    normed = (unit_rows * gain_full + shift_low.astype(jnp.float32)).astype(jnp.bfloat16)
    joined = jnp.dot(normed, inward_mat, preferred_element_type=jnp.float32).reshape(
        seq_count, block_len, 3 * D
    )
    query = (
        rotary(joined[..., :D].reshape(seq_count, block_len, H, HD), positions, 1.0)
        .astype(jnp.bfloat16)
        .reshape(seq_count, block_len, D)
    )
    keyed = (
        rotary(joined[..., D : 2 * D].reshape(seq_count, block_len, H, HD), positions, 1.0)
        .astype(jnp.bfloat16)
        .reshape(seq_count, block_len, D)
    )
    valued = joined[..., 2 * D :].astype(jnp.bfloat16)
    key_all, value_all = (
        lax.all_gather(keyed, "seq", axis=1, tiled=True),
        lax.all_gather(valued, "seq", axis=1, tiled=True),
    )

    def attend(operands):
        query_seq, key_seq, value_seq = operands
        scores = jnp.where(causal[None], scores_of(query_seq, key_seq), masked_score)
        row_max = jnp.max(scores, axis=-1, keepdims=True)
        log_total = row_max + jnp.log(jnp.sum(jnp.exp(scores - row_max), axis=-1, keepdims=True))
        weights = jnp.exp(scores - log_total).astype(jnp.bfloat16)
        mixed = jnp.einsum(
            "hqk,khd->qhd", weights, heads_of(value_seq), preferred_element_type=jnp.float32
        )
        return (mixed.reshape(-1, D).astype(jnp.bfloat16), jnp.transpose(log_total[..., 0]))

    attended, log_totals = lax.map(attend, (query, key_all, value_all))
    expanded = jnp.dot(normed, expand_mat, preferred_element_type=jnp.float32) + expand_vec.astype(
        jnp.float32
    )
    activated = gelu_tanh(expanded).astype(jnp.bfloat16)
    flat_attn = attended.reshape(row_count, D)
    result = (
        inputs
        + jnp.dot(flat_attn, outward_mat, preferred_element_type=jnp.float32)
        + jnp.dot(activated, reduce_mat, preferred_element_type=jnp.float32)
        + reduce_vec.astype(jnp.float32)
    )
    hidden_out = result.astype(jnp.bfloat16).reshape(seq_count, block_len, D)
    upstream = out_cotangent.reshape(row_count, D)
    grad_outward = jnp.einsum("rd,re->de", flat_attn, upstream, preferred_element_type=jnp.float32)
    grad_reduce = jnp.einsum("rf,re->fe", activated, upstream, preferred_element_type=jnp.float32)
    grad_redbias = jnp.sum(upstream.astype(jnp.float32), axis=0)
    attn_back = (
        jnp.einsum("re,de->rd", upstream, outward_mat, preferred_element_type=jnp.float32)
        .astype(jnp.bfloat16)
        .reshape(seq_count, block_len, D)
    )
    act_back = jnp.einsum("re,fe->rf", upstream, reduce_mat, preferred_element_type=jnp.float32)
    expand_back = gelu_back(expanded, act_back).astype(jnp.bfloat16)
    grad_expbias = jnp.sum(expand_back.astype(jnp.float32), axis=0)
    grad_expand = jnp.einsum("rd,rf->df", normed, expand_back, preferred_element_type=jnp.float32)
    norm_back = jnp.einsum("rf,df->rd", expand_back, expand_mat, preferred_element_type=jnp.float32)

    def query_side(query_seq, key_seq, value_seq, back_seq, total_seq):
        scores = jnp.where(causal[None], scores_of(query_seq, key_seq), masked_score)
        probs = jnp.exp(scores - jnp.transpose(total_seq)[:, :, None])
        prob_grad = jnp.einsum(
            "qhd,khd->hqk",
            heads_of(back_seq),
            heads_of(value_seq),
            preferred_element_type=jnp.float32,
        )
        row_delta = jnp.sum(probs * prob_grad, axis=-1, keepdims=True)
        score_grad = (probs * (prob_grad - row_delta)).astype(jnp.bfloat16)
        query_grad = (
            jnp.einsum(
                "hqk,khd->qhd", score_grad, heads_of(key_seq), preferred_element_type=jnp.float32
            )
            * score_scale
        )
        return (probs, score_grad, query_grad, row_delta)

    def attend_back(operands):
        query_seq, key_seq, value_seq, back_seq, total_seq = operands
        probs, score_grad, query_grad, row_delta = query_side(
            query_seq, key_seq, value_seq, back_seq, total_seq
        )
        key_grad = (
            jnp.einsum(
                "hqk,qhd->khd", score_grad, heads_of(query_seq), preferred_element_type=jnp.float32
            )
            * score_scale
        )
        value_grad = jnp.einsum(
            "hqk,qhd->khd",
            probs.astype(jnp.bfloat16),
            heads_of(back_seq),
            preferred_element_type=jnp.float32,
        )
        return (query_grad, key_grad.reshape(-1, D), value_grad.reshape(-1, D))

    query_grads, key_terms, value_terms = lax.map(
        attend_back, (query, key_all, value_all, attn_back, log_totals)
    )
    key_grads, value_grads = (
        lax.psum_scatter(key_terms, "seq", scatter_dimension=1, tiled=True),
        lax.psum_scatter(value_terms, "seq", scatter_dimension=1, tiled=True),
    )
    query_turned = rotary(query_grads, positions, -1.0).reshape(seq_count, block_len, D)
    key_turned = rotary(key_grads.reshape(seq_count, block_len, H, HD), positions, -1.0).reshape(
        seq_count, block_len, D
    )
    joined_back = (
        jnp.concatenate([query_turned, key_turned, value_grads], axis=-1)
        .astype(jnp.bfloat16)
        .reshape(row_count, 3 * D)
    )
    grad_inward = jnp.einsum("rd,re->de", normed, joined_back, preferred_element_type=jnp.float32)
    norm_back = norm_back + jnp.einsum(
        "re,de->rd", joined_back, inward_mat, preferred_element_type=jnp.float32
    )
    grad_gain = jnp.sum(norm_back * unit_rows, axis=0)
    grad_shift = jnp.sum(norm_back, axis=0)
    unit_back = norm_back * gain_full
    input_back = inverse * (
        unit_back
        - jnp.mean(unit_back, axis=-1, keepdims=True)
        - unit_rows * jnp.mean(unit_back * unit_rows, axis=-1, keepdims=True)
    ) + upstream.astype(jnp.float32)
    hidden_grad = input_back.astype(jnp.bfloat16).reshape(seq_count, block_len, D)
    totals = (
        lax.psum_scatter(grad_gain, ("dp", "seq"), scatter_dimension=0, tiled=True),
        lax.psum_scatter(grad_shift, ("dp", "seq"), scatter_dimension=0, tiled=True),
        lax.psum_scatter(grad_inward, ("dp", "seq"), scatter_dimension=0, tiled=True),
        lax.psum_scatter(grad_outward, ("dp", "seq"), scatter_dimension=0, tiled=True),
        lax.psum_scatter(grad_expand, ("dp", "seq"), scatter_dimension=0, tiled=True),
        lax.psum_scatter(grad_expbias, ("dp", "seq"), scatter_dimension=0, tiled=True),
        lax.psum_scatter(grad_reduce, ("dp", "seq"), scatter_dimension=0, tiled=True),
        lax.psum_scatter(grad_redbias, ("dp", "seq"), scatter_dimension=0, tiled=True),
    )
    seq_total = seq_count * lax.axis_size("dp")
    step_rate = learn_rate[0]
    decay_now = decay_rate[0]
    params = (
        norm_gain,
        norm_shift,
        attend_in,
        attend_out,
        expand_weight,
        expand_bias,
        reduce_weight,
        reduce_bias,
    )
    moments = (
        gain_moment,
        shift_moment,
        inward_moment,
        outward_moment,
        expand_moment,
        expbias_moment,
        reduce_moment,
        redbias_moment,
    )
    momenta = [
        0.5 * moment + 0.5 * (summed_grad / seq_total)
        for moment, summed_grad in zip(moments, totals)
    ]
    updated = [
        (1.0 - decay_now) * weight_now - step_rate * momentum
        for weight_now, momentum in zip(params, momenta)
    ]
    return (
        hidden_out,
        hidden_grad,
        momenta[0],
        momenta[1],
        momenta[2],
        momenta[3],
        momenta[4],
        momenta[5],
        momenta[6],
        momenta[7],
        updated[0],
        updated[1],
        updated[2],
        updated[3],
        updated[4],
        updated[5],
        updated[6],
        updated[7],
    )


F32 = jnp.float32
BF16 = jnp.bfloat16
MESH = pl.DeviceIdType.MESH
NZ = 4
NP = 8
NT = (((1,), (1,)), ((), ()))
TN = (((0,), (0,)), ((), ()))


def dot(a, b):
    return jnp.dot(a, b, preferred_element_type=F32)


def dot_nt(a, b):
    return lax.dot_general(a, b, NT, preferred_element_type=F32)


def dot_tn(a, b):
    return lax.dot_general(a, b, TN, preferred_element_type=F32)


def aligned(value, unit):
    return pl.multiple_of(value, unit)


def gelu_pair(e):
    square = e * e
    t = jnp.tanh(e * (GELU_C + (GELU_C * GELU_A) * square))
    half = 0.5 + 0.5 * t
    slope = half + (0.5 * e) * (1.0 - t * t) * (GELU_C + (3.0 * GELU_C * GELU_A) * square)
    return e * half, slope


GELU_C = 0.7978845608028654
GELU_A = 0.044715


def block_kernel(rows, *refs):
    (
        x_ref, dy_ref, gain_ref, shift_ref, win_ref, wout_ref, wexp_ref, ebias_ref, wred_ref, rbias_ref,
        mgain_ref, mshift_ref, min_ref, mout_ref, mexp_ref, mebias_ref, mred_ref, mrbias_ref,
        rate_ref, decay_ref, cosr_ref, sinr_ref, cosb_ref, sinb_ref,
        hout_ref, hgrad_ref,
        ngain_ref, nshift_ref, nin_ref, nout_ref, nexp_ref, nebias_ref, nred_ref, nrbias_ref,
        ugain_ref, ushift_ref, uin_ref, uout_ref, uexp_ref, uebias_ref, ured_ref, urbias_ref,
        xg, dyg, xn, win, wexp, wred, wout, wz, pin, pexp,
        q_s, k_s, vx, o_s, do_s, dkt, dvt, dfused, sbuf, mref, acc, dqacc,
        act_s, de_s, pdn, sib_o, sib_d, r1_o, r2_o, r1_d, r2_d,
        gin, gexp, gred, gout, gz, rz_in, rz_exp, rz_red, rz_out, ra_in, ra_exp,
        vt, vecs, geb, sv, rv, zt, rzv,
        a2a_s, a2a_r, ag_s, ag_r, z_s, z_r, vz_s, vz_r, vp_s, vp_r, wo_s, wo_r,
        rs_s, rs_r, zr_s, zr_r, go_s, go_r, b_s, b_r, sp_s, sp_r, sz_s, sz_r,
    ) = refs
    pout = xg
    d = lax.axis_index("dp")
    s = lax.axis_index("seq")
    core = lax.rem(s, 2)
    xbit = lax.rem(lax.div(s, 2), 2)
    ybit = lax.div(s, 4)
    chip = lax.div(s, 2)
    quad = lax.rem(s, 4)

    def peer(m):
        out = s
        if m & 1:
            out = out + (1 - 2 * core)
        if m & 2:
            out = out + 2 * (1 - 2 * xbit)
        if m & 4:
            out = out + 4 * (1 - 2 * ybit)
        return out

    def pair_of(t):
        return 2 * lax.rem(t, 4) + lax.div(t, 4)

    def rc(src, dst, ssem, rsem, dd, ss):
        return pltpu.make_async_remote_copy(
            src_ref=src, dst_ref=dst, send_sem=ssem, recv_sem=rsem,
            device_id=(dd, ss), device_id_type=MESH,
        )

    lanes = lax.broadcasted_iota(jnp.int32, (8, 128), 1)
    zrow = jnp.zeros((1, 96), F32)
    small = jnp.concatenate(
        [
            jnp.concatenate([r[...].astype(BF16).astype(F32), zrow], axis=1)
            for r in (gain_ref, shift_ref, rbias_ref)
        ]
        + [jnp.zeros((5, 128), F32)],
        axis=0,
    )
    small = pltpu.roll(small, 32 * quad, 1)
    rows8 = lax.broadcasted_iota(jnp.int32, (8, 128), 0)
    ebias_row = jnp.broadcast_to(ebias_ref[...].astype(BF16).astype(F32), (8, 128))
    vt[s, d] = jnp.where(rows8 == 3, ebias_row, small)

    own_rows = aligned(32 * (8 * d + s), 32)
    for m in range(NP):
        t = peer(m)
        j = pair_of(t)
        for part in range(3):
            piece = win_ref[:, pl.ds(aligned(128 * j + 1024 * part, 128), 128)].astype(BF16)
            if m == 0:
                win[pl.ds(own_rows, 32), 128 * part : 128 * (part + 1)] = piece
            else:
                pin[m, :, 128 * part : 128 * (part + 1)] = piece
        for e in range(NZ):
            piece = wexp_ref[:, pl.ds(aligned(128 * (8 * e + t), 128), 128)].astype(BF16)
            if m == 0:
                wexp[pl.ds(own_rows, 32), 128 * e : 128 * (e + 1)] = piece
            else:
                pexp[m, :, 128 * e : 128 * (e + 1)] = piece
    wz[d] = wout_ref[...].astype(BF16)
    wred[pl.ds(aligned(128 * d, 128), 128), :] = wred_ref[...].astype(BF16)
    xg[pl.ds(aligned(rows * s, rows), rows), :] = x_ref[...]
    dyg[pl.ds(aligned(rows * s, rows), rows), :] = dy_ref[...]

    barrier = pltpu.get_barrier_semaphore()
    for m in range(1, NP):
        pl.semaphore_signal(barrier, inc=1, device_id=(d, peer(m)), device_id_type=MESH)
    for dz in range(1, NZ):
        pl.semaphore_signal(barrier, inc=1, device_id=(lax.rem(d + dz, NZ), s), device_id_type=MESH)
    pl.semaphore_wait(barrier, NP - 1 + NZ - 1)

    def a2a_msg(which, m):
        src = (pin, pexp)[which].at[m]
        dst = (win, wexp)[which].at[pl.ds(own_rows, 32)]
        return rc(src, dst, a2a_s.at[which, m], a2a_r.at[which, m], d, peer(m))

    def a2a_arrived(which, m):
        dst = (win, wexp)[which].at[pl.ds(aligned(32 * (8 * d + peer(m)), 32), 32)]
        rc((pin, pexp)[which].at[m], dst, a2a_s.at[which, m], a2a_r.at[which, m], d, peer(m)).wait_recv()

    half = rows // 2
    AG = (
        (1, 0, 0, rows), (2, 0, 0, rows), (4, 0, 0, rows),
        (1, 2, 0, rows), (1, 4, 0, rows), (4, 2, half, half), (2, 4, 0, half),
        (1, 6, 0, half), (1, 6, half, half),
    )

    def ag_copy(which, i, incoming):
        to, blk, lo, n = AG[i]
        buf = (xg, dyg)[which]
        at = rows * peer(blk ^ (to if incoming else 0)) + lo
        ref = buf.at[pl.ds(aligned(at, half), n)]
        return rc(ref, ref, ag_s.at[which, i], ag_r.at[which, i], d, peer(to))

    def ag_start(which, i):
        ag_copy(which, i, False).start()

    def ag_arrived(which, i):
        ag_copy(which, i, True).wait_recv()

    ZVIEW = (
        lambda b: win.at[pl.ds(aligned(256 * b, 256), 256)],
        lambda b: wexp.at[pl.ds(aligned(256 * b, 256), 256)],
        lambda b: wred.at[pl.ds(aligned(128 * b, 128), 128)],
        lambda b: wz.at[b],
    )

    def z_direct(dest):
        ok = d != dest
        if dest == NZ - 1:
            ok = ok & (d != 0)
        if dest == 0:
            ok = ok & (d != NZ - 1)
        return ok

    def z_send(a):
        for dest in (3, 0, 2, 1):
            @pl.when(z_direct(dest))
            def _():
                rc(ZVIEW[a](d), ZVIEW[a](d), z_s.at[a, dest], z_r.at[a, d], dest, s).start()

    FWD = ((2, 0, 3), (1, 3, 0))

    def z_wait_block(a, b):
        rc(ZVIEW[a](b), ZVIEW[a](b), z_s.at[a, 4], z_r.at[a, b], d, s).wait_recv()

    def z_forward(a):
        for at, blk, dest in FWD:
            @pl.when(d == at)
            def _():
                z_wait_block(a, blk)
                rc(ZVIEW[a](blk), ZVIEW[a](blk), z_s.at[a, 4], z_r.at[a, blk], dest, s).start()

    def z_arrived(a):
        for b in range(NZ):
            need = d != b
            for at, blk, dest in FWD:
                if blk == b:
                    need = need & (d != at)

            @pl.when(need)
            def _():
                z_wait_block(a, b)

    def z_sent(a):
        for dest in range(NZ):
            @pl.when(z_direct(dest))
            def _():
                rc(ZVIEW[a](d), ZVIEW[a](d), z_s.at[a, dest], z_r.at[a, d], dest, s).wait_send()
        for at, blk, dest in FWD:
            @pl.when(d == at)
            def _():
                rc(ZVIEW[a](blk), ZVIEW[a](blk), z_s.at[a, 4], z_r.at[a, blk], dest, s).wait_send()

    def other(i):
        return lax.rem(d + i, NZ)

    def vz_copy(i, incoming):
        b = lax.rem(d + NZ - i, NZ) if incoming else d
        return rc(vt.at[s, b], vt.at[s, b], vz_s.at[i], vz_r.at[i], other(i), s)

    def vp_copy(m, incoming):
        b = peer(m) if incoming else s
        return rc(vt.at[b], vt.at[b], vp_s.at[m], vp_r.at[m], d, peer(m))

    for i in range(1, NZ):
        vz_copy(i, False).start()
    for m in range(1, NP):
        a2a_msg(0, m).start()
    z_send(3)
    for i in (1, 2, 0):
        ag_start(0, i)
    for m in range(1, NP):
        a2a_msg(1, m).start()

    for i in range(1, NZ):
        vz_copy(i, True).wait_recv()
    for m in range(1, NP):
        vp_copy(m, False).start()
    for m in range(1, NP):
        a2a_arrived(0, m)
    z_send(0)
    for m in range(1, NP):
        a2a_arrived(1, m)
    z_send(1)
    z_send(2)

    for m in range(1, NP):
        vp_copy(m, True).wait_recv()
    for dd in range(NZ):
        for yy in range(2):
            group = 2 * dd + yy
            total = vt[4 * yy, dd]
            for jj in range(1, 4):
                total = total + vt[4 * yy + jj, dd]
            vecs[:, 128 * group : 128 * (group + 1)] = total

    def unit_of(xb):
        xf = xb.astype(F32)
        mu = jnp.mean(xf, axis=1, keepdims=True)
        cen = xf - mu
        var = jnp.mean(cen * cen, axis=1, keepdims=True)
        inv = lax.rsqrt(var + epsilon)
        return cen * inv, inv

    def norm_block(b):
        def step(c, carry):
            at = aligned(rows * b + 64 * c, 64)
            unit, _ = unit_of(xg[pl.ds(at, 64), :])
            xn[pl.ds(at, 64), :] = (unit * vecs[0:1, :] + vecs[1:2, :]).astype(BF16)
            return carry
        lax.fori_loop(0, rows // 64, step, 0)

    lane_b = lax.broadcasted_iota(jnp.int32, (rows, 128), 1)
    low_head = lane_b < HD
    in_head = lax.rem(lane_b, HD)
    first_rot = in_head < ROT // 2
    second_rot = (in_head >= ROT // 2) & (in_head < ROT)

    def turn(block, b, sign):
        cb, sb = cosb_ref[pl.ds(b, 1), :], sinb_ref[pl.ds(b, 1), :]
        cr, sr = cosr_ref[...], sinr_ref[...]
        co = cr * cb - sr * sb
        si = (sr * cb + cr * sb) * sign
        co = jnp.where(in_head < ROT, co, 1.0)
        up = pltpu.roll(block, 128 - ROT // 2, 1)
        down = pltpu.roll(block, ROT // 2, 1)
        mixed = jnp.where(first_rot, -up, down) * si
        mixed = jnp.where(in_head < ROT, mixed, 0.0)
        return block * co + mixed

    ag_arrived(0, 1)
    ag_start(0, 5)
    ag_start(0, 3)
    ag_arrived(0, 2)
    ag_start(0, 6)
    ag_start(0, 4)
    for i in (1, 2, 0):
        ag_start(1, i)
    norm_block(s)
    ag_arrived(0, 0)
    norm_block(peer(1))
    norm_block(peer(2))
    norm_block(peer(4))
    ag_arrived(0, 6)
    ag_start(0, 7)
    ag_arrived(0, 5)
    ag_start(0, 8)
    ag_arrived(0, 3)
    norm_block(peer(3))
    ag_arrived(0, 4)
    norm_block(peer(5))
    norm_block(peer(6))
    ag_arrived(0, 7)
    ag_arrived(0, 8)
    norm_block(peer(7))

    z_forward(3)
    z_arrived(3)

    def wo_copy(m, incoming):
        src = wz.at[lax.rem(peer(m), 4)]
        r = lax.rem(peer(m), 4) if incoming else quad
        dst = wout.at[pl.ds(aligned(32 * r, 32), 32)]
        return rc(src, dst, wo_s.at[m], wo_r.at[m], d, peer(m))

    for m in range(1, 4):
        wo_copy(m, False).start()
    wout[pl.ds(aligned(32 * quad, 32), 32), :] = wz[quad]

    ag_arrived(1, 1)
    ag_start(1, 5)
    ag_start(1, 3)
    ag_arrived(1, 2)
    ag_start(1, 6)
    ag_start(1, 4)

    z_forward(0)
    z_arrived(0)

    def qkv_step(b, carry):
        at = aligned(rows * b, rows)
        joined = dot(xn[pl.ds(at, rows), :], win[...])
        q_s[pl.ds(at, rows), :] = turn(joined[:, :128], b, 1.0).astype(BF16) * jnp.asarray(HD**-0.5, BF16)
        k_s[pl.ds(at, rows), :] = turn(joined[:, 128:256], b, 1.0).astype(BF16)
        vx[pl.ds(at, rows), :128] = joined[:, 256:].astype(BF16)
        vx[pl.ds(at, rows), 128:] = jnp.ones((rows, 128), BF16)
        return carry

    lax.fori_loop(0, NP, qkv_step, 0)
    ag_arrived(1, 6)
    ag_start(1, 7)
    ag_arrived(1, 5)
    ag_start(1, 8)
    for i in (0, 3, 4, 7, 8):
        ag_arrived(1, i)
    for m in range(1, 4):
        wo_copy(m, True).wait_recv()

    def do_step(b, carry):
        at = aligned(rows * b, rows)
        do_s[pl.ds(at, rows), :] = dot_nt(dyg[pl.ds(at, rows), :], wout[...]).astype(BF16)
        return carry

    lax.fori_loop(0, NP, do_step, 0)

    KB = 2 * rows

    def weights_at(h, j):
        return pl.ds(aligned(rows * (NP // 2 * h + j), rows), rows)

    dkt[...] = jnp.zeros_like(dkt)
    dvt[...] = jnp.zeros_like(dvt)

    def attend_step(i, carry):
        at = aligned(rows * i, rows)
        count = lax.div(i, 2) + 1
        qi = q_s[pl.ds(at, rows), :]
        zero = jnp.zeros_like(qi)
        qh = (jnp.where(low_head, qi, zero), jnp.where(low_head, zero, qi))

        def fold(v):
            out = v[:, :128]
            for c in range(1, KB // 128):
                out = jnp.maximum(out, v[:, 128 * c : 128 * (c + 1)])
            return out

        last = count - 1
        ka = aligned(KB * last, KB)
        kj = k_s[pl.ds(ka, KB), :]
        query = at + lax.broadcasted_iota(jnp.int32, (rows, KB), 0)
        key = ka + lax.broadcasted_iota(jnp.int32, (rows, KB), 1)
        for h in range(2):
            sc = jnp.where(key <= query, dot_nt(qh[h], kj), masked_score)
            sbuf[h, last] = sc
            mref[h] = fold(sc)

        def scores(j, c2):
            kk = k_s[pl.ds(aligned(KB * j, KB), KB), :]
            for h in range(2):
                sc = dot_nt(qh[h], kk)
                sbuf[h, j] = sc
                mref[h] = jnp.maximum(mref[h], fold(sc))
            return c2

        lax.fori_loop(0, last, scores, 0)
        top = [jnp.max(mref[h], axis=1, keepdims=True) for h in range(2)]
        for h in range(2):
            mref[h] = jnp.broadcast_to(top[h], (rows, 128))
            acc[h] = jnp.zeros((rows, 256), F32)

        def weigh(j, c2):
            vj = vx[pl.ds(aligned(KB * j, KB), KB), :]
            for h in range(2):
                pj = jnp.exp(sbuf[h, j] - mref[h][:, :1]).astype(BF16)
                act_s[weights_at(h, j), :] = pj
                acc[h] = acc[h] + dot(pj, vj)
            return c2

        lax.fori_loop(0, count, weigh, 0)
        recip = [1.0 / acc[h][:, 128:] for h in range(2)]
        scale = jnp.where(low_head, recip[0], recip[1])
        of = jnp.where(low_head, acc[0][:, :128], acc[1][:, :128]) * scale
        o_s[pl.ds(at, rows), :] = of.astype(BF16)
        doi = do_s[pl.ds(at, rows), :]
        dof = doi.astype(F32)
        prod = dof * of
        delta = (
            jnp.sum(jnp.where(low_head, prod, 0.0), axis=1, keepdims=True),
            jnp.sum(jnp.where(low_head, 0.0, prod), axis=1, keepdims=True),
        )
        for h in range(2):
            mref[h] = jnp.broadcast_to(delta[h], (rows, 128))
            dqacc[h] = jnp.zeros((rows, 128), F32)
        doh = (jnp.where(low_head, doi, zero), jnp.where(low_head, zero, doi))
        dot_t = jnp.transpose(dof * scale).astype(BF16)
        qt = jnp.transpose(qi.astype(F32) * scale).astype(BF16)

        def back(j, c2):
            ja = aligned(KB * j, KB)
            kk = k_s[pl.ds(ja, KB), :]
            vj = vx[pl.ds(ja, KB), :128]
            for h in range(2):
                hs = slice(HD * h, HD * (h + 1))
                pj = act_s[weights_at(h, j), :]
                dp = dot_nt(doh[h], vj)
                ds = (pj.astype(F32) * (dp - mref[h][:, :1])).astype(BF16)
                dqacc[h] = dqacc[h] + dot(ds, kk)
                dkt[hs, pl.ds(ja, KB)] = dkt[hs, pl.ds(ja, KB)] + dot(qt[hs, :], ds)
                dvt[hs, pl.ds(ja, KB)] = dvt[hs, pl.ds(ja, KB)] + dot(dot_t[hs, :], pj)
            return c2

        lax.fori_loop(0, count, back, 0)
        dq = jnp.where(low_head, dqacc[0], dqacc[1]) * (scale * HD**-0.5)
        dfused[pl.ds(at, rows), :128] = turn(dq, i, -1.0).astype(BF16)

        @pl.when(i == 3)
        def _():
            z_forward(1)

        @pl.when(i == 6)
        def _():
            z_forward(2)
        return carry

    lax.fori_loop(0, NP, attend_step, 0)

    def kv_step(b, carry):
        at = aligned(rows * b, rows)
        dk = jnp.transpose(dkt[:, pl.ds(at, rows)])
        dv = jnp.transpose(dvt[:, pl.ds(at, rows)])
        dfused[pl.ds(at, rows), 128:256] = turn(dk, b, -1.0).astype(BF16)
        dfused[pl.ds(at, rows), 256:] = dv.astype(BF16)
        return carry

    lax.fori_loop(0, NP, kv_step, 0)

    GVIEW = (
        lambda b: gin.at[pl.ds(aligned(256 * b, 256), 256)],
        lambda b: gexp.at[pl.ds(aligned(256 * b, 256), 256)],
        lambda b: gred.at[pl.ds(aligned(128 * b, 128), 128)],
        lambda b: gz.at[b],
    )
    RZ = (rz_in, rz_exp, rz_red, rz_out)
    COMB = ((0, 1, 3), (3, 2, 0))

    def zr_direct(dest):
        ok = d != dest
        if dest == 3:
            ok = ok & (d != 0) & (d != 1)
        if dest == 0:
            ok = ok & (d != 3) & (d != 2)
        return ok

    def zr_copy(a, src_block, dest, slot, sem):
        return rc(GVIEW[a](src_block), RZ[a].at[slot], zr_s.at[a, sem], zr_r.at[a, slot], dest, s)

    def zr_first(a):
        for src, via, dest in COMB:
            @pl.when(d == src)
            def _():
                zr_copy(a, dest, via, via, dest).start()

    def zr_send(a):
        for dest in (3, 0, 2, 1):
            @pl.when(zr_direct(dest))
            def _():
                zr_copy(a, dest, dest, d, dest).start()

    def zr_join(a):
        for src, via, dest in COMB:
            @pl.when(d == via)
            def _():
                zr_copy(a, dest, dest, d, dest).wait_recv()
                ref = GVIEW[a](dest)
                ref[...] = (ref[...].astype(F32) + RZ[a][via].astype(F32)).astype(BF16)
                zr_copy(a, dest, dest, d, dest).start()

    def zr_total(a):
        ref = GVIEW[a](d)
        for src in range(NZ):
            came = d != src
            if src == 0:
                came = came & (d != 3)
            if src == 3:
                came = came & (d != 0)

            @pl.when(came)
            def _():
                zr_copy(a, d, d, src, src).wait_recv()
        use = []
        for src in range(NZ):
            came = d != src
            if src == 0:
                came = came & (d != 3)
            if src == 3:
                came = came & (d != 0)
            use.append(came)
        return ref, use

    def zr_sum(a, use, base, at, n):
        total = base
        for src in range(NZ):
            piece = RZ[a][src, pl.ds(at, n), :].astype(F32)
            total = total + jnp.where(use[src], piece, 0.0)
        return total

    def zr_sent(a):
        for dest in range(NZ):
            sent = d != dest

            @pl.when(sent)
            def _():
                zr_copy(a, dest, dest, d, dest).wait_send()

    def gin_block(b):
        at = aligned(256 * b, 256)
        gin[pl.ds(at, 256), :] = dot_tn(xn[:, pl.ds(at, 256)], dfused[...]).astype(BF16)

    def gexp_block(b):
        at = aligned(256 * b, 256)
        gexp[pl.ds(at, 256), :] = dot_tn(xn[:, pl.ds(at, 256)], de_s[...]).astype(BF16)

    def gred_block(b):
        at = aligned(128 * b, 128)
        gred[pl.ds(at, 128), :] = dot_tn(act_s[:, pl.ds(at, 128)], dyg[...]).astype(BF16)

    def loop(n, f):
        def step(i, carry):
            f(i)
            return carry
        lax.fori_loop(0, n, step, 0)

    loop(NZ, gin_block)
    zr_first(0)
    zr_send(0)
    gout[...] = dot_tn(o_s[...], dyg[...]).astype(BF16)

    def go_copy(m, incoming):
        t4 = lax.rem(peer(m), 4)
        src = gout.at[pl.ds(aligned(32 * t4, 32), 32)]
        dst = gz.at[t4 if incoming else quad]
        return rc(src, dst, go_s.at[m], go_r.at[m], d, peer(m))

    for m in range(1, 4):
        go_copy(m, False).start()
    gz[quad] = gout[pl.ds(aligned(32 * quad, 32), 32), :]

    z_arrived(1)
    z_arrived(2)
    eb = jnp.concatenate([vt[s, dd, 3:4, :] for dd in range(NZ)], axis=1)
    geb[...] = jnp.zeros_like(geb)

    def ffn_block(b):
        at = aligned(rows * b, rows)
        e = dot(xn[pl.ds(at, rows), :], wexp[...]) + eb
        up = dot_nt(dyg[pl.ds(at, rows), :], wred[...])
        a, slope = gelu_pair(e)
        act_s[pl.ds(at, rows), :] = a.astype(BF16)
        de = (up * slope).astype(BF16)
        de_s[pl.ds(at, rows), :] = de
        geb[...] = geb[...] + jnp.sum(de.astype(F32).reshape(rows // 8, 8, 4 * 128), axis=0)

    loop(NP, ffn_block)
    for m in range(1, 4):
        go_copy(m, True).wait_recv()
    zr_first(3)
    zr_send(3)
    zr_join(0)
    loop(NZ, gred_block)
    zr_first(2)
    zr_send(2)
    zr_join(3)
    loop(NZ, gexp_block)
    zr_first(1)
    zr_send(1)
    zr_join(2)

    for i in range(9):
        ag_copy(0, i, False).wait_send()

    def out_block(b):
        at = aligned(rows * b, rows)
        pout[pl.ds(at, rows), :] = (
            dot(o_s[pl.ds(at, rows), :], wout[...]) + dot(act_s[pl.ds(at, rows), :], wred[...])
        ).astype(BF16)

    def dn_block(b):
        at = aligned(rows * b, rows)
        pdn[pl.ds(at, rows), :] = (
            dot_nt(de_s[pl.ds(at, rows), :], wexp[...]) + dot_nt(dfused[pl.ds(at, rows), :], win[...])
        ).astype(BF16)

    RS = ((pout, sib_o, r1_o, r2_o), (pdn, sib_d, r1_d, r2_d))

    def part(which, m, lo, n):
        return RS[which][0].at[pl.ds(aligned(rows * peer(m) + lo, half), n)]

    RSM = (
        (1, 7, 0, rows, lambda w: RS[w][1].at[0]),
        (1, 3, 0, rows, lambda w: RS[w][1].at[1]),
        (1, 5, 0, rows, lambda w: RS[w][1].at[2]),
        (1, 1, 0, rows, lambda w: RS[w][1].at[3]),
        (2, 6, 0, half, lambda w: RS[w][2].at[0]),
        (4, 6, half, half, lambda w: RS[w][2].at[1]),
        (2, 2, 0, rows, lambda w: RS[w][3].at[0]),
        (4, 4, 0, rows, lambda w: RS[w][3].at[1]),
    )

    def rs_copy(w, i):
        to, blk, lo, n, land = RSM[i]
        return rc(part(w, blk, lo, n), land(w), rs_s.at[w, i], rs_r.at[w, i], d, peer(to))

    def add_into(w, m, lo, n, came):
        def step(c):
            ref = RS[w][0].at[pl.ds(aligned(rows * peer(m) + lo + 64 * c, 64), 64)]
            ref[...] = (ref[...].astype(F32) + came[pl.ds(aligned(64 * c, 64), 64), :].astype(F32)).astype(BF16)
        loop(n // 64, step)

    def rs_one(w):
        rs_copy(w, 0).wait_recv()
        add_into(w, 6, 0, rows, RS[w][1].at[0])
        rs_copy(w, 4).start()
        rs_copy(w, 5).start()
        rs_copy(w, 1).wait_recv()
        add_into(w, 2, 0, rows, RS[w][1].at[1])
        rs_copy(w, 2).wait_recv()
        add_into(w, 4, 0, rows, RS[w][1].at[2])

    def rs_two(w):
        rs_copy(w, 5).wait_recv()
        add_into(w, 2, half, half, RS[w][2].at[1])
        rs_copy(w, 6).start()
        rs_copy(w, 4).wait_recv()
        add_into(w, 4, 0, half, RS[w][2].at[0])
        rs_copy(w, 7).start()
        rs_copy(w, 3).wait_recv()

    def rs_three(w):
        rs_copy(w, 6).wait_recv()
        rs_copy(w, 7).wait_recv()

    def rs_total(w, c):
        at = aligned(64 * c, 64)
        own = RS[w][0][pl.ds(aligned(rows * s + 64 * c, 64), 64), :].astype(F32)
        own = own + RS[w][1][3, pl.ds(at, 64), :].astype(F32)
        own = own + RS[w][3][0, pl.ds(at, 64), :].astype(F32)
        return own + RS[w][3][1, pl.ds(at, 64), :].astype(F32)

    for i, m in enumerate((7, 3, 5, 1)):
        out_block(peer(m))
        rs_copy(0, i).start()
    for m in (6, 2, 4, 0):
        out_block(peer(m))
    zr_join(1)
    rs_one(0)
    for i, m in enumerate((7, 3, 5, 1)):
        dn_block(peer(m))
        rs_copy(1, i).start()
    rs_two(0)
    for m in (6, 2, 4, 0):
        dn_block(peer(m))
    rs_one(1)
    rs_three(0)

    def out_final(c):
        at = aligned(64 * c, 64)
        hout_ref[pl.ds(at, 64), :] = (
            x_ref[pl.ds(at, 64), :].astype(F32) + rs_total(0, c) + vecs[2:3, :]
        ).astype(BF16)

    loop(rows // 64, out_final)
    rs_two(1)

    keep = 1.0 - decay_ref[0]
    rate = rate_ref[0]
    inv_count = 0.5 / NZ

    def update(w_ref, m_ref, n_ref, u_ref, index, grad):
        mom = 0.5 * m_ref[index] + grad * inv_count
        n_ref[index] = mom
        u_ref[index] = keep * w_ref[index] - rate * mom

    def total_rows(a, n, width):
        ref, use = zr_total(a)

        def step(c):
            at = aligned(32 * c, 32)
            block = ref.at[pl.ds(at, 32)]
            block[...] = zr_sum(a, use, block[...].astype(F32), at, 32).astype(BF16)
        loop(n // 32, step)

    def back_copy(which, m, incoming):
        src = (gin, gexp)[which].at[pl.ds(aligned(256 * d + 32 * peer(m), 32), 32)]
        dst = (ra_in, ra_exp)[which].at[m]
        return rc(src, dst, b_s.at[which, m], b_r.at[which, m], d, peer(m))

    total_rows(0, 256, 384)
    for m in range(1, NP):
        back_copy(0, m, False).start()

    ref_o, use_o = zr_total(3)
    update(wout_ref, mout_ref, nout_ref, uout_ref, ..., zr_sum(3, use_o, ref_o[...].astype(F32), 0, 32))

    rs_three(1)
    sv0 = jnp.zeros((8, 1024), F32)
    geb_row = jnp.sum(geb[...], axis=0, keepdims=True)

    def grad_final(c, carry):
        at = aligned(32 * c, 32)
        dn = rs_total32(1, c)
        unit, inv = unit_of(x_ref[pl.ds(at, 32), :])
        dyf = dy_ref[pl.ds(at, 32), :].astype(F32)
        g = dn * vecs[0:1, :]
        hg = inv * (
            g - jnp.mean(g, axis=1, keepdims=True) - unit * jnp.mean(g * unit, axis=1, keepdims=True)
        ) + dyf
        hgrad_ref[pl.ds(at, 32), :] = hg.astype(BF16)

        def fold8(v):
            out = v[0:8]
            for r in range(8, 32, 8):
                out = out + v[r : r + 8]
            return out
        return (carry[0] + fold8(dn * unit), carry[1] + fold8(dn), carry[2] + fold8(dyf))

    def rs_total32(w, c):
        at = aligned(32 * c, 32)
        own = RS[w][0][pl.ds(aligned(rows * s + 32 * c, 32), 32), :].astype(F32)
        own = own + RS[w][1][3, pl.ds(at, 32), :].astype(F32)
        own = own + RS[w][3][0, pl.ds(at, 32), :].astype(F32)
        return own + RS[w][3][1, pl.ds(at, 32), :].astype(F32)

    sums = lax.fori_loop(0, rows // 32, grad_final, (sv0, sv0, sv0))
    row_sums = [jnp.sum(v, axis=0, keepdims=True) for v in sums]
    stacked = jnp.concatenate(row_sums + [jnp.zeros((5, 1024), F32)], axis=0)
    for yy in range(2):
        for dd in range(NZ):
            group = 2 * dd + yy
            sv[yy, dd] = stacked[:, 128 * group : 128 * (group + 1)]

    def sp_copy(m):
        return rc(sv.at[lax.div(peer(m), 4)], rv.at[m], sp_s.at[m], sp_r.at[m], d, peer(m))

    for m in range(1, NP):
        sp_copy(m).start()

    ref_r, use_r = zr_total(2)

    def red_update(c):
        at = aligned(16 * c, 16)
        update(
            wred_ref, mred_ref, nred_ref, ured_ref, (pl.ds(at, 16), slice(None)),
            zr_sum(2, use_r, ref_r[pl.ds(at, 16), :].astype(F32), at, 16),
        )
    loop(8, red_update)
    for m in range(1, NP):
        sp_copy(m).wait_recv()
    tiles = sv[ybit]
    for m in range(1, NP):
        tiles = tiles + rv[m]
    for dd in range(NZ):
        ebt = jnp.broadcast_to(geb_row[:, 128 * dd : 128 * (dd + 1)], (8, 128))
        zt[dd] = jnp.where(rows8 == 3, ebt, tiles[dd])

    def sz_copy(i, incoming):
        return rc(zt.at[other(i)], rzv.at[i], sz_s.at[i], sz_r.at[i], other(i), s)

    for i in range(1, NZ):
        sz_copy(i, False).start()

    total_rows(1, 256, 512)
    for m in range(1, NP):
        back_copy(1, m, False).start()

    def strip_in(m, grads):
        j = pair_of(peer(m))
        for prt in range(3):
            cols = pl.ds(aligned(128 * j + 1024 * prt, 128), 128)
            update(win_ref, min_ref, nin_ref, uin_ref, (slice(None), cols), grads[:, 128 * prt : 128 * (prt + 1)])

    def strip_exp(m, grads):
        t = peer(m)
        for e in range(NZ):
            cols = pl.ds(aligned(128 * (8 * e + t), 128), 128)
            update(wexp_ref, mexp_ref, nexp_ref, uexp_ref, (slice(None), cols), grads[:, 128 * e : 128 * (e + 1)])

    mine = pl.ds(aligned(256 * d + 32 * s, 32), 32)
    strip_in(0, gin[mine, :].astype(F32))
    for m in range(1, NP):
        back_copy(0, m, True).wait_recv()
        strip_in(m, ra_in[m].astype(F32))

    for i in range(1, NZ):
        sz_copy(i, True).wait_recv()
    tile = zt[d]
    for i in range(1, NZ):
        tile = tile + rzv[i]
    update(ebias_ref, mebias_ref, nebias_ref, uebias_ref, ..., tile[3:4, :])
    tile = pltpu.roll(tile, lax.rem(128 - 32 * quad, 128), 1)
    for r, (w, mo, n, u) in enumerate(
        (
            (gain_ref, mgain_ref, ngain_ref, ugain_ref),
            (shift_ref, mshift_ref, nshift_ref, ushift_ref),
            (rbias_ref, mrbias_ref, nrbias_ref, urbias_ref),
        )
    ):
        update(w, mo, n, u, ..., tile[r : r + 1, :32])

    strip_exp(0, gexp[mine, :].astype(F32))
    for m in range(1, NP):
        back_copy(1, m, True).wait_recv()
        strip_exp(m, ra_exp[m].astype(F32))

    for m in range(1, NP):
        a2a_msg(0, m).wait_send()
        a2a_msg(1, m).wait_send()
        vp_copy(m, False).wait_send()
        back_copy(0, m, False).wait_send()
        back_copy(1, m, False).wait_send()
        sp_copy(m).wait_send()
    for m in range(1, 4):
        wo_copy(m, False).wait_send()
        go_copy(m, False).wait_send()
    for i in range(1, NZ):
        vz_copy(i, False).wait_send()
        sz_copy(i, False).wait_send()
    for i in range(9):
        ag_copy(1, i, False).wait_send()
    for w in range(2):
        for i in range(8):
            rs_copy(w, i).wait_send()
    for a in range(4):
        z_sent(a)
        zr_sent(a)


def fused_shards(*args):
    (hidden_in, out_cotangent), weights, moments = args[:2], args[2:10], args[10:18]
    rows = hidden_in.shape[1]
    seq = rows * NP
    freq = 10000.0 ** (-2.0 * np.arange(ROT // 2) / ROT)
    lane_freq = np.tile(freq, 128 // (ROT // 2))[None, :]
    near = np.arange(rows)[:, None] * lane_freq
    far = (rows * np.arange(NP))[:, None] * lane_freq
    tables = [jnp.asarray(f(a), F32) for a in (near, far) for f in (np.cos, np.sin)]

    def flat(v):
        return v.reshape(1, -1) if v.ndim == 1 else v

    shards_in = [flat(w) for w in weights]
    ff = weights[6].shape[0] * NZ
    shard_shapes = [jax.ShapeDtypeStruct(w.shape, F32) for w in shards_in]
    vm = pltpu.VMEM
    dma = pltpu.SemaphoreType.DMA
    scratch = [
        vm((seq, D), BF16), vm((seq, D), BF16), vm((seq, D), BF16),
        vm((D, 384), BF16), vm((D, ff), BF16), vm((ff, D), BF16), vm((128, D), BF16), vm((NZ, 32, D), BF16),
        vm((NP, 32, 384), BF16), vm((NP, 32, ff), BF16),
        vm((seq, 128), BF16), vm((seq, 128), BF16), vm((seq, 256), BF16), vm((seq, 128), BF16), vm((seq, 128), BF16),
        vm((128, seq), F32), vm((128, seq), F32), vm((seq, 384), BF16),
        vm((2, NP // 2, rows, 2 * rows), F32),
        vm((2, rows, 128), F32), vm((2, rows, 256), F32), vm((2, rows, 128), F32),
        vm((seq, ff), BF16), vm((seq, ff), BF16), vm((seq, D), BF16),
        vm((4, rows, D), BF16), vm((4, rows, D), BF16),
        vm((2, rows // 2, D), BF16), vm((2, rows, D), BF16), vm((2, rows // 2, D), BF16), vm((2, rows, D), BF16),
        vm((D, 384), BF16), vm((D, ff), BF16), vm((ff, D), BF16), vm((128, D), BF16), vm((NZ, 32, D), BF16),
        vm((NZ, 256, 384), BF16), vm((NZ, 256, ff), BF16), vm((NZ, 128, D), BF16), vm((NZ, 32, D), BF16),
        vm((NP, 32, 384), BF16), vm((NP, 32, ff), BF16),
        vm((NP, NZ, 8, 128), F32), vm((8, D), F32), vm((8, ff), F32),
        vm((2, NZ, 8, 128), F32), vm((NP, NZ, 8, 128), F32), vm((NZ, 8, 128), F32), vm((NZ, 8, 128), F32),
        dma((2, NP)), dma((2, NP)), dma((2, 9)), dma((2, 9)), dma((4, 5)), dma((4, 4)),
        dma((NZ,)), dma((NZ,)), dma((NP,)), dma((NP,)), dma((4,)), dma((4,)),
        dma((2, 8)), dma((2, 8)), dma((4, 4)), dma((4, 4)), dma((4,)), dma((4,)),
        dma((2, NP)), dma((2, NP)), dma((NP,)), dma((NP,)), dma((NZ,)), dma((NZ,)),
    ]
    in_vmem = pl.BlockSpec(memory_space=pltpu.VMEM)
    in_smem = pl.BlockSpec(memory_space=pltpu.SMEM)

    def body(*refs):
        block_kernel(rows, *refs)

    rows_shape = jax.ShapeDtypeStruct((rows, D), BF16)
    outs = pl.pallas_call(
        body,
        out_shape=[rows_shape, rows_shape] + shard_shapes + shard_shapes,
        in_specs=[in_vmem] * 18 + [in_smem] * 2 + [in_vmem] * 4,
        out_specs=[in_vmem] * 18,
        scratch_shapes=scratch,
        compiler_params=pltpu.CompilerParams(
            collective_id=0, has_side_effects=True, vmem_limit_bytes=63 * 2**20
        ),
        name="block_step",
    )(
        hidden_in.reshape(rows, D), out_cotangent.reshape(rows, D), *shards_in,
        *[flat(m) for m in moments], args[18], args[19], tables[0], tables[1], tables[2], tables[3],
    )
    small = [w.shape for w in weights]
    return (
        outs[0].reshape(hidden_in.shape),
        outs[1].reshape(hidden_in.shape),
        *[o.reshape(sh) for o, sh in zip(outs[2:], small + small)],
    )


def fits(mesh):
    return mesh.shape["dp"] == NZ and mesh.shape["seq"] == NP


def solution(mesh):
    placed = (
        P("dp", "seq", None),
        P("dp", "seq", None),
        P(("dp", "seq")),
        P(("dp", "seq")),
        P(("dp", "seq"), None),
        P(("dp", "seq"), None),
        P(("dp", "seq"), None),
        P(("dp", "seq")),
        P(("dp", "seq"), None),
        P(("dp", "seq")),
        P(("dp", "seq")),
        P(("dp", "seq")),
        P(("dp", "seq"), None),
        P(("dp", "seq"), None),
        P(("dp", "seq"), None),
        P(("dp", "seq")),
        P(("dp", "seq"), None),
        P(("dp", "seq")),
        P(),
        P(),
    )
    return jax.shard_map(
        fused_shards if fits(mesh) else shards,
        mesh=mesh,
        in_specs=placed,
        out_specs=(
            P("dp", "seq", None),
            P("dp", "seq", None),
            P(("dp", "seq")),
            P(("dp", "seq")),
            P(("dp", "seq"), None),
            P(("dp", "seq"), None),
            P(("dp", "seq"), None),
            P(("dp", "seq")),
            P(("dp", "seq"), None),
            P(("dp", "seq")),
            P(("dp", "seq")),
            P(("dp", "seq")),
            P(("dp", "seq"), None),
            P(("dp", "seq"), None),
            P(("dp", "seq"), None),
            P(("dp", "seq")),
            P(("dp", "seq"), None),
            P(("dp", "seq")),
        ),
        check_vma=False,
    )
```

```python
import jax
import jax.numpy as jnp
import numpy as np
from jax import lax
from jax.experimental import pallas as pl
from jax.experimental.pallas import tpu as pltpu
from jax.sharding import PartitionSpec as P

D = 1024
H = 16
HD = 64
ROT = 32


epsilon = 1e-05
masked_score = -1e30


def rotary(block, positions, direction):
    half_rot = ROT // 2
    frequency = 10000.0 ** (-2.0 * jnp.arange(half_rot, dtype=jnp.float32) / ROT)
    angles = direction * positions[:, None] * frequency[None, :]
    cosine = jnp.cos(angles)[:, None, :]
    sine_part = jnp.sin(angles)[:, None, :]
    first_half = block[..., :half_rot]
    second = block[..., half_rot:ROT]
    return jnp.concatenate(
        [
            first_half * cosine - second * sine_part,
            second * cosine + first_half * sine_part,
            block[..., ROT:],
        ],
        axis=-1,
    )


def gelu_tanh(values):
    return jax.nn.gelu(values, approximate=True)


def gelu_back(expanded, upstream):
    unused_out, pullback = jax.vjp(gelu_tanh, expanded)
    return pullback(upstream)[0]


def heads_of(rows):
    return rows.reshape(rows.shape[0], H, HD)


def scores_of(query_rows, key_rows):
    score_scale = HD ** (-0.5)
    return (
        jnp.einsum(
            "qhd,khd->hqk",
            heads_of(query_rows),
            heads_of(key_rows),
            preferred_element_type=jnp.float32,
        )
        * score_scale
    )


def shards(
    hidden_in,
    out_cotangent,
    norm_gain,
    norm_shift,
    attend_in,
    attend_out,
    expand_weight,
    expand_bias,
    reduce_weight,
    reduce_bias,
    gain_moment,
    shift_moment,
    inward_moment,
    outward_moment,
    expand_moment,
    expbias_moment,
    reduce_moment,
    redbias_moment,
    learn_rate,
    decay_rate,
):
    score_scale = HD ** (-0.5)
    gain_low, shift_low, inward_mat, outward_mat, expand_mat, expand_vec, reduce_mat, reduce_vec = (
        lax.all_gather(norm_gain.astype(jnp.bfloat16), ("dp", "seq"), axis=0, tiled=True),
        lax.all_gather(norm_shift.astype(jnp.bfloat16), ("dp", "seq"), axis=0, tiled=True),
        lax.all_gather(attend_in.astype(jnp.bfloat16), ("dp", "seq"), axis=0, tiled=True),
        lax.all_gather(attend_out.astype(jnp.bfloat16), ("dp", "seq"), axis=0, tiled=True),
        lax.all_gather(expand_weight.astype(jnp.bfloat16), ("dp", "seq"), axis=0, tiled=True),
        lax.all_gather(expand_bias.astype(jnp.bfloat16), ("dp", "seq"), axis=0, tiled=True),
        lax.all_gather(reduce_weight.astype(jnp.bfloat16), ("dp", "seq"), axis=0, tiled=True),
        lax.all_gather(reduce_bias.astype(jnp.bfloat16), ("dp", "seq"), axis=0, tiled=True),
    )
    seq_count, block_len, model_width = hidden_in.shape
    row_count = seq_count * block_len
    full_len = block_len * lax.axis_size("seq")
    seq_start = lax.axis_index("seq") * block_len
    query_index = seq_start + jnp.arange(block_len, dtype=jnp.int32)
    key_index = jnp.arange(full_len, dtype=jnp.int32)
    causal = key_index[None, :] <= query_index[:, None]
    positions = query_index.astype(jnp.float32)
    inputs = hidden_in.astype(jnp.float32).reshape(row_count, model_width)
    row_mean = jnp.mean(inputs, axis=-1, keepdims=True)
    centred = inputs - row_mean
    row_var = jnp.mean(centred * centred, axis=-1, keepdims=True)
    inverse = lax.rsqrt(row_var + epsilon)
    unit_rows = centred * inverse
    gain_full = gain_low.astype(jnp.float32)
    normed = (unit_rows * gain_full + shift_low.astype(jnp.float32)).astype(jnp.bfloat16)
    joined = jnp.dot(normed, inward_mat, preferred_element_type=jnp.float32).reshape(
        seq_count, block_len, 3 * D
    )
    query = (
        rotary(joined[..., :D].reshape(seq_count, block_len, H, HD), positions, 1.0)
        .astype(jnp.bfloat16)
        .reshape(seq_count, block_len, D)
    )
    keyed = (
        rotary(joined[..., D : 2 * D].reshape(seq_count, block_len, H, HD), positions, 1.0)
        .astype(jnp.bfloat16)
        .reshape(seq_count, block_len, D)
    )
    valued = joined[..., 2 * D :].astype(jnp.bfloat16)
    key_all, value_all = (
        lax.all_gather(keyed, "seq", axis=1, tiled=True),
        lax.all_gather(valued, "seq", axis=1, tiled=True),
    )

    def attend(operands):
        query_seq, key_seq, value_seq = operands
        scores = jnp.where(causal[None], scores_of(query_seq, key_seq), masked_score)
        row_max = jnp.max(scores, axis=-1, keepdims=True)
        log_total = row_max + jnp.log(jnp.sum(jnp.exp(scores - row_max), axis=-1, keepdims=True))
        weights = jnp.exp(scores - log_total).astype(jnp.bfloat16)
        mixed = jnp.einsum(
            "hqk,khd->qhd", weights, heads_of(value_seq), preferred_element_type=jnp.float32
        )
        return (mixed.reshape(-1, D).astype(jnp.bfloat16), jnp.transpose(log_total[..., 0]))

    attended, log_totals = lax.map(attend, (query, key_all, value_all))
    expanded = jnp.dot(normed, expand_mat, preferred_element_type=jnp.float32) + expand_vec.astype(
        jnp.float32
    )
    activated = gelu_tanh(expanded).astype(jnp.bfloat16)
    flat_attn = attended.reshape(row_count, D)
    result = (
        inputs
        + jnp.dot(flat_attn, outward_mat, preferred_element_type=jnp.float32)
        + jnp.dot(activated, reduce_mat, preferred_element_type=jnp.float32)
        + reduce_vec.astype(jnp.float32)
    )
    hidden_out = result.astype(jnp.bfloat16).reshape(seq_count, block_len, D)
    upstream = out_cotangent.reshape(row_count, D)
    grad_outward = jnp.einsum("rd,re->de", flat_attn, upstream, preferred_element_type=jnp.float32)
    grad_reduce = jnp.einsum("rf,re->fe", activated, upstream, preferred_element_type=jnp.float32)
    grad_redbias = jnp.sum(upstream.astype(jnp.float32), axis=0)
    attn_back = (
        jnp.einsum("re,de->rd", upstream, outward_mat, preferred_element_type=jnp.float32)
        .astype(jnp.bfloat16)
        .reshape(seq_count, block_len, D)
    )
    act_back = jnp.einsum("re,fe->rf", upstream, reduce_mat, preferred_element_type=jnp.float32)
    expand_back = gelu_back(expanded, act_back).astype(jnp.bfloat16)
    grad_expbias = jnp.sum(expand_back.astype(jnp.float32), axis=0)
    grad_expand = jnp.einsum("rd,rf->df", normed, expand_back, preferred_element_type=jnp.float32)
    norm_back = jnp.einsum("rf,df->rd", expand_back, expand_mat, preferred_element_type=jnp.float32)

    def query_side(query_seq, key_seq, value_seq, back_seq, total_seq):
        scores = jnp.where(causal[None], scores_of(query_seq, key_seq), masked_score)
        probs = jnp.exp(scores - jnp.transpose(total_seq)[:, :, None])
        prob_grad = jnp.einsum(
            "qhd,khd->hqk",
            heads_of(back_seq),
            heads_of(value_seq),
            preferred_element_type=jnp.float32,
        )
        row_delta = jnp.sum(probs * prob_grad, axis=-1, keepdims=True)
        score_grad = (probs * (prob_grad - row_delta)).astype(jnp.bfloat16)
        query_grad = (
            jnp.einsum(
                "hqk,khd->qhd", score_grad, heads_of(key_seq), preferred_element_type=jnp.float32
            )
            * score_scale
        )
        return (probs, score_grad, query_grad, row_delta)

    def attend_back(operands):
        query_seq, key_seq, value_seq, back_seq, total_seq = operands
        probs, score_grad, query_grad, row_delta = query_side(
            query_seq, key_seq, value_seq, back_seq, total_seq
        )
        key_grad = (
            jnp.einsum(
                "hqk,qhd->khd", score_grad, heads_of(query_seq), preferred_element_type=jnp.float32
            )
            * score_scale
        )
        value_grad = jnp.einsum(
            "hqk,qhd->khd",
            probs.astype(jnp.bfloat16),
            heads_of(back_seq),
            preferred_element_type=jnp.float32,
        )
        return (query_grad, key_grad.reshape(-1, D), value_grad.reshape(-1, D))

    query_grads, key_terms, value_terms = lax.map(
        attend_back, (query, key_all, value_all, attn_back, log_totals)
    )
    key_grads, value_grads = (
        lax.psum_scatter(key_terms, "seq", scatter_dimension=1, tiled=True),
        lax.psum_scatter(value_terms, "seq", scatter_dimension=1, tiled=True),
    )
    query_turned = rotary(query_grads, positions, -1.0).reshape(seq_count, block_len, D)
    key_turned = rotary(key_grads.reshape(seq_count, block_len, H, HD), positions, -1.0).reshape(
        seq_count, block_len, D
    )
    joined_back = (
        jnp.concatenate([query_turned, key_turned, value_grads], axis=-1)
        .astype(jnp.bfloat16)
        .reshape(row_count, 3 * D)
    )
    grad_inward = jnp.einsum("rd,re->de", normed, joined_back, preferred_element_type=jnp.float32)
    norm_back = norm_back + jnp.einsum(
        "re,de->rd", joined_back, inward_mat, preferred_element_type=jnp.float32
    )
    grad_gain = jnp.sum(norm_back * unit_rows, axis=0)
    grad_shift = jnp.sum(norm_back, axis=0)
    unit_back = norm_back * gain_full
    input_back = inverse * (
        unit_back
        - jnp.mean(unit_back, axis=-1, keepdims=True)
        - unit_rows * jnp.mean(unit_back * unit_rows, axis=-1, keepdims=True)
    ) + upstream.astype(jnp.float32)
    hidden_grad = input_back.astype(jnp.bfloat16).reshape(seq_count, block_len, D)
    totals = (
        lax.psum_scatter(grad_gain, ("dp", "seq"), scatter_dimension=0, tiled=True),
        lax.psum_scatter(grad_shift, ("dp", "seq"), scatter_dimension=0, tiled=True),
        lax.psum_scatter(grad_inward, ("dp", "seq"), scatter_dimension=0, tiled=True),
        lax.psum_scatter(grad_outward, ("dp", "seq"), scatter_dimension=0, tiled=True),
        lax.psum_scatter(grad_expand, ("dp", "seq"), scatter_dimension=0, tiled=True),
        lax.psum_scatter(grad_expbias, ("dp", "seq"), scatter_dimension=0, tiled=True),
        lax.psum_scatter(grad_reduce, ("dp", "seq"), scatter_dimension=0, tiled=True),
        lax.psum_scatter(grad_redbias, ("dp", "seq"), scatter_dimension=0, tiled=True),
    )
    seq_total = seq_count * lax.axis_size("dp")
    step_rate = learn_rate[0]
    decay_now = decay_rate[0]
    params = (
        norm_gain,
        norm_shift,
        attend_in,
        attend_out,
        expand_weight,
        expand_bias,
        reduce_weight,
        reduce_bias,
    )
    moments = (
        gain_moment,
        shift_moment,
        inward_moment,
        outward_moment,
        expand_moment,
        expbias_moment,
        reduce_moment,
        redbias_moment,
    )
    momenta = [
        0.5 * moment + 0.5 * (summed_grad / seq_total)
        for moment, summed_grad in zip(moments, totals)
    ]
    updated = [
        (1.0 - decay_now) * weight_now - step_rate * momentum
        for weight_now, momentum in zip(params, momenta)
    ]
    return (
        hidden_out,
        hidden_grad,
        momenta[0],
        momenta[1],
        momenta[2],
        momenta[3],
        momenta[4],
        momenta[5],
        momenta[6],
        momenta[7],
        updated[0],
        updated[1],
        updated[2],
        updated[3],
        updated[4],
        updated[5],
        updated[6],
        updated[7],
    )


F32 = jnp.float32
BF16 = jnp.bfloat16
MESH = pl.DeviceIdType.MESH
NZ = 4
NP = 8
NT = (((1,), (1,)), ((), ()))
TN = (((0,), (0,)), ((), ()))


def dot(a, b):
    return jnp.dot(a, b, preferred_element_type=F32)


def dot_nt(a, b):
    return lax.dot_general(a, b, NT, preferred_element_type=F32)


def dot_tn(a, b):
    return lax.dot_general(a, b, TN, preferred_element_type=F32)


def aligned(value, unit):
    return pl.multiple_of(value, unit)


def gelu_pair(e):
    square = e * e
    t = jnp.tanh(e * (GELU_C + (GELU_C * GELU_A) * square))
    half = 0.5 + 0.5 * t
    slope = half + (0.5 * e) * (1.0 - t * t) * (GELU_C + (3.0 * GELU_C * GELU_A) * square)
    return e * half, slope


GELU_C = 0.7978845608028654
GELU_A = 0.044715


def block_kernel(rows, *refs):
    (
        x_ref, dy_ref, gain_ref, shift_ref, win_ref, wout_ref, wexp_ref, ebias_ref, wred_ref, rbias_ref,
        cosr_ref, sinr_ref, cosb_ref, sinb_ref,
        hout_ref, hgrad_ref, ra_in, ra_exp, tred_ref, tout_ref, tile_ref,
        xg, dyg, xn, win, wexp, wred, wout, wz, pin, pexp,
        q_s, k_s, vx, o_s, do_s, dkt, dvt, dfused, sbuf, lse, mref, acc, dqacc,
        act_s, de_s, pdn, sib_o, sib_d, r1_o, r2_o, r1_d, r2_d,
        gin, gexp, gred, gout, gz, rz_in, rz_exp, rz_red, rz_out, rb_in, rb_exp,
        vt, vecs, geb, sums, sv, rv, zt, rzv,
        a2a_s, a2a_r, ag_s, ag_r, z_s, z_r, vz_s, vz_r, vp_s, vp_r, wo_s, wo_r,
        rs_s, rs_r, zr_s, zr_r, go_s, go_r, b_s, b_r, sp_s, sp_r, sz_s, sz_r,
    ) = refs
    pout = xg
    d = lax.axis_index("dp")
    s = lax.axis_index("seq")
    core = lax.rem(s, 2)
    xbit = lax.rem(lax.div(s, 2), 2)
    ybit = lax.div(s, 4)
    chip = lax.div(s, 2)
    quad = lax.rem(s, 4)

    def peer(m):
        out = s
        if m & 1:
            out = out + (1 - 2 * core)
        if m & 2:
            out = out + 2 * (1 - 2 * xbit)
        if m & 4:
            out = out + 4 * (1 - 2 * ybit)
        return out

    def pair_of(t):
        return 2 * lax.rem(t, 4) + lax.div(t, 4)

    def rc(src, dst, ssem, rsem, dd, ss):
        return pltpu.make_async_remote_copy(
            src_ref=src, dst_ref=dst, send_sem=ssem, recv_sem=rsem,
            device_id=(dd, ss), device_id_type=MESH,
        )

    barrier = pltpu.get_barrier_semaphore()
    for m in range(1, NP):
        pl.semaphore_signal(barrier, inc=1, device_id=(d, peer(m)), device_id_type=MESH)
    for dz in range(1, NZ):
        pl.semaphore_signal(barrier, inc=1, device_id=(lax.rem(d + dz, NZ), s), device_id_type=MESH)

    zrow = jnp.zeros((1, 96), F32)
    small = jnp.concatenate(
        [
            jnp.concatenate([r[...].astype(BF16).astype(F32), zrow], axis=1)
            for r in (gain_ref, shift_ref, rbias_ref)
        ]
        + [jnp.zeros((5, 128), F32)],
        axis=0,
    )
    small = pltpu.roll(small, 32 * quad, 1)
    rows8 = lax.broadcasted_iota(jnp.int32, (8, 128), 0)
    ebias_row = jnp.broadcast_to(ebias_ref[...].astype(BF16).astype(F32), (8, 128))
    vt[s, d] = jnp.where(rows8 == 3, ebias_row, small)
    wz[d] = wout_ref[...].astype(BF16)
    xg[pl.ds(aligned(rows * s, rows), rows), :] = x_ref[...]
    own_rows = aligned(32 * (8 * d + s), 32)

    def pack_in():
        for m in range(NP):
            j = pair_of(peer(m))
            for part in range(3):
                piece = win_ref[:, pl.ds(aligned(128 * j + 1024 * part, 128), 128)].astype(BF16)
                if m == 0:
                    win[pl.ds(own_rows, 32), 128 * part : 128 * (part + 1)] = piece
                else:
                    pin[m, :, 128 * part : 128 * (part + 1)] = piece

    def pack_exp():
        for m in range(NP):
            t = peer(m)
            for e in range(NZ):
                piece = wexp_ref[:, pl.ds(aligned(128 * (8 * e + t), 128), 128)].astype(BF16)
                if m == 0:
                    wexp[pl.ds(own_rows, 32), 128 * e : 128 * (e + 1)] = piece
                else:
                    pexp[m, :, 128 * e : 128 * (e + 1)] = piece

    pack_in()
    pl.semaphore_wait(barrier, NP - 1 + NZ - 1)

    def a2a_msg(which, m):
        src = (pin, pexp)[which].at[m]
        dst = (win, wexp)[which].at[pl.ds(own_rows, 32)]
        return rc(src, dst, a2a_s.at[which, m], a2a_r.at[which, m], d, peer(m))

    def a2a_arrived(which, m):
        dst = (win, wexp)[which].at[pl.ds(aligned(32 * (8 * d + peer(m)), 32), 32)]
        rc((pin, pexp)[which].at[m], dst, a2a_s.at[which, m], a2a_r.at[which, m], d, peer(m)).wait_recv()

    half = rows // 2
    AG = (
        (1, 0, 0, rows), (2, 0, 0, rows), (4, 0, 0, rows),
        (1, 2, 0, rows), (1, 4, 0, rows), (4, 2, half, half), (2, 4, 0, half),
        (1, 6, 0, half), (1, 6, half, half),
    )

    def ag_copy(which, i, incoming):
        to, blk, lo, n = AG[i]
        buf = (xg, dyg)[which]
        at = rows * peer(blk ^ (to if incoming else 0)) + lo
        ref = buf.at[pl.ds(aligned(at, half), n)]
        return rc(ref, ref, ag_s.at[which, i], ag_r.at[which, i], d, peer(to))

    def ag_start(which, i):
        ag_copy(which, i, False).start()

    def ag_arrived(which, i):
        ag_copy(which, i, True).wait_recv()

    ZVIEW = (
        lambda b: win.at[pl.ds(aligned(256 * b, 256), 256)],
        lambda b: wexp.at[pl.ds(aligned(256 * b, 256), 256)],
        lambda b: wred.at[pl.ds(aligned(128 * b, 128), 128)],
        lambda b: wz.at[b],
    )

    def z_direct(dest):
        ok = d != dest
        if dest == NZ - 1:
            ok = ok & (d != 0)
        if dest == 0:
            ok = ok & (d != NZ - 1)
        return ok

    def z_send(a):
        for dest in (3, 0, 2, 1):
            @pl.when(z_direct(dest))
            def _():
                rc(ZVIEW[a](d), ZVIEW[a](d), z_s.at[a, dest], z_r.at[a, d], dest, s).start()

    FWD = ((2, 0, 3), (1, 3, 0))

    def z_wait_block(a, b):
        rc(ZVIEW[a](b), ZVIEW[a](b), z_s.at[a, 4], z_r.at[a, b], d, s).wait_recv()

    def z_forward(a):
        for at, blk, dest in FWD:
            @pl.when(d == at)
            def _():
                z_wait_block(a, blk)
                rc(ZVIEW[a](blk), ZVIEW[a](blk), z_s.at[a, 4], z_r.at[a, blk], dest, s).start()

    def z_arrived(a):
        for b in range(NZ):
            need = d != b
            for at, blk, dest in FWD:
                if blk == b:
                    need = need & (d != at)

            @pl.when(need)
            def _():
                z_wait_block(a, b)

    def z_sent(a):
        for dest in range(NZ):
            @pl.when(z_direct(dest))
            def _():
                rc(ZVIEW[a](d), ZVIEW[a](d), z_s.at[a, dest], z_r.at[a, d], dest, s).wait_send()
        for at, blk, dest in FWD:
            @pl.when(d == at)
            def _():
                rc(ZVIEW[a](blk), ZVIEW[a](blk), z_s.at[a, 4], z_r.at[a, blk], dest, s).wait_send()

    def other(i):
        return lax.rem(d + i, NZ)

    def vz_copy(i, incoming):
        b = lax.rem(d + NZ - i, NZ) if incoming else d
        return rc(vt.at[s, b], vt.at[s, b], vz_s.at[i], vz_r.at[i], other(i), s)

    def vp_copy(m, incoming):
        b = peer(m) if incoming else s
        return rc(vt.at[b], vt.at[b], vp_s.at[m], vp_r.at[m], d, peer(m))

    for i in range(1, NZ):
        vz_copy(i, False).start()
    for m in range(1, NP):
        a2a_msg(0, m).start()
    z_send(3)
    for i in (1, 2, 0):
        ag_start(0, i)
    pack_exp()
    for m in range(1, NP):
        a2a_msg(1, m).start()
    wred[pl.ds(aligned(128 * d, 128), 128), :] = wred_ref[...].astype(BF16)
    dyg[pl.ds(aligned(rows * s, rows), rows), :] = dy_ref[...]
    for i in range(1, NZ):
        vz_copy(i, True).wait_recv()
    for m in range(1, NP):
        vp_copy(m, False).start()
    for m in range(1, NP):
        a2a_arrived(0, m)
    z_send(0)
    for m in range(1, NP):
        a2a_arrived(1, m)
    z_send(1)

    def wo_copy(m, incoming):
        src = wz.at[lax.rem(peer(m), 4)]
        r = lax.rem(peer(m), 4) if incoming else quad
        dst = wout.at[pl.ds(aligned(32 * r, 32), 32)]
        return rc(src, dst, wo_s.at[m], wo_r.at[m], d, peer(m))

    for m in range(1, NP):
        vp_copy(m, True).wait_recv()
    for dd in range(NZ):
        for yy in range(2):
            group = 2 * dd + yy
            total = vt[4 * yy, dd]
            for jj in range(1, 4):
                total = total + vt[4 * yy + jj, dd]
            vecs[:, 128 * group : 128 * (group + 1)] = total

    def unit_of(xb):
        xf = xb.astype(F32)
        mu = jnp.mean(xf, axis=1, keepdims=True)
        cen = xf - mu
        var = jnp.mean(cen * cen, axis=1, keepdims=True)
        inv = lax.rsqrt(var + epsilon)
        return cen * inv, inv

    def norm_block(b):
        def step(c, carry):
            at = aligned(rows * b + 64 * c, 64)
            unit, _ = unit_of(xg[pl.ds(at, 64), :])
            xn[pl.ds(at, 64), :] = (unit * vecs[0:1, :] + vecs[1:2, :]).astype(BF16)
            return carry
        lax.fori_loop(0, rows // 64, step, 0)

    lane_b = lax.broadcasted_iota(jnp.int32, (rows, 128), 1)
    low_head = lane_b < HD
    in_head = lax.rem(lane_b, HD)
    first_rot = in_head < ROT // 2
    second_rot = (in_head >= ROT // 2) & (in_head < ROT)

    def turn(block, b, sign):
        cb, sb = cosb_ref[pl.ds(b, 1), :], sinb_ref[pl.ds(b, 1), :]
        cr, sr = cosr_ref[...], sinr_ref[...]
        co = cr * cb - sr * sb
        si = (sr * cb + cr * sb) * sign
        co = jnp.where(in_head < ROT, co, 1.0)
        up = pltpu.roll(block, 128 - ROT // 2, 1)
        down = pltpu.roll(block, ROT // 2, 1)
        mixed = jnp.where(first_rot, -up, down) * si
        mixed = jnp.where(in_head < ROT, mixed, 0.0)
        return block * co + mixed

    ag_arrived(0, 1)
    ag_start(0, 5)
    ag_start(0, 3)
    ag_arrived(0, 2)
    ag_start(0, 6)
    ag_start(0, 4)
    for i in (1, 2, 0):
        ag_start(1, i)
    norm_block(s)
    ag_arrived(0, 0)
    norm_block(peer(1))
    norm_block(peer(2))
    ag_arrived(0, 6)
    ag_start(0, 7)
    ag_arrived(0, 5)
    ag_start(0, 8)
    norm_block(peer(4))
    z_forward(3)
    ag_arrived(0, 3)
    norm_block(peer(3))
    ag_arrived(0, 4)
    norm_block(peer(5))
    norm_block(peer(6))
    ag_arrived(0, 7)
    ag_arrived(0, 8)
    norm_block(peer(7))
    z_arrived(3)
    for m in range(1, 4):
        wo_copy(m, False).start()
    wout[pl.ds(aligned(32 * quad, 32), 32), :] = wz[quad]
    z_forward(0)
    z_send(2)
    ag_arrived(1, 1)
    ag_start(1, 5)
    ag_start(1, 3)
    ag_arrived(1, 2)
    ag_start(1, 6)
    ag_start(1, 4)
    z_arrived(0)

    def qkv_step(b, carry):
        at = aligned(rows * b, rows)
        joined = dot(xn[pl.ds(at, rows), :], win[...])
        q_s[pl.ds(at, rows), :] = turn(joined[:, :128], b, 1.0).astype(BF16) * jnp.asarray(HD**-0.5, BF16)
        k_s[pl.ds(at, rows), :] = turn(joined[:, 128:256], b, 1.0).astype(BF16)
        vx[pl.ds(at, rows), :128] = joined[:, 256:].astype(BF16)
        vx[pl.ds(at, rows), 128:] = jnp.ones((rows, 128), BF16)
        return carry

    lax.fori_loop(0, NP, qkv_step, 0)
    KB = 2 * rows

    def wide(tile):
        return jnp.concatenate([tile] * (KB // 128), axis=1)

    def fold(v):
        out = v[:, :128]
        for c in range(1, KB // 128):
            out = jnp.maximum(out, v[:, 128 * c : 128 * (c + 1)])
        return out

    def by_head(block):
        zero = jnp.zeros_like(block)
        return jnp.where(low_head, block, zero), jnp.where(low_head, zero, block)

    def hidden(i, j):
        query = rows * i + lax.broadcasted_iota(jnp.int32, (rows, KB), 0)
        key = KB * j + lax.broadcasted_iota(jnp.int32, (rows, KB), 1)
        return key > query

    def attend_step(i, carry):
        at = aligned(rows * i, rows)
        last = lax.div(i, 2)
        qh = by_head(q_s[pl.ds(at, rows), :])
        kj = k_s[pl.ds(aligned(KB * last, KB), KB), :]
        mask = hidden(i, last)
        for h in range(2):
            sc = jnp.where(mask, masked_score, dot_nt(qh[h], kj))
            sbuf[h, last] = sc
            mref[h] = fold(sc)

        def scores(j, c2):
            kk = k_s[pl.ds(aligned(KB * j, KB), KB), :]
            for h in range(2):
                sc = dot_nt(qh[h], kk)
                sbuf[h, j] = sc
                mref[h] = jnp.maximum(mref[h], fold(sc))
            return c2

        lax.fori_loop(0, last, scores, 0)
        for h in range(2):
            mref[h] = jnp.broadcast_to(jnp.max(mref[h], axis=1, keepdims=True), (rows, 128))
            acc[h] = jnp.zeros((rows, 256), F32)

        def weigh(j, c2):
            vj = vx[pl.ds(aligned(KB * j, KB), KB), :]
            for h in range(2):
                pj = jnp.exp(sbuf[h, j] - wide(mref[h])).astype(BF16)
                acc[h] = acc[h] + dot(pj, vj)
            return c2

        lax.fori_loop(0, last + 1, weigh, 0)
        o_s[pl.ds(at, rows), :] = jnp.where(
            low_head, acc[0][:, :128] / acc[0][:, 128:], acc[1][:, :128] / acc[1][:, 128:]
        ).astype(BF16)
        for h in range(2):
            lse[h, pl.ds(at, rows), :] = mref[h] + jnp.log(acc[h][:, 128:])

        @pl.when(i == 4)
        def _():
            z_forward(1)
        return carry

    lax.fori_loop(0, NP, attend_step, 0)
    ag_arrived(1, 6)
    ag_start(1, 7)
    ag_arrived(1, 5)
    ag_start(1, 8)
    dkt[...] = jnp.zeros_like(dkt)
    dvt[...] = jnp.zeros_like(dvt)

    def attend_back(i):
        at = aligned(rows * i, rows)
        last = lax.div(i, 2)
        qi = q_s[pl.ds(at, rows), :]
        doi = do_s[pl.ds(at, rows), :]
        dof = doi.astype(F32)
        qh = by_head(qi)
        doh = by_head(doi)
        qt = jnp.transpose(qi.astype(F32)).astype(BF16)
        dot_t = jnp.transpose(dof).astype(BF16)
        prod = dof * o_s[pl.ds(at, rows), :].astype(F32)
        parts = by_head(prod)
        for h in range(2):
            mref[h] = jnp.broadcast_to(jnp.sum(parts[h], axis=1, keepdims=True), (rows, 128))
            dqacc[h] = jnp.zeros((rows, 128), F32)

        def unit(j, mask):
            ja = aligned(KB * j, KB)
            kk = k_s[pl.ds(ja, KB), :]
            vj = vx[pl.ds(ja, KB), :128]
            for h in range(2):
                hs = slice(HD * h, HD * (h + 1))
                p = jnp.exp(dot_nt(qh[h], kk) - wide(lse[h, pl.ds(at, rows), :]))
                if mask is not None:
                    p = jnp.where(mask, 0.0, p)
                ds = (p * (dot_nt(doh[h], vj) - wide(mref[h]))).astype(BF16)
                dqacc[h] = dqacc[h] + dot(ds, kk)
                dkt[hs, pl.ds(ja, KB)] = dkt[hs, pl.ds(ja, KB)] + dot(qt[hs, :], ds)
                dvt[hs, pl.ds(ja, KB)] = dvt[hs, pl.ds(ja, KB)] + dot(dot_t[hs, :], p.astype(BF16))

        def free(j, c2):
            unit(j, None)
            return c2

        lax.fori_loop(0, last, free, 0)
        unit(last, hidden(i, last))
        dq = jnp.where(low_head, dqacc[0], dqacc[1]) * HD**-0.5
        dfused[pl.ds(at, rows), :128] = turn(dq, i, -1.0).astype(BF16)

    for i in (0, 3, 4, 7, 8):
        ag_arrived(1, i)
    for m in range(1, 4):
        wo_copy(m, True).wait_recv()

    def loop(n, f):
        def step(i, carry):
            f(i)
            return carry
        lax.fori_loop(0, n, step, 0)

    def do_block(b):
        at = aligned(rows * b, rows)
        do_s[pl.ds(at, rows), :] = dot_nt(dyg[pl.ds(at, rows), :], wout[...]).astype(BF16)

    loop(NP, do_block)
    gout[...] = dot_tn(o_s[...], dyg[...]).astype(BF16)

    def go_copy(m, incoming):
        t4 = lax.rem(peer(m), 4)
        src = gout.at[pl.ds(aligned(32 * t4, 32), 32)]
        dst = gz.at[t4 if incoming else quad]
        return rc(src, dst, go_s.at[m], go_r.at[m], d, peer(m))

    for m in range(1, 4):
        go_copy(m, False).start()
    gz[quad] = gout[pl.ds(aligned(32 * quad, 32), 32), :]
    early = 2

    def back_early(step):
        attend_back(NP - 1 - step)

        @pl.when(step == 0)
        def _():
            z_forward(2)

    loop(early, back_early)
    z_arrived(1)
    z_arrived(2)

    eb = jnp.concatenate([vt[s, dd, 3:4, :] for dd in range(NZ)], axis=1)
    geb[...] = jnp.zeros_like(geb)
    sums[...] = jnp.zeros_like(sums)
    sums[2:3, :] = jnp.sum(dy_ref[...].astype(F32), axis=0, keepdims=True)

    def ffn_block(b):
        at = aligned(rows * b, rows)
        e = dot(xn[pl.ds(at, rows), :], wexp[...]) + eb
        up = dot_nt(dyg[pl.ds(at, rows), :], wred[...])
        a, slope = gelu_pair(e)
        act_s[pl.ds(at, rows), :] = a.astype(BF16)
        de = (up * slope).astype(BF16)
        de_s[pl.ds(at, rows), :] = de
        geb[...] = geb[...] + jnp.sum(de.astype(F32).reshape(rows // 8, 8, 4 * 128), axis=0)

    loop(NP, ffn_block)

    GVIEW = (
        lambda b: gin.at[pl.ds(aligned(256 * b, 256), 256)],
        lambda b: gexp.at[pl.ds(aligned(256 * b, 256), 256)],
        lambda b: gred.at[pl.ds(aligned(128 * b, 128), 128)],
        lambda b: gz.at[b],
    )
    RZ = (rz_in, rz_exp, rz_red, rz_out)
    COMB = ((0, 1, 3), (3, 2, 0))

    def zr_direct(dest):
        ok = d != dest
        if dest == 3:
            ok = ok & (d != 0) & (d != 1)
        if dest == 0:
            ok = ok & (d != 3) & (d != 2)
        return ok

    def zr_copy(a, src_block, dest, slot, sem):
        return rc(GVIEW[a](src_block), RZ[a].at[slot], zr_s.at[a, sem], zr_r.at[a, slot], dest, s)

    def zr_first(a):
        for src, via, dest in COMB:
            @pl.when(d == src)
            def _():
                zr_copy(a, dest, via, via, dest).start()

    def zr_send(a):
        for dest in (3, 0, 2, 1):
            @pl.when(zr_direct(dest))
            def _():
                zr_copy(a, dest, dest, d, dest).start()

    def zr_join(a):
        for src, via, dest in COMB:
            @pl.when(d == via)
            def _():
                zr_copy(a, dest, dest, d, dest).wait_recv()
                ref = GVIEW[a](dest)
                ref[...] = (ref[...].astype(F32) + RZ[a][via].astype(F32)).astype(BF16)
                zr_copy(a, dest, dest, d, dest).start()

    def zr_total(a):
        ref = GVIEW[a](d)
        for src in range(NZ):
            came = d != src
            if src == 0:
                came = came & (d != 3)
            if src == 3:
                came = came & (d != 0)

            @pl.when(came)
            def _():
                zr_copy(a, d, d, src, src).wait_recv()
        use = []
        for src in range(NZ):
            came = d != src
            if src == 0:
                came = came & (d != 3)
            if src == 3:
                came = came & (d != 0)
            use.append(came)
        return ref, use

    def zr_sum(a, use, base, at, n):
        total = base
        for src in range(NZ):
            piece = RZ[a][src, pl.ds(at, n), :].astype(F32)
            total = total + jnp.where(use[src], piece, 0.0)
        return total

    def zr_sent(a):
        for dest in range(NZ):
            sent = d != dest

            @pl.when(sent)
            def _():
                zr_copy(a, dest, dest, d, dest).wait_send()

    def gexp_block(b):
        at = aligned(256 * b, 256)
        gexp[pl.ds(at, 256), :] = dot_tn(xn[:, pl.ds(at, 256)], de_s[...]).astype(BF16)

    def gred_block(b):
        at = aligned(128 * b, 128)
        gred[pl.ds(at, 128), :] = dot_tn(act_s[:, pl.ds(at, 128)], dyg[...]).astype(BF16)

    def dest_send(a, dest):
        for src, via, to in COMB:
            if to == dest:
                @pl.when(d == src)
                def _():
                    zr_copy(a, to, via, via, to).start()

        @pl.when(zr_direct(dest))
        def _():
            zr_copy(a, dest, dest, d, dest).start()

    for dest in (3, 0, 2, 1):
        gred_block(dest)
        dest_send(2, dest)
    for m in range(1, 4):
        go_copy(m, True).wait_recv()
    for dest in (3, 0, 2, 1):
        dest_send(3, dest)

    for i in range(9):
        ag_copy(0, i, False).wait_send()

    def out_block(b):
        at = aligned(rows * b, rows)
        pout[pl.ds(at, rows), :] = (
            dot(o_s[pl.ds(at, rows), :], wout[...]) + dot(act_s[pl.ds(at, rows), :], wred[...])
        ).astype(BF16)

    def dn_block(b):
        at = aligned(rows * b, rows)
        dn = dot_nt(de_s[pl.ds(at, rows), :], wexp[...]) + dot_nt(dfused[pl.ds(at, rows), :], win[...])
        pdn[pl.ds(at, rows), :] = dn.astype(BF16)
        sums[0:1, :] = sums[0:1, :] + jnp.sum(dn * xn[pl.ds(at, rows), :].astype(F32), axis=0, keepdims=True)
        sums[1:2, :] = sums[1:2, :] + jnp.sum(dn, axis=0, keepdims=True)

    RS = ((pout, sib_o, r1_o, r2_o), (pdn, sib_d, r1_d, r2_d))

    def part(which, m, lo, n):
        return RS[which][0].at[pl.ds(aligned(rows * peer(m) + lo, half), n)]

    RSM = (
        (1, 7, 0, rows, lambda w: RS[w][1].at[0]),
        (1, 3, 0, rows, lambda w: RS[w][1].at[1]),
        (1, 5, 0, rows, lambda w: RS[w][1].at[2]),
        (1, 1, 0, rows, lambda w: RS[w][1].at[3]),
        (2, 6, 0, half, lambda w: RS[w][2].at[0]),
        (4, 6, half, half, lambda w: RS[w][2].at[1]),
        (2, 2, 0, rows, lambda w: RS[w][3].at[0]),
        (4, 4, 0, rows, lambda w: RS[w][3].at[1]),
    )

    def rs_copy(w, i):
        to, blk, lo, n, land = RSM[i]
        return rc(part(w, blk, lo, n), land(w), rs_s.at[w, i], rs_r.at[w, i], d, peer(to))

    def add_into(w, m, lo, n, came):
        def step(c):
            ref = RS[w][0].at[pl.ds(aligned(rows * peer(m) + lo + 64 * c, 64), 64)]
            ref[...] = (ref[...].astype(F32) + came[pl.ds(aligned(64 * c, 64), 64), :].astype(F32)).astype(BF16)
        loop(n // 64, step)

    def rs_across(w):
        rs_copy(w, 0).wait_recv()
        add_into(w, 6, 0, rows, RS[w][1].at[0])
        rs_copy(w, 4).start()
        rs_copy(w, 5).start()

    def rs_pair(w, which):
        rs_copy(w, 1 + which).wait_recv()
        add_into(w, (2, 4)[which], 0, rows, RS[w][1].at[1 + which])

    def rs_near(w, which):
        rs_copy(w, 5 - which).wait_recv()
        add_into(w, (2, 4)[which], (half, 0)[which], half, RS[w][2].at[1 - which])
        rs_copy(w, 6 + which).start()

    def rs_last(w):
        for i in (3, 6, 7):
            rs_copy(w, i).wait_recv()

    for i, m in enumerate((7, 3, 5, 1)):
        out_block(peer(m))
        rs_copy(0, i).start()
    for dest in (3, 0, 2, 1):
        gexp_block(dest)
        dest_send(1, dest)
    for m in (6, 2, 4, 0):
        out_block(peer(m))

    def back_late(step):
        attend_back(NP - 1 - early - step)

        @pl.when(step == 0)
        def _():
            rs_across(0)
            zr_join(2)

        @pl.when(step == 1)
        def _():
            rs_pair(0, 0)
            rs_pair(0, 1)
            zr_join(3)

        @pl.when(step == 2)
        def _():
            rs_near(0, 0)
            rs_near(0, 1)
            zr_join(1)

    loop(NP - early, back_late)

    def kv_block(b):
        at = aligned(rows * b, rows)
        dk = jnp.transpose(dkt[:, pl.ds(at, rows)])
        dv = jnp.transpose(dvt[:, pl.ds(at, rows)])
        dfused[pl.ds(at, rows), 128:256] = turn(dk, b, -1.0).astype(BF16)
        dfused[pl.ds(at, rows), 256:] = dv.astype(BF16)

    loop(NP, kv_block)

    def gin_block(b):
        at = aligned(256 * b, 256)
        gin[pl.ds(at, 256), :] = dot_tn(xn[:, pl.ds(at, 256)], dfused[...]).astype(BF16)

    for dest in (3, 0):
        gin_block(dest)
        dest_send(0, dest)
    dn_block(peer(7))
    rs_copy(1, 0).start()
    for dest in (2, 1):
        gin_block(dest)
        dest_send(0, dest)
    for i, m in ((1, 3), (2, 5), (3, 1)):
        dn_block(peer(m))
        rs_copy(1, i).start()
    zr_join(0)
    dn_block(peer(6))
    rs_across(1)
    dn_block(peer(2))
    rs_pair(1, 0)
    dn_block(peer(4))
    rs_pair(1, 1)
    dn_block(s)
    for yy in range(2):
        for dd in range(NZ):
            group = 2 * dd + yy
            sv[yy, dd] = sums[:, 128 * group : 128 * (group + 1)]

    def sp_copy(m):
        return rc(sv.at[lax.div(peer(m), 4)], rv.at[m], sp_s.at[m], sp_r.at[m], d, peer(m))

    for m in range(1, NP):
        sp_copy(m).start()

    geb_row = jnp.sum(geb[...], axis=0, keepdims=True)

    def total_rows(a, n):
        ref, use = zr_total(a)

        def step(c):
            at = aligned(32 * c, 32)
            block = ref.at[pl.ds(at, 32)]
            block[...] = zr_sum(a, use, block[...].astype(F32), at, 32).astype(BF16)
        loop(n // 32, step)

    def back_copy(which, m, incoming):
        src = (gin, gexp)[which].at[pl.ds(aligned(256 * d + 32 * peer(m), 32), 32)]
        dst = (rb_in, rb_exp)[which].at[m]
        return rc(src, dst, b_s.at[which, m], b_r.at[which, m], d, peer(m))

    total_rows(1, 256)
    for m in range(1, NP):
        back_copy(1, m, False).start()
    rs_near(1, 0)
    rs_near(1, 1)

    ref_r, use_r = zr_total(2)

    def red_total(c):
        at = aligned(32 * c, 32)
        tred_ref[pl.ds(at, 32), :] = zr_sum(2, use_r, ref_r[pl.ds(at, 32), :].astype(F32), at, 32)
    loop(4, red_total)
    rs_last(0)

    def out_final(c):
        at = aligned(32 * c, 32)
        hout_ref[pl.ds(at, 32), :] = (
            x_ref[pl.ds(at, 32), :].astype(F32) + rs_total32(0, c) + vecs[2:3, :]
        ).astype(BF16)

    def rs_total32(w, c):
        at = aligned(32 * c, 32)
        own = RS[w][0][pl.ds(aligned(rows * s + 32 * c, 32), 32), :].astype(F32)
        own = own + RS[w][1][3, pl.ds(at, 32), :].astype(F32)
        own = own + RS[w][3][0, pl.ds(at, 32), :].astype(F32)
        return own + RS[w][3][1, pl.ds(at, 32), :].astype(F32)

    loop(rows // 32, out_final)
    def grad_final(c):
        at = aligned(32 * c, 32)
        dn = rs_total32(1, c)
        unit, inv = unit_of(x_ref[pl.ds(at, 32), :])
        dyf = dy_ref[pl.ds(at, 32), :].astype(F32)
        g = dn * vecs[0:1, :]
        hg = inv * (
            g - jnp.mean(g, axis=1, keepdims=True) - unit * jnp.mean(g * unit, axis=1, keepdims=True)
        ) + dyf
        hgrad_ref[pl.ds(at, 32), :] = hg.astype(BF16)

    for m in range(1, NP):
        sp_copy(m).wait_recv()
    tiles = sv[ybit]
    for m in range(1, NP):
        tiles = tiles + rv[m]
    for dd in range(NZ):
        ebt = jnp.broadcast_to(geb_row[:, 128 * dd : 128 * (dd + 1)], (8, 128))
        zt[dd] = jnp.where(rows8 == 3, ebt, tiles[dd])

    def sz_copy(i, incoming):
        return rc(zt.at[other(i)], rzv.at[i], sz_s.at[i], sz_r.at[i], other(i), s)

    for i in range(1, NZ):
        sz_copy(i, False).start()
    total_rows(0, 256)
    for m in range(1, NP):
        back_copy(0, m, False).start()
    rs_last(1)
    loop(rows // 32, grad_final)
    ref_o, use_o = zr_total(3)
    tout_ref[...] = zr_sum(3, use_o, ref_o[...].astype(F32), 0, 32)

    mine = pl.ds(aligned(256 * d + 32 * s, 32), 32)
    ra_exp[0] = gexp[mine, :]
    ra_in[0] = gin[mine, :]
    for m in range(1, NP):
        back_copy(1, m, True).wait_recv()
        ra_exp[m] = rb_exp[m]
    for m in range(1, NP):
        back_copy(0, m, True).wait_recv()
        ra_in[m] = rb_in[m]
    for i in range(1, NZ):
        sz_copy(i, True).wait_recv()
    tile = zt[d]
    for i in range(1, NZ):
        tile = tile + rzv[i]
    tile_ref[...] = jnp.where(rows8 == 3, tile, pltpu.roll(tile, lax.rem(128 - 32 * quad, 128), 1))

    for m in range(1, NP):
        a2a_msg(0, m).wait_send()
        a2a_msg(1, m).wait_send()
        vp_copy(m, False).wait_send()
        back_copy(0, m, False).wait_send()
        back_copy(1, m, False).wait_send()
        sp_copy(m).wait_send()
    for m in range(1, 4):
        wo_copy(m, False).wait_send()
        go_copy(m, False).wait_send()
    for i in range(1, NZ):
        vz_copy(i, False).wait_send()
        sz_copy(i, False).wait_send()
    for i in range(9):
        ag_copy(1, i, False).wait_send()
    for w in range(2):
        for i in range(8):
            rs_copy(w, i).wait_send()
    for a in range(4):
        z_sent(a)
        zr_sent(a)


def update_kernel(*refs):
    weights, moments = refs[0:8], refs[8:16]
    rate_ref, decay_ref, hout_in, hgrad_in, gin, gexp, gred, gout, tile = refs[16:25]
    hout, hgrad = refs[25:27]
    new_moments, new_weights = refs[27:35], refs[35:43]
    s = lax.axis_index("seq")
    keep = 1.0 - decay_ref[0]
    rate = rate_ref[0]

    def update(k, index, grad):
        moment = 0.5 * moments[k][index] + grad * (0.5 / NZ)
        new_moments[k][index] = moment
        new_weights[k][index] = keep * weights[k][index] - rate * moment

    hout[...] = hout_in[...]
    hgrad[...] = hgrad_in[...]
    gain = weights[0][...].astype(BF16).astype(F32)
    shift = weights[1][...].astype(BF16).astype(F32)
    shift_grad = tile[1:2, :32]
    update(0, ..., (tile[0:1, :32] - shift * shift_grad) / gain)
    update(1, ..., shift_grad)
    update(7, ..., tile[2:3, :32])
    update(5, ..., tile[3:4, :])
    update(6, ..., gred[...])
    update(3, ..., gout[...])
    core = lax.rem(s, 2)
    xbit = lax.rem(lax.div(s, 2), 2)
    ybit = lax.div(s, 4)
    for m in range(NP):
        t = s
        if m & 1:
            t = t + (1 - 2 * core)
        if m & 2:
            t = t + 2 * (1 - 2 * xbit)
        if m & 4:
            t = t + 4 * (1 - 2 * ybit)
        pair = 2 * lax.rem(t, 4) + lax.div(t, 4)
        for part in range(3):
            cols = pl.ds(aligned(128 * pair + 1024 * part, 128), 128)
            update(2, (slice(None), cols), gin[m, :, 128 * part : 128 * (part + 1)].astype(F32))
        for e in range(NZ):
            cols = pl.ds(aligned(128 * (8 * e + t), 128), 128)
            update(4, (slice(None), cols), gexp[m, :, 128 * e : 128 * (e + 1)].astype(F32))


def fused_shards(*args):
    (hidden_in, out_cotangent), weights, moments = args[:2], args[2:10], args[10:18]
    rows = hidden_in.shape[1]
    seq = rows * NP
    freq = 10000.0 ** (-2.0 * np.arange(ROT // 2) / ROT)
    lane_freq = np.tile(freq, 128 // (ROT // 2))[None, :]
    near = np.arange(rows)[:, None] * lane_freq
    far = (rows * np.arange(NP))[:, None] * lane_freq
    tables = [jnp.asarray(f(a), F32) for a in (near, far) for f in (np.cos, np.sin)]

    def flat(v):
        return v.reshape(1, -1) if v.ndim == 1 else v

    shards_in = [flat(w) for w in weights]
    ff = weights[6].shape[0] * NZ
    moments_in = [flat(m) for m in moments]
    shard_shapes = [jax.ShapeDtypeStruct(w.shape, F32) for w in shards_in]
    vm = pltpu.VMEM
    dma = pltpu.SemaphoreType.DMA
    scratch = [
        vm((seq, D), BF16), vm((seq, D), BF16), vm((seq, D), BF16),
        vm((D, 384), BF16), vm((D, ff), BF16), vm((ff, D), BF16), vm((128, D), BF16), vm((NZ, 32, D), BF16),
        vm((NP, 32, 384), BF16), vm((NP, 32, ff), BF16),
        vm((seq, 128), BF16), vm((seq, 128), BF16), vm((seq, 256), BF16), vm((seq, 128), BF16), vm((seq, 128), BF16),
        vm((128, seq), F32), vm((128, seq), F32), vm((seq, 384), BF16),
        vm((2, NP // 2, rows, 2 * rows), F32), vm((2, seq, 128), F32),
        vm((2, rows, 128), F32), vm((2, rows, 256), F32), vm((2, rows, 128), F32),
        vm((seq, ff), BF16), vm((seq, ff), BF16), vm((seq, D), BF16),
        vm((4, rows, D), BF16), vm((4, rows, D), BF16),
        vm((2, rows // 2, D), BF16), vm((2, rows, D), BF16), vm((2, rows // 2, D), BF16), vm((2, rows, D), BF16),
        vm((D, 384), BF16), vm((D, ff), BF16), vm((ff, D), BF16), vm((128, D), BF16), vm((NZ, 32, D), BF16),
        vm((NZ, 256, 384), BF16), vm((NZ, 256, ff), BF16), vm((NZ, 128, D), BF16), vm((NZ, 32, D), BF16),
        vm((NP, 32, 384), BF16), vm((NP, 32, ff), BF16),
        vm((NP, NZ, 8, 128), F32), vm((8, D), F32), vm((8, ff), F32), vm((8, D), F32),
        vm((2, NZ, 8, 128), F32), vm((NP, NZ, 8, 128), F32), vm((NZ, 8, 128), F32), vm((NZ, 8, 128), F32),
        dma((2, NP)), dma((2, NP)), dma((2, 9)), dma((2, 9)), dma((4, 5)), dma((4, 4)),
        dma((NZ,)), dma((NZ,)), dma((NP,)), dma((NP,)), dma((4,)), dma((4,)),
        dma((2, 8)), dma((2, 8)), dma((4, 4)), dma((4, 4)), dma((4,)), dma((4,)),
        dma((2, NP)), dma((2, NP)), dma((NP,)), dma((NP,)), dma((NZ,)), dma((NZ,)),
    ]
    in_vmem = pl.BlockSpec(memory_space=pltpu.VMEM)
    in_smem = pl.BlockSpec(memory_space=pltpu.SMEM)

    def body(*refs):
        block_kernel(rows, *refs)

    rows_shape = jax.ShapeDtypeStruct((rows, D), BF16)
    grads = pl.pallas_call(
        body,
        out_shape=[
            rows_shape, rows_shape,
            jax.ShapeDtypeStruct((NP, 32, 384), BF16), jax.ShapeDtypeStruct((NP, 32, ff), BF16),
            jax.ShapeDtypeStruct((128, D), F32), jax.ShapeDtypeStruct((32, D), F32),
            jax.ShapeDtypeStruct((8, 128), F32),
        ],
        in_specs=[in_vmem] * 14,
        out_specs=[in_vmem] * 7,
        scratch_shapes=scratch,
        compiler_params=pltpu.CompilerParams(
            collective_id=0, has_side_effects=True, vmem_limit_bytes=63 * 2**20
        ),
        name="block_step",
    )(
        hidden_in.reshape(rows, D), out_cotangent.reshape(rows, D), *shards_in, *tables,
    )
    outs = pl.pallas_call(
        update_kernel,
        out_shape=[rows_shape, rows_shape] + shard_shapes + shard_shapes,
        in_specs=[in_vmem] * 16 + [in_smem] * 2 + [in_vmem] * 7,
        out_specs=[in_vmem] * 18,
        compiler_params=pltpu.CompilerParams(vmem_limit_bytes=63 * 2**20),
        name="block_update",
    )(*shards_in, *moments_in, args[18], args[19], *grads)
    small = [w.shape for w in weights]
    return (
        outs[0].reshape(hidden_in.shape),
        outs[1].reshape(hidden_in.shape),
        *[o.reshape(sh) for o, sh in zip(outs[2:], small + small)],
    )


def fits(mesh):
    return mesh.shape["dp"] == NZ and mesh.shape["seq"] == NP


def solution(mesh):
    placed = (
        P("dp", "seq", None),
        P("dp", "seq", None),
        P(("dp", "seq")),
        P(("dp", "seq")),
        P(("dp", "seq"), None),
        P(("dp", "seq"), None),
        P(("dp", "seq"), None),
        P(("dp", "seq")),
        P(("dp", "seq"), None),
        P(("dp", "seq")),
        P(("dp", "seq")),
        P(("dp", "seq")),
        P(("dp", "seq"), None),
        P(("dp", "seq"), None),
        P(("dp", "seq"), None),
        P(("dp", "seq")),
        P(("dp", "seq"), None),
        P(("dp", "seq")),
        P(),
        P(),
    )
    return jax.shard_map(
        fused_shards if fits(mesh) else shards,
        mesh=mesh,
        in_specs=placed,
        out_specs=(
            P("dp", "seq", None),
            P("dp", "seq", None),
            P(("dp", "seq")),
            P(("dp", "seq")),
            P(("dp", "seq"), None),
            P(("dp", "seq"), None),
            P(("dp", "seq"), None),
            P(("dp", "seq")),
            P(("dp", "seq"), None),
            P(("dp", "seq")),
            P(("dp", "seq")),
            P(("dp", "seq")),
            P(("dp", "seq"), None),
            P(("dp", "seq"), None),
            P(("dp", "seq"), None),
            P(("dp", "seq")),
            P(("dp", "seq"), None),
            P(("dp", "seq")),
        ),
        check_vma=False,
    )
```

```python
import jax
import jax.numpy as jnp
import numpy as np
from jax import lax
from jax.experimental import pallas as pl
from jax.experimental.pallas import tpu as pltpu
from jax.sharding import PartitionSpec as P

D = 1024
H = 16
HD = 64
ROT = 32


epsilon = 1e-05
masked_score = -1e30


def rotary(block, positions, direction):
    half_rot = ROT // 2
    frequency = 10000.0 ** (-2.0 * jnp.arange(half_rot, dtype=jnp.float32) / ROT)
    angles = direction * positions[:, None] * frequency[None, :]
    cosine = jnp.cos(angles)[:, None, :]
    sine_part = jnp.sin(angles)[:, None, :]
    first_half = block[..., :half_rot]
    second = block[..., half_rot:ROT]
    return jnp.concatenate(
        [
            first_half * cosine - second * sine_part,
            second * cosine + first_half * sine_part,
            block[..., ROT:],
        ],
        axis=-1,
    )


def gelu_tanh(values):
    return jax.nn.gelu(values, approximate=True)


def gelu_back(expanded, upstream):
    unused_out, pullback = jax.vjp(gelu_tanh, expanded)
    return pullback(upstream)[0]


def heads_of(rows):
    return rows.reshape(rows.shape[0], H, HD)


def scores_of(query_rows, key_rows):
    score_scale = HD ** (-0.5)
    return (
        jnp.einsum(
            "qhd,khd->hqk",
            heads_of(query_rows),
            heads_of(key_rows),
            preferred_element_type=jnp.float32,
        )
        * score_scale
    )


def shards(
    hidden_in,
    out_cotangent,
    norm_gain,
    norm_shift,
    attend_in,
    attend_out,
    expand_weight,
    expand_bias,
    reduce_weight,
    reduce_bias,
    gain_moment,
    shift_moment,
    inward_moment,
    outward_moment,
    expand_moment,
    expbias_moment,
    reduce_moment,
    redbias_moment,
    learn_rate,
    decay_rate,
):
    score_scale = HD ** (-0.5)
    gain_low, shift_low, inward_mat, outward_mat, expand_mat, expand_vec, reduce_mat, reduce_vec = (
        lax.all_gather(norm_gain.astype(jnp.bfloat16), ("dp", "seq"), axis=0, tiled=True),
        lax.all_gather(norm_shift.astype(jnp.bfloat16), ("dp", "seq"), axis=0, tiled=True),
        lax.all_gather(attend_in.astype(jnp.bfloat16), ("dp", "seq"), axis=0, tiled=True),
        lax.all_gather(attend_out.astype(jnp.bfloat16), ("dp", "seq"), axis=0, tiled=True),
        lax.all_gather(expand_weight.astype(jnp.bfloat16), ("dp", "seq"), axis=0, tiled=True),
        lax.all_gather(expand_bias.astype(jnp.bfloat16), ("dp", "seq"), axis=0, tiled=True),
        lax.all_gather(reduce_weight.astype(jnp.bfloat16), ("dp", "seq"), axis=0, tiled=True),
        lax.all_gather(reduce_bias.astype(jnp.bfloat16), ("dp", "seq"), axis=0, tiled=True),
    )
    seq_count, block_len, model_width = hidden_in.shape
    row_count = seq_count * block_len
    full_len = block_len * lax.axis_size("seq")
    seq_start = lax.axis_index("seq") * block_len
    query_index = seq_start + jnp.arange(block_len, dtype=jnp.int32)
    key_index = jnp.arange(full_len, dtype=jnp.int32)
    causal = key_index[None, :] <= query_index[:, None]
    positions = query_index.astype(jnp.float32)
    inputs = hidden_in.astype(jnp.float32).reshape(row_count, model_width)
    row_mean = jnp.mean(inputs, axis=-1, keepdims=True)
    centred = inputs - row_mean
    row_var = jnp.mean(centred * centred, axis=-1, keepdims=True)
    inverse = lax.rsqrt(row_var + epsilon)
    unit_rows = centred * inverse
    gain_full = gain_low.astype(jnp.float32)
    normed = (unit_rows * gain_full + shift_low.astype(jnp.float32)).astype(jnp.bfloat16)
    joined = jnp.dot(normed, inward_mat, preferred_element_type=jnp.float32).reshape(
        seq_count, block_len, 3 * D
    )
    query = (
        rotary(joined[..., :D].reshape(seq_count, block_len, H, HD), positions, 1.0)
        .astype(jnp.bfloat16)
        .reshape(seq_count, block_len, D)
    )
    keyed = (
        rotary(joined[..., D : 2 * D].reshape(seq_count, block_len, H, HD), positions, 1.0)
        .astype(jnp.bfloat16)
        .reshape(seq_count, block_len, D)
    )
    valued = joined[..., 2 * D :].astype(jnp.bfloat16)
    key_all, value_all = (
        lax.all_gather(keyed, "seq", axis=1, tiled=True),
        lax.all_gather(valued, "seq", axis=1, tiled=True),
    )

    def attend(operands):
        query_seq, key_seq, value_seq = operands
        scores = jnp.where(causal[None], scores_of(query_seq, key_seq), masked_score)
        row_max = jnp.max(scores, axis=-1, keepdims=True)
        log_total = row_max + jnp.log(jnp.sum(jnp.exp(scores - row_max), axis=-1, keepdims=True))
        weights = jnp.exp(scores - log_total).astype(jnp.bfloat16)
        mixed = jnp.einsum(
            "hqk,khd->qhd", weights, heads_of(value_seq), preferred_element_type=jnp.float32
        )
        return (mixed.reshape(-1, D).astype(jnp.bfloat16), jnp.transpose(log_total[..., 0]))

    attended, log_totals = lax.map(attend, (query, key_all, value_all))
    expanded = jnp.dot(normed, expand_mat, preferred_element_type=jnp.float32) + expand_vec.astype(
        jnp.float32
    )
    activated = gelu_tanh(expanded).astype(jnp.bfloat16)
    flat_attn = attended.reshape(row_count, D)
    result = (
        inputs
        + jnp.dot(flat_attn, outward_mat, preferred_element_type=jnp.float32)
        + jnp.dot(activated, reduce_mat, preferred_element_type=jnp.float32)
        + reduce_vec.astype(jnp.float32)
    )
    hidden_out = result.astype(jnp.bfloat16).reshape(seq_count, block_len, D)
    upstream = out_cotangent.reshape(row_count, D)
    grad_outward = jnp.einsum("rd,re->de", flat_attn, upstream, preferred_element_type=jnp.float32)
    grad_reduce = jnp.einsum("rf,re->fe", activated, upstream, preferred_element_type=jnp.float32)
    grad_redbias = jnp.sum(upstream.astype(jnp.float32), axis=0)
    attn_back = (
        jnp.einsum("re,de->rd", upstream, outward_mat, preferred_element_type=jnp.float32)
        .astype(jnp.bfloat16)
        .reshape(seq_count, block_len, D)
    )
    act_back = jnp.einsum("re,fe->rf", upstream, reduce_mat, preferred_element_type=jnp.float32)
    expand_back = gelu_back(expanded, act_back).astype(jnp.bfloat16)
    grad_expbias = jnp.sum(expand_back.astype(jnp.float32), axis=0)
    grad_expand = jnp.einsum("rd,rf->df", normed, expand_back, preferred_element_type=jnp.float32)
    norm_back = jnp.einsum("rf,df->rd", expand_back, expand_mat, preferred_element_type=jnp.float32)

    def query_side(query_seq, key_seq, value_seq, back_seq, total_seq):
        scores = jnp.where(causal[None], scores_of(query_seq, key_seq), masked_score)
        probs = jnp.exp(scores - jnp.transpose(total_seq)[:, :, None])
        prob_grad = jnp.einsum(
            "qhd,khd->hqk",
            heads_of(back_seq),
            heads_of(value_seq),
            preferred_element_type=jnp.float32,
        )
        row_delta = jnp.sum(probs * prob_grad, axis=-1, keepdims=True)
        score_grad = (probs * (prob_grad - row_delta)).astype(jnp.bfloat16)
        query_grad = (
            jnp.einsum(
                "hqk,khd->qhd", score_grad, heads_of(key_seq), preferred_element_type=jnp.float32
            )
            * score_scale
        )
        return (probs, score_grad, query_grad, row_delta)

    def attend_back(operands):
        query_seq, key_seq, value_seq, back_seq, total_seq = operands
        probs, score_grad, query_grad, row_delta = query_side(
            query_seq, key_seq, value_seq, back_seq, total_seq
        )
        key_grad = (
            jnp.einsum(
                "hqk,qhd->khd", score_grad, heads_of(query_seq), preferred_element_type=jnp.float32
            )
            * score_scale
        )
        value_grad = jnp.einsum(
            "hqk,qhd->khd",
            probs.astype(jnp.bfloat16),
            heads_of(back_seq),
            preferred_element_type=jnp.float32,
        )
        return (query_grad, key_grad.reshape(-1, D), value_grad.reshape(-1, D))

    query_grads, key_terms, value_terms = lax.map(
        attend_back, (query, key_all, value_all, attn_back, log_totals)
    )
    key_grads, value_grads = (
        lax.psum_scatter(key_terms, "seq", scatter_dimension=1, tiled=True),
        lax.psum_scatter(value_terms, "seq", scatter_dimension=1, tiled=True),
    )
    query_turned = rotary(query_grads, positions, -1.0).reshape(seq_count, block_len, D)
    key_turned = rotary(key_grads.reshape(seq_count, block_len, H, HD), positions, -1.0).reshape(
        seq_count, block_len, D
    )
    joined_back = (
        jnp.concatenate([query_turned, key_turned, value_grads], axis=-1)
        .astype(jnp.bfloat16)
        .reshape(row_count, 3 * D)
    )
    grad_inward = jnp.einsum("rd,re->de", normed, joined_back, preferred_element_type=jnp.float32)
    norm_back = norm_back + jnp.einsum(
        "re,de->rd", joined_back, inward_mat, preferred_element_type=jnp.float32
    )
    grad_gain = jnp.sum(norm_back * unit_rows, axis=0)
    grad_shift = jnp.sum(norm_back, axis=0)
    unit_back = norm_back * gain_full
    input_back = inverse * (
        unit_back
        - jnp.mean(unit_back, axis=-1, keepdims=True)
        - unit_rows * jnp.mean(unit_back * unit_rows, axis=-1, keepdims=True)
    ) + upstream.astype(jnp.float32)
    hidden_grad = input_back.astype(jnp.bfloat16).reshape(seq_count, block_len, D)
    totals = (
        lax.psum_scatter(grad_gain, ("dp", "seq"), scatter_dimension=0, tiled=True),
        lax.psum_scatter(grad_shift, ("dp", "seq"), scatter_dimension=0, tiled=True),
        lax.psum_scatter(grad_inward, ("dp", "seq"), scatter_dimension=0, tiled=True),
        lax.psum_scatter(grad_outward, ("dp", "seq"), scatter_dimension=0, tiled=True),
        lax.psum_scatter(grad_expand, ("dp", "seq"), scatter_dimension=0, tiled=True),
        lax.psum_scatter(grad_expbias, ("dp", "seq"), scatter_dimension=0, tiled=True),
        lax.psum_scatter(grad_reduce, ("dp", "seq"), scatter_dimension=0, tiled=True),
        lax.psum_scatter(grad_redbias, ("dp", "seq"), scatter_dimension=0, tiled=True),
    )
    seq_total = seq_count * lax.axis_size("dp")
    step_rate = learn_rate[0]
    decay_now = decay_rate[0]
    params = (
        norm_gain,
        norm_shift,
        attend_in,
        attend_out,
        expand_weight,
        expand_bias,
        reduce_weight,
        reduce_bias,
    )
    moments = (
        gain_moment,
        shift_moment,
        inward_moment,
        outward_moment,
        expand_moment,
        expbias_moment,
        reduce_moment,
        redbias_moment,
    )
    momenta = [
        0.5 * moment + 0.5 * (summed_grad / seq_total)
        for moment, summed_grad in zip(moments, totals)
    ]
    updated = [
        (1.0 - decay_now) * weight_now - step_rate * momentum
        for weight_now, momentum in zip(params, momenta)
    ]
    return (
        hidden_out,
        hidden_grad,
        momenta[0],
        momenta[1],
        momenta[2],
        momenta[3],
        momenta[4],
        momenta[5],
        momenta[6],
        momenta[7],
        updated[0],
        updated[1],
        updated[2],
        updated[3],
        updated[4],
        updated[5],
        updated[6],
        updated[7],
    )


F32 = jnp.float32
BF16 = jnp.bfloat16
MESH = pl.DeviceIdType.MESH
NZ = 4
NP = 8
NT = (((1,), (1,)), ((), ()))
TN = (((0,), (0,)), ((), ()))


def dot(a, b):
    return jnp.dot(a, b, preferred_element_type=F32)


def dot_nt(a, b):
    return lax.dot_general(a, b, NT, preferred_element_type=F32)


def dot_tn(a, b):
    return lax.dot_general(a, b, TN, preferred_element_type=F32)


def aligned(value, unit):
    return pl.multiple_of(value, unit)


def gelu_pair(e):
    square = e * e
    t = jnp.tanh(e * (GELU_C + (GELU_C * GELU_A) * square))
    half = 0.5 + 0.5 * t
    slope = half + (0.5 * e) * (1.0 - t * t) * (GELU_C + (3.0 * GELU_C * GELU_A) * square)
    return e * half, slope


GELU_C = 0.7978845608028654
GELU_A = 0.044715


def block_kernel(rows, *refs):
    (
        x_ref, dy_ref, gain_ref, shift_ref, win_ref, wout_ref, wexp_ref, ebias_ref, wred_ref, rbias_ref,
        cosr_ref, sinr_ref, cosb_ref, sinb_ref,
        hout_ref, hgrad_ref, ra_in, ra_exp, tred_ref, tout_ref, tile_ref,
        xg, dyg, xn, win, wexp, wred, wout, wz, pin, pexp,
        o_s, do_s, dkt, dvt, dfused, sbuf, lse, mref, acc,
        act_s, de_s, pdn, sib_o, sib_d, r1_o, r2_o, r1_d, r2_d,
        gin, gexp, gred, gout, gz, rz_in, rz_exp, rz_red, rz_out, rb_in, rb_exp,
        vt, vecs, ebs, geb, sums, sv, rv, zt, rzv,
        a2a_s, a2a_r, ag_s, ag_r, z_s, z_r, vz_s, vz_r, vp_s, vp_r, wo_s, wo_r,
        rs_s, rs_r, zr_s, zr_r, go_s, go_r, b_s, b_r, sp_s, sp_r, sz_s, sz_r, dy_sem,
    ) = refs
    pout = xg
    d = lax.axis_index("dp")
    s = lax.axis_index("seq")
    core = lax.rem(s, 2)
    xbit = lax.rem(lax.div(s, 2), 2)
    ybit = lax.div(s, 4)
    chip = lax.div(s, 2)
    quad = lax.rem(s, 4)

    def peer(m):
        out = s
        if m & 1:
            out = out + (1 - 2 * core)
        if m & 2:
            out = out + 2 * (1 - 2 * xbit)
        if m & 4:
            out = out + 4 * (1 - 2 * ybit)
        return out

    def pair_of(t):
        return 2 * lax.rem(t, 4) + lax.div(t, 4)

    def rc(src, dst, ssem, rsem, dd, ss):
        return pltpu.make_async_remote_copy(
            src_ref=src, dst_ref=dst, send_sem=ssem, recv_sem=rsem,
            device_id=(dd, ss), device_id_type=MESH,
        )

    barrier = pltpu.get_barrier_semaphore()
    for m in range(1, NP):
        pl.semaphore_signal(barrier, inc=1, device_id=(d, peer(m)), device_id_type=MESH)
    for dz in range(1, NZ):
        pl.semaphore_signal(barrier, inc=1, device_id=(lax.rem(d + dz, NZ), s), device_id_type=MESH)

    zrow = jnp.zeros((1, 96), F32)
    small = jnp.concatenate(
        [
            jnp.concatenate([r[...].astype(BF16).astype(F32), zrow], axis=1)
            for r in (gain_ref, shift_ref, rbias_ref)
        ]
        + [jnp.zeros((5, 128), F32)],
        axis=0,
    )
    small = pltpu.roll(small, 32 * quad, 1)
    rows8 = lax.broadcasted_iota(jnp.int32, (8, 128), 0)
    ebias_row = jnp.broadcast_to(ebias_ref[...].astype(BF16).astype(F32), (8, 128))
    vt[s, d] = jnp.where(rows8 == 3, ebias_row, small)
    wz[d] = wout_ref[...].astype(BF16)
    own_dy = pltpu.make_async_copy(dy_ref, dyg.at[pl.ds(aligned(rows * s, rows), rows)], dy_sem)
    own_dy.start()
    xg[pl.ds(aligned(rows * s, rows), rows), :] = x_ref[...]
    own_rows = aligned(32 * (8 * d + s), 32)

    def pack_in():
        for m in range(NP):
            j = pair_of(peer(m))
            for part in range(3):
                piece = win_ref[:, pl.ds(aligned(128 * j + 1024 * part, 128), 128)].astype(BF16)
                if m == 0:
                    win[pl.ds(own_rows, 32), 128 * part : 128 * (part + 1)] = piece
                else:
                    pin[m, :, 128 * part : 128 * (part + 1)] = piece

    def pack_exp():
        for m in range(NP):
            t = peer(m)
            for e in range(NZ):
                piece = wexp_ref[:, pl.ds(aligned(128 * (8 * e + t), 128), 128)].astype(BF16)
                if m == 0:
                    wexp[pl.ds(own_rows, 32), 128 * e : 128 * (e + 1)] = piece
                else:
                    pexp[m, :, 128 * e : 128 * (e + 1)] = piece

    pack_in()
    pl.semaphore_wait(barrier, NP - 1 + NZ - 1)

    def a2a_msg(which, m):
        src = (pin, pexp)[which].at[m]
        dst = (win, wexp)[which].at[pl.ds(own_rows, 32)]
        return rc(src, dst, a2a_s.at[which, m], a2a_r.at[which, m], d, peer(m))

    def a2a_arrived(which, m):
        dst = (win, wexp)[which].at[pl.ds(aligned(32 * (8 * d + peer(m)), 32), 32)]
        rc((pin, pexp)[which].at[m], dst, a2a_s.at[which, m], a2a_r.at[which, m], d, peer(m)).wait_recv()

    half = rows // 2
    AG = (
        (1, 0, 0, rows), (2, 0, 0, rows), (4, 0, 0, rows),
        (1, 2, 0, rows), (1, 4, 0, rows), (4, 2, half, half), (2, 4, 0, half),
        (1, 6, 0, half), (1, 6, half, half),
    )

    def ag_copy(which, i, incoming):
        to, blk, lo, n = AG[i]
        buf = (xg, dyg)[which]
        at = rows * peer(blk ^ (to if incoming else 0)) + lo
        ref = buf.at[pl.ds(aligned(at, half), n)]
        return rc(ref, ref, ag_s.at[which, i], ag_r.at[which, i], d, peer(to))

    def ag_start(which, i):
        ag_copy(which, i, False).start()

    def ag_arrived(which, i):
        ag_copy(which, i, True).wait_recv()

    ZVIEW = (
        lambda b: win.at[pl.ds(aligned(256 * b, 256), 256)],
        lambda b: wexp.at[pl.ds(aligned(256 * b, 256), 256)],
        lambda b: wred.at[pl.ds(aligned(128 * b, 128), 128)],
        lambda b: wz.at[b],
    )

    def z_direct(dest):
        ok = d != dest
        if dest == NZ - 1:
            ok = ok & (d != 0)
        if dest == 0:
            ok = ok & (d != NZ - 1)
        return ok

    def z_send(a):
        for dest in (3, 0, 2, 1):
            @pl.when(z_direct(dest))
            def _():
                rc(ZVIEW[a](d), ZVIEW[a](d), z_s.at[a, dest], z_r.at[a, d], dest, s).start()

    FWD = ((2, 0, 3), (1, 3, 0))

    def z_wait_block(a, b):
        rc(ZVIEW[a](b), ZVIEW[a](b), z_s.at[a, 4], z_r.at[a, b], d, s).wait_recv()

    def z_forward(a):
        for at, blk, dest in FWD:
            @pl.when(d == at)
            def _():
                z_wait_block(a, blk)
                rc(ZVIEW[a](blk), ZVIEW[a](blk), z_s.at[a, 4], z_r.at[a, blk], dest, s).start()

    PACE = ((0, 1), (3, 2))

    def z_pace(a):
        for at, blk in PACE:
            @pl.when(d == at)
            def _():
                z_wait_block(a, blk)

    def z_arrived(a, paced=False):
        for b in range(NZ):
            need = d != b
            for at, blk, dest in FWD:
                if blk == b:
                    need = need & (d != at)
            for at, blk in PACE:
                if paced and blk == b:
                    need = need & (d != at)

            @pl.when(need)
            def _():
                z_wait_block(a, b)

    def z_sent(a):
        for dest in range(NZ):
            @pl.when(z_direct(dest))
            def _():
                rc(ZVIEW[a](d), ZVIEW[a](d), z_s.at[a, dest], z_r.at[a, d], dest, s).wait_send()
        for at, blk, dest in FWD:
            @pl.when(d == at)
            def _():
                rc(ZVIEW[a](blk), ZVIEW[a](blk), z_s.at[a, 4], z_r.at[a, blk], dest, s).wait_send()

    def other(i):
        return lax.rem(d + i, NZ)

    def vz_copy(i, incoming):
        b = lax.rem(d + NZ - i, NZ) if incoming else d
        return rc(vt.at[s, b], vt.at[s, b], vz_s.at[i], vz_r.at[i], other(i), s)

    def vp_copy(m, incoming):
        b = peer(m) if incoming else s
        return rc(vt.at[b], vt.at[b], vp_s.at[m], vp_r.at[m], d, peer(m))

    for i in range(1, NZ):
        vz_copy(i, False).start()
    for m in range(1, NP):
        a2a_msg(0, m).start()
    z_send(3)
    for i in (1, 2, 0):
        ag_start(0, i)
    pack_exp()
    wred[pl.ds(aligned(128 * d, 128), 128), :] = wred_ref[...].astype(BF16)
    for i in range(1, NZ):
        vz_copy(i, True).wait_recv()
    for m in range(1, NP):
        vp_copy(m, False).start()
    for m in range(1, NP):
        a2a_arrived(0, m)
    z_send(0)
    for m in range(1, NP):
        a2a_msg(1, m).start()
    z_forward(3)
    z_pace(0)
    z_forward(0)
    z_send(2)
    ag_arrived(0, 1)
    ag_start(0, 5)
    ag_start(0, 3)
    ag_arrived(0, 2)
    ag_start(0, 6)
    ag_start(0, 4)
    for m in range(1, NP):
        a2a_arrived(1, m)
    z_send(1)

    def wo_copy(m, incoming):
        src = wz.at[lax.rem(peer(m), 4)]
        r = lax.rem(peer(m), 4) if incoming else quad
        dst = wout.at[pl.ds(aligned(32 * r, 32), 32)]
        return rc(src, dst, wo_s.at[m], wo_r.at[m], d, peer(m))

    for m in range(1, NP):
        vp_copy(m, True).wait_recv()
    for dd in range(NZ):
        for yy in range(2):
            group = 2 * dd + yy
            total = vt[4 * yy, dd]
            for jj in range(1, 4):
                total = total + vt[4 * yy + jj, dd]
            vecs[:, 128 * group : 128 * (group + 1)] = total

    def unit_of(xb):
        xf = xb.astype(F32)
        mu = jnp.mean(xf, axis=1, keepdims=True)
        cen = xf - mu
        var = jnp.mean(cen * cen, axis=1, keepdims=True)
        inv = lax.rsqrt(var + epsilon)
        return cen * inv, inv

    def norm_block(b):
        def step(c, carry):
            at = aligned(rows * b + 64 * c, 64)
            unit, _ = unit_of(xg[pl.ds(at, 64), :])
            xn[pl.ds(at, 64), :] = (unit * vecs[0:1, :] + vecs[1:2, :]).astype(BF16)
            return carry
        lax.fori_loop(0, rows // 64, step, 0)

    lane_b = lax.broadcasted_iota(jnp.int32, (rows, 128), 1)
    low_head = lane_b < HD
    in_head = lax.rem(lane_b, HD)
    first_rot = in_head < ROT // 2
    second_rot = (in_head >= ROT // 2) & (in_head < ROT)

    def angles(b):
        cb, sb = cosb_ref[pl.ds(b, 1), :], sinb_ref[pl.ds(b, 1), :]
        cr, sr = cosr_ref[...], sinr_ref[...]
        co = jnp.where(in_head < ROT, cr * cb - sr * sb, 1.0)
        si = sr * cb + cr * sb
        return co, jnp.where(first_rot, -si, 0.0), jnp.where(second_rot, si, 0.0)

    def turn(block, table, back=False):
        co, up, down = table
        moved = pltpu.roll(block, 128 - ROT // 2, 1) * up + pltpu.roll(block, ROT // 2, 1) * down
        return block * co - moved if back else block * co + moved

    norm_block(s)
    ag_arrived(0, 0)
    norm_block(peer(1))
    own_dy.wait()
    for i in (1, 2, 0):
        ag_start(1, i)
    norm_block(peer(2))
    norm_block(peer(4))
    ag_arrived(0, 3)
    norm_block(peer(3))
    ag_arrived(0, 4)
    norm_block(peer(5))
    ag_arrived(0, 6)
    ag_start(0, 7)
    ag_arrived(0, 5)
    ag_start(0, 8)
    norm_block(peer(6))
    ag_arrived(0, 7)
    ag_arrived(0, 8)
    norm_block(peer(7))
    z_arrived(3)
    for m in range(1, 4):
        wo_copy(m, False).start()
    wout[pl.ds(aligned(32 * quad, 32), 32), :] = wz[quad]
    z_arrived(0, paced=True)

    def qkv_step(b, carry):
        at = aligned(rows * b, rows)
        joined = dot(xn[pl.ds(at, rows), :], win[...])
        table = angles(b)
        dfused[pl.ds(at, rows), :128] = (turn(joined[:, :128], table) * HD**-0.5).astype(BF16)
        dfused[pl.ds(at, rows), 128:256] = turn(joined[:, 128:256], table).astype(BF16)
        dfused[pl.ds(at, rows), 256:] = joined[:, 256:].astype(BF16)
        return carry

    lax.fori_loop(0, NP, qkv_step, 0)
    QB = 2 * rows
    lane_q = lax.broadcasted_iota(jnp.int32, (QB, 128), 1) < HD

    def wide(tile):
        return jnp.concatenate([tile] * (QB // 128), axis=1)

    def fold(v):
        out = v[:, :128]
        for c in range(1, QB // 128):
            out = jnp.maximum(out, v[:, 128 * c : 128 * (c + 1)])
        return out

    def by_head(block):
        zero = jnp.zeros_like(block)
        return jnp.where(lane_q, block, zero), jnp.where(lane_q, zero, block)

    def hidden():
        return lax.broadcasted_iota(jnp.int32, (QB, QB), 1) > lax.broadcasted_iota(jnp.int32, (QB, QB), 0)

    ones = jnp.ones((QB, 128), BF16)

    def attend_step(i, carry):
        at = aligned(QB * i, QB)
        qh = by_head(dfused[pl.ds(at, QB), :128])
        kj = dfused[pl.ds(at, QB), 128:256]
        mask = hidden()
        for h in range(2):
            sc = jnp.where(mask, masked_score, dot_nt(qh[h], kj))
            sbuf[h, i] = sc
            mref[h] = fold(sc)

        def scores(j, c2):
            kk = dfused[pl.ds(aligned(QB * j, QB), QB), 128:256]
            for h in range(2):
                sc = dot_nt(qh[h], kk)
                sbuf[h, j] = sc
                mref[h] = jnp.maximum(mref[h], fold(sc))
            return c2

        lax.fori_loop(0, i, scores, 0)
        for h in range(2):
            mref[h] = jnp.broadcast_to(jnp.max(mref[h], axis=1, keepdims=True), (QB, 128))
            acc[h] = jnp.zeros((QB, 256), F32)

        def weigh(j, c2):
            vj = jnp.concatenate([dfused[pl.ds(aligned(QB * j, QB), QB), 256:], ones], axis=1)
            for h in range(2):
                pj = jnp.exp(sbuf[h, j] - wide(mref[h])).astype(BF16)
                acc[h] = acc[h] + dot(pj, vj)
            return c2

        lax.fori_loop(0, i + 1, weigh, 0)
        o_s[pl.ds(at, QB), :] = jnp.where(
            lane_q, acc[0][:, :128] / acc[0][:, 128:], acc[1][:, :128] / acc[1][:, 128:]
        ).astype(BF16)
        lse[pl.ds(at, QB), :] = jnp.where(
            lane_q, mref[0] + jnp.log(acc[0][:, 128:]), mref[1] + jnp.log(acc[1][:, 128:])
        )

        @pl.when(i == 1)
        def _():
            z_forward(2)

        @pl.when(i == 1)
        def _():
            ag_arrived(1, 1)
            ag_start(1, 5)
            ag_start(1, 3)
            ag_arrived(1, 2)
            ag_start(1, 6)
            ag_start(1, 4)
        return carry

    lax.fori_loop(0, NP // 2, attend_step, 0)
    z_forward(1)
    ag_arrived(1, 6)
    ag_start(1, 7)
    ag_arrived(1, 5)
    ag_start(1, 8)

    dkt[...] = jnp.zeros_like(dkt)
    dvt[...] = jnp.zeros_like(dvt)

    def attend_back(i):
        at = aligned(QB * i, QB)
        qi = dfused[pl.ds(at, QB), :128]
        doi = do_s[pl.ds(at, QB), :]
        dof = doi.astype(F32)
        qh = by_head(qi)
        doh = by_head(doi)
        qt = jnp.transpose(qi.astype(F32)).astype(BF16)
        dot_t = jnp.transpose(dof).astype(BF16)
        parts = by_head(dof * o_s[pl.ds(at, QB), :].astype(F32))
        for h in range(2):
            mref[h] = jnp.broadcast_to(jnp.sum(parts[h], axis=1, keepdims=True), (QB, 128))
            acc[h, :, :128] = jnp.broadcast_to(lse[pl.ds(at, QB), HD * h : HD * h + 1], (QB, 128))
            acc[h, :, 128:] = jnp.zeros((QB, 128), F32)

        def unit(j, mask):
            ja = aligned(QB * j, QB)
            kk = dfused[pl.ds(ja, QB), 128:256]
            vj = dfused[pl.ds(ja, QB), 256:]
            for h in range(2):
                hs = slice(HD * h, HD * (h + 1))
                p = jnp.exp(dot_nt(qh[h], kk) - wide(acc[h, :, :128]))
                if mask is not None:
                    p = jnp.where(mask, 0.0, p)
                ds = (p * (dot_nt(doh[h], vj) - wide(mref[h]))).astype(BF16)
                acc[h, :, 128:] = acc[h, :, 128:] + dot(ds, kk)
                dkt[hs, pl.ds(ja, QB)] = dkt[hs, pl.ds(ja, QB)] + dot(qt[hs, :], ds)
                dvt[hs, pl.ds(ja, QB)] = dvt[hs, pl.ds(ja, QB)] + dot(dot_t[hs, :], p.astype(BF16))

        def free(j, c2):
            unit(j, None)
            return c2

        lax.fori_loop(0, i, free, 0)
        unit(i, hidden())
        for part in range(2):
            piece = slice(rows * part, rows * (part + 1))
            dq = jnp.where(low_head, acc[0, piece, 128:], acc[1, piece, 128:]) * HD**-0.5
            dfused[pl.ds(aligned(at + rows * part, rows), rows), :128] = turn(dq, angles(2 * i + part), True).astype(BF16)

    GVIEW = (
        lambda b: gin.at[pl.ds(aligned(256 * b, 256), 256)],
        lambda b: gexp.at[pl.ds(aligned(256 * b, 256), 256)],
        lambda b: gred.at[pl.ds(aligned(128 * b, 128), 128)],
        lambda b: gz.at[b],
    )
    RZ = (rz_in, rz_exp, rz_red, rz_out)
    COMB = ((0, 1, 3), (3, 2, 0))

    def zr_direct(dest):
        ok = d != dest
        if dest == 3:
            ok = ok & (d != 0) & (d != 1)
        if dest == 0:
            ok = ok & (d != 3) & (d != 2)
        return ok

    def zr_copy(a, src_block, dest, slot, sem):
        return rc(GVIEW[a](src_block), RZ[a].at[slot], zr_s.at[a, sem], zr_r.at[a, slot], dest, s)

    def zr_first(a):
        for src, via, dest in COMB:
            @pl.when(d == src)
            def _():
                zr_copy(a, dest, via, via, dest).start()

    def zr_send(a):
        for dest in (3, 0, 2, 1):
            @pl.when(zr_direct(dest))
            def _():
                zr_copy(a, dest, dest, d, dest).start()

    def zr_join(a):
        for src, via, dest in COMB:
            @pl.when(d == via)
            def _():
                zr_copy(a, dest, dest, d, dest).wait_recv()
                ref = GVIEW[a](dest)
                ref[...] = (ref[...].astype(F32) + RZ[a][via].astype(F32)).astype(BF16)
                zr_copy(a, dest, dest, d, dest).start()

    def zr_total(a):
        ref = GVIEW[a](d)
        for src in range(NZ):
            came = d != src
            if src == 0:
                came = came & (d != 3)
            if src == 3:
                came = came & (d != 0)

            @pl.when(came)
            def _():
                zr_copy(a, d, d, src, src).wait_recv()
        use = []
        for src in range(NZ):
            came = d != src
            if src == 0:
                came = came & (d != 3)
            if src == 3:
                came = came & (d != 0)
            use.append(came)
        return ref, use

    def zr_sum(a, use, base, at, n):
        total = base
        for src in range(NZ):
            piece = RZ[a][src, pl.ds(at, n), :].astype(F32)
            total = total + jnp.where(use[src], piece, 0.0)
        return total

    def zr_sent(a):
        for dest in range(NZ):
            sent = d != dest

            @pl.when(sent)
            def _():
                zr_copy(a, dest, dest, d, dest).wait_send()

    def dest_send(a, dest):
        for src, via, to in COMB:
            if to == dest:
                @pl.when(d == src)
                def _():
                    zr_copy(a, to, via, via, to).start()

        @pl.when(zr_direct(dest))
        def _():
            zr_copy(a, dest, dest, d, dest).start()

    for i in (0, 3, 4, 7, 8):
        ag_arrived(1, i)
    for m in range(1, 4):
        wo_copy(m, True).wait_recv()

    def loop(n, f):
        def step(i, carry):
            f(i)
            return carry
        lax.fori_loop(0, n, step, 0)

    def do_block(b):
        at = aligned(4 * rows * b, 4 * rows)
        do_s[pl.ds(at, 4 * rows), :] = dot_nt(dyg[pl.ds(at, 4 * rows), :], wout[...]).astype(BF16)

    loop(NP // 4, do_block)
    gout[...] = dot_tn(o_s[...], dyg[...]).astype(BF16)

    def go_copy(m, incoming):
        t4 = lax.rem(peer(m), 4)
        src = gout.at[pl.ds(aligned(32 * t4, 32), 32)]
        dst = gz.at[t4 if incoming else quad]
        return rc(src, dst, go_s.at[m], go_r.at[m], d, peer(m))

    for m in range(1, 4):
        go_copy(m, False).start()
    gz[quad] = gout[pl.ds(aligned(32 * quad, 32), 32), :]
    early = 1

    def back_early(step):
        attend_back(NP // 2 - 1 - step)

    loop(early, back_early)
    for m in range(1, 4):
        go_copy(m, True).wait_recv()
    for dest in (3, 0, 2, 1):
        dest_send(3, dest)
    z_arrived(1)
    z_arrived(2)

    for dd in range(NZ):
        ebs[:, 128 * dd : 128 * (dd + 1)] = jnp.broadcast_to(vt[s, dd, 3:4, :], (8, 128))
    geb[...] = jnp.zeros_like(geb)
    sums[...] = jnp.zeros_like(sums)
    sums[2:3, :] = jnp.sum(dyg[pl.ds(aligned(rows * s, rows), rows), :].astype(F32), axis=0, keepdims=True)

    def ffn_block(b):
        at = pl.ds(aligned(rows * b, rows), rows)
        e = dot(xn[at, :], wexp[...]) + ebs[0:1, :]
        up = dot_nt(dyg[at, :], wred[...])
        a, slope = gelu_pair(e)
        act_s[at, :] = a.astype(BF16)
        de = (up * slope).astype(BF16)
        de_s[at, :] = de
        geb[...] = geb[...] + jnp.sum(de.astype(F32).reshape(rows // 8, 8, 4 * 128), axis=0)

    loop(NP, ffn_block)

    def gexp_block(b):
        at = aligned(256 * b, 256)
        gexp[pl.ds(at, 256), :] = dot_tn(xn[:, pl.ds(at, 256)], de_s[...]).astype(BF16)

    def gred_block(b):
        at = aligned(128 * b, 128)
        gred[pl.ds(at, 128), :] = dot_tn(act_s[:, pl.ds(at, 128)], dyg[...]).astype(BF16)

    for dest in (3, 0, 2, 1):
        gred_block(dest)
        dest_send(2, dest)

    for i in range(9):
        ag_copy(0, i, False).wait_send()

    def chip_rows(m):
        return aligned(2 * rows * lax.div(peer(m), 2), 2 * rows)

    def out_block(m):
        at = pl.ds(chip_rows(m), 2 * rows)
        for c in range(0, D, D // 2):
            cols = slice(c, c + D // 2)
            pout[at, cols] = (dot(o_s[at, :], wout[:, cols]) + dot(act_s[at, :], wred[:, cols])).astype(BF16)

    def dn_block(m):
        at = pl.ds(chip_rows(m), 2 * rows)
        for c in range(0, D, D // 2):
            cols = slice(c, c + D // 2)
            dn = dot_nt(de_s[at, :], wexp[cols, :]) + dot_nt(dfused[at, :], win[cols, :])
            pdn[at, cols] = dn.astype(BF16)
            sums[0:1, cols] = sums[0:1, cols] + jnp.sum(dn * xn[at, cols].astype(F32), axis=0, keepdims=True)
            sums[1:2, cols] = sums[1:2, cols] + jnp.sum(dn, axis=0, keepdims=True)

    RS = ((pout, sib_o, r1_o, r2_o), (pdn, sib_d, r1_d, r2_d))

    def part(which, m, lo, n):
        return RS[which][0].at[pl.ds(aligned(rows * peer(m) + lo, half), n)]

    RSM = (
        (1, 7, 0, rows, lambda w: RS[w][1].at[0]),
        (1, 3, 0, rows, lambda w: RS[w][1].at[1]),
        (1, 5, 0, rows, lambda w: RS[w][1].at[2]),
        (1, 1, 0, rows, lambda w: RS[w][1].at[3]),
        (2, 6, 0, half, lambda w: RS[w][2].at[0]),
        (4, 6, half, half, lambda w: RS[w][2].at[1]),
        (2, 2, 0, half, lambda w: RS[w][3].at[0, pl.ds(0, half)]),
        (4, 4, half, half, lambda w: RS[w][3].at[1, pl.ds(half, half)]),
        (2, 2, half, half, lambda w: RS[w][3].at[0, pl.ds(half, half)]),
        (4, 4, 0, half, lambda w: RS[w][3].at[1, pl.ds(0, half)]),
    )

    def rs_copy(w, i):
        to, blk, lo, n, land = RSM[i]
        return rc(part(w, blk, lo, n), land(w), rs_s.at[w, i], rs_r.at[w, i], d, peer(to))

    def add_into(w, m, lo, n, came):
        def step(c):
            ref = RS[w][0].at[pl.ds(aligned(rows * peer(m) + lo + 64 * c, 64), 64)]
            ref[...] = (ref[...].astype(F32) + came[pl.ds(aligned(64 * c, 64), 64), :].astype(F32)).astype(BF16)
        loop(n // 64, step)

    def rs_across(w):
        rs_copy(w, 0).wait_recv()
        add_into(w, 6, 0, rows, RS[w][1].at[0])
        rs_copy(w, 4).start()
        rs_copy(w, 5).start()

    def rs_pair(w, which):
        rs_copy(w, 1 + which).wait_recv()
        add_into(w, (2, 4)[which], 0, rows, RS[w][1].at[1 + which])
        rs_copy(w, 6 + which).start()

    def rs_near(w, which):
        rs_copy(w, 5 - which).wait_recv()
        add_into(w, (2, 4)[which], (half, 0)[which], half, RS[w][2].at[1 - which])
        rs_copy(w, 8 + which).start()

    def rs_last(w):
        for i in (3, 6, 7, 8, 9):
            rs_copy(w, i).wait_recv()

    for i, m in enumerate((7, 3)):
        out_block(m)
        rs_copy(0, i).start()
    for dest in (3, 0, 2, 1):
        gexp_block(dest)
        dest_send(1, dest)
    for i, m in ((2, 5), (3, 1)):
        out_block(m)
        rs_copy(0, i).start()

    def back_step(step):
        attend_back(NP // 2 - 1 - early - step)

        @pl.when(step == 0)
        def _():
            rs_across(0)
            zr_join(2)
            rs_pair(0, 0)
            rs_pair(0, 1)

        @pl.when(step == 1)
        def _():
            zr_join(3)
            rs_near(0, 0)
            rs_near(0, 1)

        @pl.when(step == 2)
        def _():
            zr_join(1)

    loop(NP // 2 - early, back_step)

    def kv_block(b):
        at = aligned(rows * b, rows)
        dk = jnp.transpose(dkt[:, pl.ds(at, rows)])
        dv = jnp.transpose(dvt[:, pl.ds(at, rows)])
        dfused[pl.ds(at, rows), 128:256] = turn(dk, angles(b), True).astype(BF16)
        dfused[pl.ds(at, rows), 256:] = dv.astype(BF16)

    loop(NP, kv_block)

    def gin_block(b):
        at = aligned(256 * b, 256)
        gin[pl.ds(at, 256), :] = dot_tn(xn[:, pl.ds(at, 256)], dfused[...]).astype(BF16)

    for i, m in enumerate((7, 3, 5)):
        dn_block(m)
        rs_copy(1, i).start()
    rs_across(1)
    dn_block(1)
    for yy in range(2):
        for dd in range(NZ):
            group = 2 * dd + yy
            sv[yy, dd] = sums[:, 128 * group : 128 * (group + 1)]

    def sp_copy(m):
        return rc(sv.at[lax.div(peer(m), 4)], rv.at[m], sp_s.at[m], sp_r.at[m], d, peer(m))

    for m in range(1, NP):
        sp_copy(m).start()
    rs_copy(1, 3).start()
    rs_pair(1, 0)
    rs_pair(1, 1)
    for dest in (3, 0, 2, 1):
        gin_block(dest)
        dest_send(0, dest)
    rs_near(1, 0)
    rs_near(1, 1)
    zr_join(0)
    geb_row = jnp.sum(geb[...], axis=0, keepdims=True)
    for m in range(1, NP):
        sp_copy(m).wait_recv()
    tiles = sv[ybit]
    for m in range(1, NP):
        tiles = tiles + rv[m]
    for dd in range(NZ):
        ebt = jnp.broadcast_to(geb_row[:, 128 * dd : 128 * (dd + 1)], (8, 128))
        zt[dd] = jnp.where(rows8 == 3, ebt, tiles[dd])

    def sz_copy(i, incoming):
        return rc(zt.at[other(i)], rzv.at[i], sz_s.at[i], sz_r.at[i], other(i), s)

    for i in range(1, NZ):
        sz_copy(i, False).start()

    def total_rows(a, n):
        ref, use = zr_total(a)

        def step(c):
            at = aligned(32 * c, 32)
            block = ref.at[pl.ds(at, 32)]
            block[...] = zr_sum(a, use, block[...].astype(F32), at, 32).astype(BF16)
        loop(n // 32, step)

    def back_copy(which, m, incoming):
        src = (gin, gexp)[which].at[pl.ds(aligned(256 * d + 32 * peer(m), 32), 32)]
        dst = (rb_in, rb_exp)[which].at[m]
        return rc(src, dst, b_s.at[which, m], b_r.at[which, m], d, peer(m))

    total_rows(1, 256)
    for m in range(1, NP):
        back_copy(1, m, False).start()

    ref_r, use_r = zr_total(2)

    def red_total(c):
        at = aligned(32 * c, 32)
        tred_ref[pl.ds(at, 32), :] = zr_sum(2, use_r, ref_r[pl.ds(at, 32), :].astype(F32), at, 32)
    loop(4, red_total)
    rs_last(0)

    def out_final(c):
        at = aligned(32 * c, 32)
        hout_ref[pl.ds(at, 32), :] = (
            x_ref[pl.ds(at, 32), :].astype(F32) + rs_total32(0, c) + vecs[2:3, :]
        ).astype(BF16)

    def rs_total32(w, c):
        at = aligned(32 * c, 32)
        own = RS[w][0][pl.ds(aligned(rows * s + 32 * c, 32), 32), :].astype(F32)
        own = own + RS[w][1][3, pl.ds(at, 32), :].astype(F32)
        own = own + RS[w][3][0, pl.ds(at, 32), :].astype(F32)
        return own + RS[w][3][1, pl.ds(at, 32), :].astype(F32)

    loop(rows // 32, out_final)
    def grad_final(c):
        at = aligned(32 * c, 32)
        dn = rs_total32(1, c)
        unit, inv = unit_of(x_ref[pl.ds(at, 32), :])
        dyf = dyg[pl.ds(aligned(rows * s + 32 * c, 32), 32), :].astype(F32)
        g = dn * vecs[0:1, :]
        hg = inv * (
            g - jnp.mean(g, axis=1, keepdims=True) - unit * jnp.mean(g * unit, axis=1, keepdims=True)
        ) + dyf
        hgrad_ref[pl.ds(at, 32), :] = hg.astype(BF16)

    total_rows(0, 256)
    for m in range(1, NP):
        back_copy(0, m, False).start()
    rs_last(1)
    loop(rows // 32, grad_final)
    ref_o, use_o = zr_total(3)
    tout_ref[...] = zr_sum(3, use_o, ref_o[...].astype(F32), 0, 32)

    mine = pl.ds(aligned(256 * d + 32 * s, 32), 32)
    ra_exp[0] = gexp[mine, :]
    ra_in[0] = gin[mine, :]
    for m in range(1, NP):
        back_copy(1, m, True).wait_recv()
        ra_exp[m] = rb_exp[m]
    for m in range(1, NP):
        back_copy(0, m, True).wait_recv()
        ra_in[m] = rb_in[m]
    for i in range(1, NZ):
        sz_copy(i, True).wait_recv()
    tile = zt[d]
    for i in range(1, NZ):
        tile = tile + rzv[i]
    tile_ref[...] = jnp.where(rows8 == 3, tile, pltpu.roll(tile, lax.rem(128 - 32 * quad, 128), 1))

    for m in range(1, NP):
        a2a_msg(0, m).wait_send()
        a2a_msg(1, m).wait_send()
        vp_copy(m, False).wait_send()
        back_copy(0, m, False).wait_send()
        back_copy(1, m, False).wait_send()
        sp_copy(m).wait_send()
    for m in range(1, 4):
        wo_copy(m, False).wait_send()
        go_copy(m, False).wait_send()
    for i in range(1, NZ):
        vz_copy(i, False).wait_send()
        sz_copy(i, False).wait_send()
    for i in range(9):
        ag_copy(1, i, False).wait_send()
    for w in range(2):
        for i in range(10):
            rs_copy(w, i).wait_send()
    for a in range(4):
        z_sent(a)
        zr_sent(a)


def update_kernel(*refs):
    weights, moments = refs[0:8], refs[8:16]
    rate_ref, decay_ref, hout_in, hgrad_in, gin, gexp, gred, gout, tile = refs[16:25]
    hout, hgrad = refs[25:27]
    new_moments, new_weights = refs[27:35], refs[35:43]
    s = lax.axis_index("seq")
    keep = 1.0 - decay_ref[0]
    rate = rate_ref[0]

    def update(k, index, grad):
        moment = 0.5 * moments[k][index] + grad * (0.5 / NZ)
        new_moments[k][index] = moment
        new_weights[k][index] = keep * weights[k][index] - rate * moment

    hout[...] = hout_in[...]
    hgrad[...] = hgrad_in[...]
    gain = weights[0][...].astype(BF16).astype(F32)
    shift = weights[1][...].astype(BF16).astype(F32)
    shift_grad = tile[1:2, :32]
    update(0, ..., (tile[0:1, :32] - shift * shift_grad) / gain)
    update(1, ..., shift_grad)
    update(7, ..., tile[2:3, :32])
    update(5, ..., tile[3:4, :])
    update(6, ..., gred[...])
    update(3, ..., gout[...])
    core = lax.rem(s, 2)
    xbit = lax.rem(lax.div(s, 2), 2)
    ybit = lax.div(s, 4)
    for m in range(NP):
        t = s
        if m & 1:
            t = t + (1 - 2 * core)
        if m & 2:
            t = t + 2 * (1 - 2 * xbit)
        if m & 4:
            t = t + 4 * (1 - 2 * ybit)
        pair = 2 * lax.rem(t, 4) + lax.div(t, 4)
        for part in range(3):
            cols = pl.ds(aligned(128 * pair + 1024 * part, 128), 128)
            update(2, (slice(None), cols), gin[m, :, 128 * part : 128 * (part + 1)].astype(F32))
        for e in range(NZ):
            cols = pl.ds(aligned(128 * (8 * e + t), 128), 128)
            update(4, (slice(None), cols), gexp[m, :, 128 * e : 128 * (e + 1)].astype(F32))


def fused_shards(*args):
    (hidden_in, out_cotangent), weights, moments = args[:2], args[2:10], args[10:18]
    rows = hidden_in.shape[1]
    seq = rows * NP
    freq = 10000.0 ** (-2.0 * np.arange(ROT // 2) / ROT)
    lane_freq = np.tile(freq, 128 // (ROT // 2))[None, :]
    near = np.arange(rows)[:, None] * lane_freq
    far = (rows * np.arange(NP))[:, None] * lane_freq
    tables = [jnp.asarray(f(a), F32) for a in (near, far) for f in (np.cos, np.sin)]

    def flat(v):
        return v.reshape(1, -1) if v.ndim == 1 else v

    shards_in = [flat(w) for w in weights]
    ff = weights[6].shape[0] * NZ
    moments_in = [flat(m) for m in moments]
    shard_shapes = [jax.ShapeDtypeStruct(w.shape, F32) for w in shards_in]
    vm = pltpu.VMEM
    dma = pltpu.SemaphoreType.DMA
    scratch = [
        vm((seq, D), BF16), vm((seq, D), BF16), vm((seq, D), BF16),
        vm((D, 384), BF16), vm((D, ff), BF16), vm((ff, D), BF16), vm((128, D), BF16), vm((NZ, 32, D), BF16),
        vm((NP, 32, 384), BF16), vm((NP, 32, ff), BF16),
        vm((seq, 128), BF16), vm((seq, 128), BF16),
        vm((128, seq), F32), vm((128, seq), F32), vm((seq, 384), BF16),
        vm((2, NP // 2, 2 * rows, 2 * rows), F32), vm((seq, 128), F32),
        vm((2, 2 * rows, 128), F32), vm((2, 2 * rows, 256), F32),
        vm((seq, ff), BF16), vm((seq, ff), BF16), vm((seq, D), BF16),
        vm((4, rows, D), BF16), vm((4, rows, D), BF16),
        vm((2, rows // 2, D), BF16), vm((2, rows, D), BF16), vm((2, rows // 2, D), BF16), vm((2, rows, D), BF16),
        vm((D, 384), BF16), vm((D, ff), BF16), vm((ff, D), BF16), vm((128, D), BF16), vm((NZ, 32, D), BF16),
        vm((NZ, 256, 384), BF16), vm((NZ, 256, ff), BF16), vm((NZ, 128, D), BF16), vm((NZ, 32, D), BF16),
        vm((NP, 32, 384), BF16), vm((NP, 32, ff), BF16),
        vm((NP, NZ, 8, 128), F32), vm((8, D), F32), vm((8, ff), F32), vm((8, ff), F32), vm((8, D), F32),
        vm((2, NZ, 8, 128), F32), vm((NP, NZ, 8, 128), F32), vm((NZ, 8, 128), F32), vm((NZ, 8, 128), F32),
        dma((2, NP)), dma((2, NP)), dma((2, 9)), dma((2, 9)), dma((4, 5)), dma((4, 4)),
        dma((NZ,)), dma((NZ,)), dma((NP,)), dma((NP,)), dma((4,)), dma((4,)),
        dma((2, 10)), dma((2, 10)), dma((4, 4)), dma((4, 4)), dma((4,)), dma((4,)),
        dma((2, NP)), dma((2, NP)), dma((NP,)), dma((NP,)), dma((NZ,)), dma((NZ,)), dma,
    ]
    in_vmem = pl.BlockSpec(memory_space=pltpu.VMEM)
    in_smem = pl.BlockSpec(memory_space=pltpu.SMEM)

    def body(*refs):
        block_kernel(rows, *refs)

    rows_shape = jax.ShapeDtypeStruct((rows, D), BF16)
    grads = pl.pallas_call(
        body,
        out_shape=[
            rows_shape, rows_shape,
            jax.ShapeDtypeStruct((NP, 32, 384), BF16), jax.ShapeDtypeStruct((NP, 32, ff), BF16),
            jax.ShapeDtypeStruct((128, D), F32), jax.ShapeDtypeStruct((32, D), F32),
            jax.ShapeDtypeStruct((8, 128), F32),
        ],
        in_specs=[in_vmem, pl.BlockSpec(memory_space=pl.ANY)] + [in_vmem] * 12,
        out_specs=[in_vmem] * 7,
        scratch_shapes=scratch,
        compiler_params=pltpu.CompilerParams(
            collective_id=0, has_side_effects=True, vmem_limit_bytes=63 * 2**20
        ),
        name="block_step",
    )(
        hidden_in.reshape(rows, D), out_cotangent.reshape(rows, D), *shards_in, *tables,
    )
    outs = pl.pallas_call(
        update_kernel,
        out_shape=[rows_shape, rows_shape] + shard_shapes + shard_shapes,
        in_specs=[in_vmem] * 16 + [in_smem] * 2 + [in_vmem] * 7,
        out_specs=[in_vmem] * 18,
        compiler_params=pltpu.CompilerParams(vmem_limit_bytes=63 * 2**20),
        name="block_update",
    )(*shards_in, *moments_in, args[18], args[19], *grads)
    small = [w.shape for w in weights]
    return (
        outs[0].reshape(hidden_in.shape),
        outs[1].reshape(hidden_in.shape),
        *[o.reshape(sh) for o, sh in zip(outs[2:], small + small)],
    )


def fits(mesh):
    return mesh.shape["dp"] == NZ and mesh.shape["seq"] == NP


def solution(mesh):
    placed = (
        P("dp", "seq", None),
        P("dp", "seq", None),
        P(("dp", "seq")),
        P(("dp", "seq")),
        P(("dp", "seq"), None),
        P(("dp", "seq"), None),
        P(("dp", "seq"), None),
        P(("dp", "seq")),
        P(("dp", "seq"), None),
        P(("dp", "seq")),
        P(("dp", "seq")),
        P(("dp", "seq")),
        P(("dp", "seq"), None),
        P(("dp", "seq"), None),
        P(("dp", "seq"), None),
        P(("dp", "seq")),
        P(("dp", "seq"), None),
        P(("dp", "seq")),
        P(),
        P(),
    )
    return jax.shard_map(
        fused_shards if fits(mesh) else shards,
        mesh=mesh,
        in_specs=placed,
        out_specs=(
            P("dp", "seq", None),
            P("dp", "seq", None),
            P(("dp", "seq")),
            P(("dp", "seq")),
            P(("dp", "seq"), None),
            P(("dp", "seq"), None),
            P(("dp", "seq"), None),
            P(("dp", "seq")),
            P(("dp", "seq"), None),
            P(("dp", "seq")),
            P(("dp", "seq")),
            P(("dp", "seq")),
            P(("dp", "seq"), None),
            P(("dp", "seq"), None),
            P(("dp", "seq"), None),
            P(("dp", "seq")),
            P(("dp", "seq"), None),
            P(("dp", "seq")),
        ),
        check_vma=False,
    )
```

```python
import jax
import jax.numpy as jnp
import numpy as np
from jax import lax
from jax.experimental import pallas as pl
from jax.experimental.pallas import tpu as pltpu
from jax.sharding import PartitionSpec as P

D = 1024
H = 16
HD = 64
ROT = 32


epsilon = 1e-05
masked_score = -1e30


def rotary(block, positions, direction):
    half_rot = ROT // 2
    frequency = 10000.0 ** (-2.0 * jnp.arange(half_rot, dtype=jnp.float32) / ROT)
    angles = direction * positions[:, None] * frequency[None, :]
    cosine = jnp.cos(angles)[:, None, :]
    sine_part = jnp.sin(angles)[:, None, :]
    first_half = block[..., :half_rot]
    second = block[..., half_rot:ROT]
    return jnp.concatenate(
        [
            first_half * cosine - second * sine_part,
            second * cosine + first_half * sine_part,
            block[..., ROT:],
        ],
        axis=-1,
    )


def gelu_tanh(values):
    return jax.nn.gelu(values, approximate=True)


def gelu_back(expanded, upstream):
    unused_out, pullback = jax.vjp(gelu_tanh, expanded)
    return pullback(upstream)[0]


def heads_of(rows):
    return rows.reshape(rows.shape[0], H, HD)


def scores_of(query_rows, key_rows):
    score_scale = HD ** (-0.5)
    return (
        jnp.einsum(
            "qhd,khd->hqk",
            heads_of(query_rows),
            heads_of(key_rows),
            preferred_element_type=jnp.float32,
        )
        * score_scale
    )


def shards(
    hidden_in,
    out_cotangent,
    norm_gain,
    norm_shift,
    attend_in,
    attend_out,
    expand_weight,
    expand_bias,
    reduce_weight,
    reduce_bias,
    gain_moment,
    shift_moment,
    inward_moment,
    outward_moment,
    expand_moment,
    expbias_moment,
    reduce_moment,
    redbias_moment,
    learn_rate,
    decay_rate,
):
    score_scale = HD ** (-0.5)
    gain_low, shift_low, inward_mat, outward_mat, expand_mat, expand_vec, reduce_mat, reduce_vec = (
        lax.all_gather(norm_gain.astype(jnp.bfloat16), ("dp", "seq"), axis=0, tiled=True),
        lax.all_gather(norm_shift.astype(jnp.bfloat16), ("dp", "seq"), axis=0, tiled=True),
        lax.all_gather(attend_in.astype(jnp.bfloat16), ("dp", "seq"), axis=0, tiled=True),
        lax.all_gather(attend_out.astype(jnp.bfloat16), ("dp", "seq"), axis=0, tiled=True),
        lax.all_gather(expand_weight.astype(jnp.bfloat16), ("dp", "seq"), axis=0, tiled=True),
        lax.all_gather(expand_bias.astype(jnp.bfloat16), ("dp", "seq"), axis=0, tiled=True),
        lax.all_gather(reduce_weight.astype(jnp.bfloat16), ("dp", "seq"), axis=0, tiled=True),
        lax.all_gather(reduce_bias.astype(jnp.bfloat16), ("dp", "seq"), axis=0, tiled=True),
    )
    seq_count, block_len, model_width = hidden_in.shape
    row_count = seq_count * block_len
    full_len = block_len * lax.axis_size("seq")
    seq_start = lax.axis_index("seq") * block_len
    query_index = seq_start + jnp.arange(block_len, dtype=jnp.int32)
    key_index = jnp.arange(full_len, dtype=jnp.int32)
    causal = key_index[None, :] <= query_index[:, None]
    positions = query_index.astype(jnp.float32)
    inputs = hidden_in.astype(jnp.float32).reshape(row_count, model_width)
    row_mean = jnp.mean(inputs, axis=-1, keepdims=True)
    centred = inputs - row_mean
    row_var = jnp.mean(centred * centred, axis=-1, keepdims=True)
    inverse = lax.rsqrt(row_var + epsilon)
    unit_rows = centred * inverse
    gain_full = gain_low.astype(jnp.float32)
    normed = (unit_rows * gain_full + shift_low.astype(jnp.float32)).astype(jnp.bfloat16)
    joined = jnp.dot(normed, inward_mat, preferred_element_type=jnp.float32).reshape(
        seq_count, block_len, 3 * D
    )
    query = (
        rotary(joined[..., :D].reshape(seq_count, block_len, H, HD), positions, 1.0)
        .astype(jnp.bfloat16)
        .reshape(seq_count, block_len, D)
    )
    keyed = (
        rotary(joined[..., D : 2 * D].reshape(seq_count, block_len, H, HD), positions, 1.0)
        .astype(jnp.bfloat16)
        .reshape(seq_count, block_len, D)
    )
    valued = joined[..., 2 * D :].astype(jnp.bfloat16)
    key_all, value_all = (
        lax.all_gather(keyed, "seq", axis=1, tiled=True),
        lax.all_gather(valued, "seq", axis=1, tiled=True),
    )

    def attend(operands):
        query_seq, key_seq, value_seq = operands
        scores = jnp.where(causal[None], scores_of(query_seq, key_seq), masked_score)
        row_max = jnp.max(scores, axis=-1, keepdims=True)
        log_total = row_max + jnp.log(jnp.sum(jnp.exp(scores - row_max), axis=-1, keepdims=True))
        weights = jnp.exp(scores - log_total).astype(jnp.bfloat16)
        mixed = jnp.einsum(
            "hqk,khd->qhd", weights, heads_of(value_seq), preferred_element_type=jnp.float32
        )
        return (mixed.reshape(-1, D).astype(jnp.bfloat16), jnp.transpose(log_total[..., 0]))

    attended, log_totals = lax.map(attend, (query, key_all, value_all))
    expanded = jnp.dot(normed, expand_mat, preferred_element_type=jnp.float32) + expand_vec.astype(
        jnp.float32
    )
    activated = gelu_tanh(expanded).astype(jnp.bfloat16)
    flat_attn = attended.reshape(row_count, D)
    result = (
        inputs
        + jnp.dot(flat_attn, outward_mat, preferred_element_type=jnp.float32)
        + jnp.dot(activated, reduce_mat, preferred_element_type=jnp.float32)
        + reduce_vec.astype(jnp.float32)
    )
    hidden_out = result.astype(jnp.bfloat16).reshape(seq_count, block_len, D)
    upstream = out_cotangent.reshape(row_count, D)
    grad_outward = jnp.einsum("rd,re->de", flat_attn, upstream, preferred_element_type=jnp.float32)
    grad_reduce = jnp.einsum("rf,re->fe", activated, upstream, preferred_element_type=jnp.float32)
    grad_redbias = jnp.sum(upstream.astype(jnp.float32), axis=0)
    attn_back = (
        jnp.einsum("re,de->rd", upstream, outward_mat, preferred_element_type=jnp.float32)
        .astype(jnp.bfloat16)
        .reshape(seq_count, block_len, D)
    )
    act_back = jnp.einsum("re,fe->rf", upstream, reduce_mat, preferred_element_type=jnp.float32)
    expand_back = gelu_back(expanded, act_back).astype(jnp.bfloat16)
    grad_expbias = jnp.sum(expand_back.astype(jnp.float32), axis=0)
    grad_expand = jnp.einsum("rd,rf->df", normed, expand_back, preferred_element_type=jnp.float32)
    norm_back = jnp.einsum("rf,df->rd", expand_back, expand_mat, preferred_element_type=jnp.float32)

    def query_side(query_seq, key_seq, value_seq, back_seq, total_seq):
        scores = jnp.where(causal[None], scores_of(query_seq, key_seq), masked_score)
        probs = jnp.exp(scores - jnp.transpose(total_seq)[:, :, None])
        prob_grad = jnp.einsum(
            "qhd,khd->hqk",
            heads_of(back_seq),
            heads_of(value_seq),
            preferred_element_type=jnp.float32,
        )
        row_delta = jnp.sum(probs * prob_grad, axis=-1, keepdims=True)
        score_grad = (probs * (prob_grad - row_delta)).astype(jnp.bfloat16)
        query_grad = (
            jnp.einsum(
                "hqk,khd->qhd", score_grad, heads_of(key_seq), preferred_element_type=jnp.float32
            )
            * score_scale
        )
        return (probs, score_grad, query_grad, row_delta)

    def attend_back(operands):
        query_seq, key_seq, value_seq, back_seq, total_seq = operands
        probs, score_grad, query_grad, row_delta = query_side(
            query_seq, key_seq, value_seq, back_seq, total_seq
        )
        key_grad = (
            jnp.einsum(
                "hqk,qhd->khd", score_grad, heads_of(query_seq), preferred_element_type=jnp.float32
            )
            * score_scale
        )
        value_grad = jnp.einsum(
            "hqk,qhd->khd",
            probs.astype(jnp.bfloat16),
            heads_of(back_seq),
            preferred_element_type=jnp.float32,
        )
        return (query_grad, key_grad.reshape(-1, D), value_grad.reshape(-1, D))

    query_grads, key_terms, value_terms = lax.map(
        attend_back, (query, key_all, value_all, attn_back, log_totals)
    )
    key_grads, value_grads = (
        lax.psum_scatter(key_terms, "seq", scatter_dimension=1, tiled=True),
        lax.psum_scatter(value_terms, "seq", scatter_dimension=1, tiled=True),
    )
    query_turned = rotary(query_grads, positions, -1.0).reshape(seq_count, block_len, D)
    key_turned = rotary(key_grads.reshape(seq_count, block_len, H, HD), positions, -1.0).reshape(
        seq_count, block_len, D
    )
    joined_back = (
        jnp.concatenate([query_turned, key_turned, value_grads], axis=-1)
        .astype(jnp.bfloat16)
        .reshape(row_count, 3 * D)
    )
    grad_inward = jnp.einsum("rd,re->de", normed, joined_back, preferred_element_type=jnp.float32)
    norm_back = norm_back + jnp.einsum(
        "re,de->rd", joined_back, inward_mat, preferred_element_type=jnp.float32
    )
    grad_gain = jnp.sum(norm_back * unit_rows, axis=0)
    grad_shift = jnp.sum(norm_back, axis=0)
    unit_back = norm_back * gain_full
    input_back = inverse * (
        unit_back
        - jnp.mean(unit_back, axis=-1, keepdims=True)
        - unit_rows * jnp.mean(unit_back * unit_rows, axis=-1, keepdims=True)
    ) + upstream.astype(jnp.float32)
    hidden_grad = input_back.astype(jnp.bfloat16).reshape(seq_count, block_len, D)
    totals = (
        lax.psum_scatter(grad_gain, ("dp", "seq"), scatter_dimension=0, tiled=True),
        lax.psum_scatter(grad_shift, ("dp", "seq"), scatter_dimension=0, tiled=True),
        lax.psum_scatter(grad_inward, ("dp", "seq"), scatter_dimension=0, tiled=True),
        lax.psum_scatter(grad_outward, ("dp", "seq"), scatter_dimension=0, tiled=True),
        lax.psum_scatter(grad_expand, ("dp", "seq"), scatter_dimension=0, tiled=True),
        lax.psum_scatter(grad_expbias, ("dp", "seq"), scatter_dimension=0, tiled=True),
        lax.psum_scatter(grad_reduce, ("dp", "seq"), scatter_dimension=0, tiled=True),
        lax.psum_scatter(grad_redbias, ("dp", "seq"), scatter_dimension=0, tiled=True),
    )
    seq_total = seq_count * lax.axis_size("dp")
    step_rate = learn_rate[0]
    decay_now = decay_rate[0]
    params = (
        norm_gain,
        norm_shift,
        attend_in,
        attend_out,
        expand_weight,
        expand_bias,
        reduce_weight,
        reduce_bias,
    )
    moments = (
        gain_moment,
        shift_moment,
        inward_moment,
        outward_moment,
        expand_moment,
        expbias_moment,
        reduce_moment,
        redbias_moment,
    )
    momenta = [
        0.5 * moment + 0.5 * (summed_grad / seq_total)
        for moment, summed_grad in zip(moments, totals)
    ]
    updated = [
        (1.0 - decay_now) * weight_now - step_rate * momentum
        for weight_now, momentum in zip(params, momenta)
    ]
    return (
        hidden_out,
        hidden_grad,
        momenta[0],
        momenta[1],
        momenta[2],
        momenta[3],
        momenta[4],
        momenta[5],
        momenta[6],
        momenta[7],
        updated[0],
        updated[1],
        updated[2],
        updated[3],
        updated[4],
        updated[5],
        updated[6],
        updated[7],
    )


F32 = jnp.float32
BF16 = jnp.bfloat16
MESH = pl.DeviceIdType.MESH
NZ = 4
NP = 8
NT = (((1,), (1,)), ((), ()))
TN = (((0,), (0,)), ((), ()))


def dot(a, b):
    return jnp.dot(a, b, preferred_element_type=F32)


def dot_nt(a, b):
    return lax.dot_general(a, b, NT, preferred_element_type=F32)


def dot_tn(a, b):
    return lax.dot_general(a, b, TN, preferred_element_type=F32)


def aligned(value, unit):
    return pl.multiple_of(value, unit)


def gelu_pair(e):
    square = e * e
    t = jnp.tanh(e * (GELU_C + (GELU_C * GELU_A) * square))
    half = 0.5 + 0.5 * t
    slope = half + (0.5 * e) * (1.0 - t * t) * (GELU_C + (3.0 * GELU_C * GELU_A) * square)
    return e * half, slope


GELU_C = 0.7978845608028654
GELU_A = 0.044715


def block_kernel(rows, *refs):
    (
        x_ref, dy_ref, gain_ref, shift_ref, win_ref, wout_ref, wexp_ref, ebias_ref, wred_ref, rbias_ref,
        cosr_ref, sinr_ref, cosb_ref, sinb_ref,
        hout_out, hgrad_out, in_out, exp_out, tred_out, tout_out, tile_ref,
        xg, dyg, xn, win, wexp, wred, wout, wz, pin, pexp,
        o_s, do_s, dkt, dvt, dfused, sbuf, lse, mref, acc,
        act_s, de_s, pdn, sib_o, sib_d, r1_o, r2_o, r1_d, r2_d,
        gin, gexp, gred, gout, gz, rz_in, rz_exp, rz_red, rz_out, rb_in, rb_exp,
        vt, vecs, ebs, geb, sums, sv, rv, zt, rzv,
        a2a_s, a2a_r, ag_s, ag_r, z_s, z_r, vz_s, vz_r, vp_s, vp_r, wo_s, wo_r,
        rs_s, rs_r, zr_s, zr_r, go_s, go_r, b_s, b_r, sp_s, sp_r, sz_s, sz_r, dy_sem,
        hout_ref, hgrad_ref, tred_ref, tout_ref, out_sem,
    ) = refs
    pout = xg
    d = lax.axis_index("dp")
    s = lax.axis_index("seq")
    core = lax.rem(s, 2)
    xbit = lax.rem(lax.div(s, 2), 2)
    ybit = lax.div(s, 4)
    chip = lax.div(s, 2)
    quad = lax.rem(s, 4)

    def peer(m):
        out = s
        if m & 1:
            out = out + (1 - 2 * core)
        if m & 2:
            out = out + 2 * (1 - 2 * xbit)
        if m & 4:
            out = out + 4 * (1 - 2 * ybit)
        return out

    def pair_of(t):
        return 2 * lax.rem(t, 4) + lax.div(t, 4)

    def rc(src, dst, ssem, rsem, dd, ss):
        return pltpu.make_async_remote_copy(
            src_ref=src, dst_ref=dst, send_sem=ssem, recv_sem=rsem,
            device_id=(dd, ss), device_id_type=MESH,
        )

    barrier = pltpu.get_barrier_semaphore()
    for m in range(1, NP):
        pl.semaphore_signal(barrier, inc=1, device_id=(d, peer(m)), device_id_type=MESH)
    for dz in range(1, NZ):
        pl.semaphore_signal(barrier, inc=1, device_id=(lax.rem(d + dz, NZ), s), device_id_type=MESH)

    zrow = jnp.zeros((1, 96), F32)
    small = jnp.concatenate(
        [
            jnp.concatenate([r[...].astype(BF16).astype(F32), zrow], axis=1)
            for r in (gain_ref, shift_ref, rbias_ref)
        ]
        + [jnp.zeros((5, 128), F32)],
        axis=0,
    )
    small = pltpu.roll(small, 32 * quad, 1)
    rows8 = lax.broadcasted_iota(jnp.int32, (8, 128), 0)
    ebias_row = jnp.broadcast_to(ebias_ref[...].astype(BF16).astype(F32), (8, 128))
    vt[s, d] = jnp.where(rows8 == 3, ebias_row, small)
    wz[d] = wout_ref[...].astype(BF16)
    own_dy = pltpu.make_async_copy(dy_ref, dyg.at[pl.ds(aligned(rows * s, rows), rows)], dy_sem)
    own_dy.start()
    xg[pl.ds(aligned(rows * s, rows), rows), :] = x_ref[...]
    own_rows = aligned(32 * (8 * d + s), 32)

    def pack_in():
        for m in range(NP):
            j = pair_of(peer(m))
            for part in range(3):
                piece = win_ref[:, pl.ds(aligned(128 * j + 1024 * part, 128), 128)].astype(BF16)
                if m == 0:
                    win[pl.ds(own_rows, 32), 128 * part : 128 * (part + 1)] = piece
                else:
                    pin[m, :, 128 * part : 128 * (part + 1)] = piece

    def pack_exp():
        for m in range(NP):
            t = peer(m)
            for e in range(NZ):
                piece = wexp_ref[:, pl.ds(aligned(128 * (8 * e + t), 128), 128)].astype(BF16)
                if m == 0:
                    wexp[pl.ds(own_rows, 32), 128 * e : 128 * (e + 1)] = piece
                else:
                    pexp[m, :, 128 * e : 128 * (e + 1)] = piece

    pack_in()
    pl.semaphore_wait(barrier, NP - 1 + NZ - 1)

    def bundle(ref, ssem, rsem):
        return rc(ref, ref, ssem, rsem, d, peer(1))

    def a2a_msg(which, m):
        src = (pin, pexp)[which].at[m]
        dst = (win, wexp)[which].at[pl.ds(own_rows, 32)]
        return rc(src, dst, a2a_s.at[which], a2a_r.at[which], d, peer(m))

    def a2a_group(which):
        return bundle((pin, pexp)[which].at[pl.ds(1, NP - 1)], a2a_s.at[which], a2a_r.at[which])

    half = rows // 2
    AG = (
        (1, 0, 0, rows), (2, 0, 0, rows), (4, 0, 0, rows),
        (1, 2, 0, rows), (1, 4, 0, rows), (4, 2, half, half), (2, 4, 0, half),
        (1, 6, 0, half), (1, 6, half, half),
    )

    def ag_copy(which, i, incoming):
        to, blk, lo, n = AG[i]
        buf = (xg, dyg)[which]
        at = rows * peer(blk ^ (to if incoming else 0)) + lo
        ref = buf.at[pl.ds(aligned(at, half), n)]
        return rc(ref, ref, ag_s.at[which], ag_r.at[which, i], d, peer(to))

    def ag_sent(which):
        bundle((xg, dyg)[which].at[pl.ds(0, 7 * rows)], ag_s.at[which], ag_r.at[which, 0]).wait_send()

    def ag_start(which, i):
        ag_copy(which, i, False).start()

    def ag_arrived(which, i):
        ag_copy(which, i, True).wait_recv()

    ZVIEW = (
        lambda b: win.at[pl.ds(aligned(256 * b, 256), 256)],
        lambda b: wexp.at[pl.ds(aligned(256 * b, 256), 256)],
        lambda b: wred.at[pl.ds(aligned(128 * b, 128), 128)],
        lambda b: wz.at[b],
    )

    def z_direct(dest):
        ok = d != dest
        if dest == NZ - 1:
            ok = ok & (d != 0)
        if dest == 0:
            ok = ok & (d != NZ - 1)
        return ok

    def z_send(a):
        for dest in (3, 0, 2, 1):
            @pl.when(z_direct(dest))
            def _():
                rc(ZVIEW[a](d), ZVIEW[a](d), z_s.at[a], z_r.at[a, d], dest, s).start()

    FWD = ((2, 0, 3), (1, 3, 0))

    def z_wait_block(a, b):
        rc(ZVIEW[a](b), ZVIEW[a](b), z_s.at[a], z_r.at[a, b], d, s).wait_recv()

    def z_forward(a):
        for at, blk, dest in FWD:
            @pl.when(d == at)
            def _():
                z_wait_block(a, blk)
                rc(ZVIEW[a](blk), ZVIEW[a](blk), z_s.at[a], z_r.at[a, blk], dest, s).start()

    PACE = ((0, 1), (3, 2))

    def z_pace(a):
        for at, blk in PACE:
            @pl.when(d == at)
            def _():
                z_wait_block(a, blk)

    def z_arrived(a, paced=False):
        for b in range(NZ):
            need = d != b
            for at, blk, dest in FWD:
                if blk == b:
                    need = need & (d != at)
            for at, blk in PACE:
                if paced and blk == b:
                    need = need & (d != at)

            @pl.when(need)
            def _():
                z_wait_block(a, b)

    def z_sent(a):
        whole = (win, wexp, wred, wz)[a]
        inner = (d == 1) | (d == 2)

        @pl.when(inner)
        def _():
            bundle(whole, z_s.at[a], z_r.at[a, 0]).wait_send()

        @pl.when(jnp.logical_not(inner))
        def _():
            bundle(whole.at[pl.ds(0, whole.shape[0] // 2)], z_s.at[a], z_r.at[a, 0]).wait_send()

    def other(i):
        return lax.rem(d + i, NZ)

    def vz_copy(i, incoming):
        b = lax.rem(d + NZ - i, NZ) if incoming else d
        return rc(vt.at[s, b], vt.at[s, b], vz_s.at[0], vz_r.at[0], other(i), s)

    def vp_copy(m, incoming):
        b = peer(m) if incoming else s
        return rc(vt.at[b], vt.at[b], vp_s.at[0], vp_r.at[0], d, peer(m))

    for i in range(1, NZ):
        vz_copy(i, False).start()
    for m in range(1, NP):
        a2a_msg(0, m).start()
    z_send(3)
    for i in (1, 2, 0):
        ag_start(0, i)
    pack_exp()
    wred[pl.ds(aligned(128 * d, 128), 128), :] = wred_ref[...].astype(BF16)
    vz_group = bundle(zt.at[pl.ds(1, NZ - 1)], vz_s.at[0], vz_r.at[0])
    vz_group.wait_recv()
    for m in range(1, NP):
        vp_copy(m, False).start()
    a2a_group(0).wait_recv()
    z_send(0)
    for m in range(1, NP):
        a2a_msg(1, m).start()
    z_forward(3)
    z_pace(0)
    z_forward(0)
    z_send(2)
    ag_arrived(0, 1)
    ag_start(0, 5)
    ag_start(0, 3)
    ag_arrived(0, 2)
    ag_start(0, 6)
    ag_start(0, 4)
    a2a_group(1).wait_recv()
    z_send(1)

    def wo_copy(m, incoming):
        src = wz.at[lax.rem(peer(m), 4)]
        r = lax.rem(peer(m), 4) if incoming else quad
        dst = wout.at[pl.ds(aligned(32 * r, 32), 32)]
        return rc(src, dst, wo_s.at[0], wo_r.at[0], d, peer(m))

    vp_group = bundle(rv.at[pl.ds(1, NP - 1)], vp_s.at[0], vp_r.at[0])
    vp_group.wait_recv()
    for dd in range(NZ):
        for yy in range(2):
            group = 2 * dd + yy
            total = vt[4 * yy, dd]
            for jj in range(1, 4):
                total = total + vt[4 * yy + jj, dd]
            vecs[:, 128 * group : 128 * (group + 1)] = total

    def unit_of(xb):
        xf = xb.astype(F32)
        mu = jnp.mean(xf, axis=1, keepdims=True)
        cen = xf - mu
        var = jnp.mean(cen * cen, axis=1, keepdims=True)
        inv = lax.rsqrt(var + epsilon)
        return cen * inv, inv

    def norm_block(b):
        def step(c, carry):
            at = aligned(rows * b + 64 * c, 64)
            unit, _ = unit_of(xg[pl.ds(at, 64), :])
            xn[pl.ds(at, 64), :] = (unit * vecs[0:1, :] + vecs[1:2, :]).astype(BF16)
            return carry
        lax.fori_loop(0, rows // 64, step, 0)

    lane_b = lax.broadcasted_iota(jnp.int32, (rows, 128), 1)
    low_head = lane_b < HD
    in_head = lax.rem(lane_b, HD)
    first_rot = in_head < ROT // 2
    second_rot = (in_head >= ROT // 2) & (in_head < ROT)

    def angles(b):
        cb, sb = cosb_ref[pl.ds(b, 1), :], sinb_ref[pl.ds(b, 1), :]
        cr, sr = cosr_ref[...], sinr_ref[...]
        co = jnp.where(in_head < ROT, cr * cb - sr * sb, 1.0)
        si = sr * cb + cr * sb
        return co, jnp.where(first_rot, -si, 0.0), jnp.where(second_rot, si, 0.0)

    def turn(block, table, back=False):
        co, up, down = table
        moved = pltpu.roll(block, 128 - ROT // 2, 1) * up + pltpu.roll(block, ROT // 2, 1) * down
        return block * co - moved if back else block * co + moved

    norm_block(s)
    ag_arrived(0, 0)
    norm_block(peer(1))
    own_dy.wait()
    for i in (1, 2, 0):
        ag_start(1, i)
    norm_block(peer(2))
    norm_block(peer(4))
    ag_arrived(0, 3)
    norm_block(peer(3))
    ag_arrived(0, 4)
    norm_block(peer(5))
    ag_arrived(0, 6)
    ag_start(0, 7)
    ag_arrived(0, 5)
    ag_start(0, 8)
    norm_block(peer(6))
    ag_arrived(0, 7)
    ag_arrived(0, 8)
    norm_block(peer(7))
    z_arrived(3)
    for m in range(1, 4):
        wo_copy(m, False).start()
    wout[pl.ds(aligned(32 * quad, 32), 32), :] = wz[quad]
    z_arrived(0, paced=True)

    def qkv_step(n, carry):
        joined = dot(xn[pl.ds(aligned(2 * rows * n, 2 * rows), 2 * rows), :], win[...])
        for part in range(2):
            b = 2 * n + part
            at = pl.ds(aligned(rows * b, rows), rows)
            piece = joined[rows * part : rows * (part + 1)]
            table = angles(b)
            dfused[at, :128] = (turn(piece[:, :128], table) * HD**-0.5).astype(BF16)
            dfused[at, 128:256] = turn(piece[:, 128:256], table).astype(BF16)
            dfused[at, 256:] = piece[:, 256:].astype(BF16)
        return carry

    lax.fori_loop(0, NP // 2, qkv_step, 0)
    QB = 2 * rows
    lane_q = lax.broadcasted_iota(jnp.int32, (QB, 128), 1) < HD

    def wide(tile):
        return jnp.concatenate([tile] * (QB // 128), axis=1)

    def fold(v):
        out = v[:, :128]
        for c in range(1, QB // 128):
            out = jnp.maximum(out, v[:, 128 * c : 128 * (c + 1)])
        return out

    def by_head(block):
        zero = jnp.zeros_like(block)
        return jnp.where(lane_q, block, zero), jnp.where(lane_q, zero, block)

    def hidden():
        return lax.broadcasted_iota(jnp.int32, (QB, QB), 1) > lax.broadcasted_iota(jnp.int32, (QB, QB), 0)

    ones = jnp.ones((QB, 128), BF16)

    def attend_step(i, carry):
        at = aligned(QB * i, QB)
        qh = by_head(dfused[pl.ds(at, QB), :128])
        kj = dfused[pl.ds(at, QB), 128:256]
        mask = hidden()
        for h in range(2):
            sc = jnp.where(mask, masked_score, dot_nt(qh[h], kj))
            sbuf[h, i] = sc
            mref[h] = fold(sc)

        def scores(j, c2):
            kk = dfused[pl.ds(aligned(QB * j, QB), QB), 128:256]
            for h in range(2):
                sc = dot_nt(qh[h], kk)
                sbuf[h, j] = sc
                mref[h] = jnp.maximum(mref[h], fold(sc))
            return c2

        lax.fori_loop(0, i, scores, 0)
        for h in range(2):
            mref[h] = jnp.broadcast_to(jnp.max(mref[h], axis=1, keepdims=True), (QB, 128))
            acc[h] = jnp.zeros((QB, 256), F32)

        def weigh(j, c2):
            vj = jnp.concatenate([dfused[pl.ds(aligned(QB * j, QB), QB), 256:], ones], axis=1)
            for h in range(2):
                pj = jnp.exp(sbuf[h, j] - wide(mref[h])).astype(BF16)
                acc[h] = acc[h] + dot(pj, vj)
            return c2

        lax.fori_loop(0, i + 1, weigh, 0)
        o_s[pl.ds(at, QB), :] = jnp.where(
            lane_q, acc[0][:, :128] / acc[0][:, 128:], acc[1][:, :128] / acc[1][:, 128:]
        ).astype(BF16)
        lse[pl.ds(at, QB), :] = jnp.where(
            lane_q, mref[0] + jnp.log(acc[0][:, 128:]), mref[1] + jnp.log(acc[1][:, 128:])
        )

        @pl.when(i == 1)
        def _():
            z_forward(2)

        @pl.when(i == 1)
        def _():
            ag_arrived(1, 1)
            ag_start(1, 5)
            ag_start(1, 3)
            ag_arrived(1, 2)
            ag_start(1, 6)
            ag_start(1, 4)
        return carry

    lax.fori_loop(0, NP // 2, attend_step, 0)
    z_forward(1)
    ag_arrived(1, 6)
    ag_start(1, 7)
    ag_arrived(1, 5)
    ag_start(1, 8)

    dkt[...] = jnp.zeros_like(dkt)
    dvt[...] = jnp.zeros_like(dvt)

    def attend_back(i):
        at = aligned(QB * i, QB)
        qi = dfused[pl.ds(at, QB), :128]
        doi = do_s[pl.ds(at, QB), :]
        dof = doi.astype(F32)
        qh = by_head(qi)
        doh = by_head(doi)
        qt = jnp.transpose(qi.astype(F32)).astype(BF16)
        dot_t = jnp.transpose(dof).astype(BF16)
        parts = by_head(dof * o_s[pl.ds(at, QB), :].astype(F32))
        for h in range(2):
            mref[h] = jnp.broadcast_to(jnp.sum(parts[h], axis=1, keepdims=True), (QB, 128))
            acc[h, :, :128] = jnp.broadcast_to(lse[pl.ds(at, QB), HD * h : HD * h + 1], (QB, 128))
            acc[h, :, 128:] = jnp.zeros((QB, 128), F32)

        def unit(j, mask):
            ja = aligned(QB * j, QB)
            kk = dfused[pl.ds(ja, QB), 128:256]
            vj = dfused[pl.ds(ja, QB), 256:]
            for h in range(2):
                hs = slice(HD * h, HD * (h + 1))
                p = jnp.exp(dot_nt(qh[h], kk) - wide(acc[h, :, :128]))
                if mask is not None:
                    p = jnp.where(mask, 0.0, p)
                ds = (p * (dot_nt(doh[h], vj) - wide(mref[h]))).astype(BF16)
                acc[h, :, 128:] = acc[h, :, 128:] + dot(ds, kk)
                dkt[hs, pl.ds(ja, QB)] = dkt[hs, pl.ds(ja, QB)] + dot(qt[hs, :], ds)
                dvt[hs, pl.ds(ja, QB)] = dvt[hs, pl.ds(ja, QB)] + dot(dot_t[hs, :], p.astype(BF16))

        def free(j, c2):
            unit(j, None)
            return c2

        lax.fori_loop(0, i, free, 0)
        unit(i, hidden())
        for part in range(2):
            piece = slice(rows * part, rows * (part + 1))
            dq = jnp.where(low_head, acc[0, piece, 128:], acc[1, piece, 128:]) * HD**-0.5
            dfused[pl.ds(aligned(at + rows * part, rows), rows), :128] = turn(dq, angles(2 * i + part), True).astype(BF16)

    GVIEW = (
        lambda b: gin.at[pl.ds(aligned(256 * b, 256), 256)],
        lambda b: gexp.at[pl.ds(aligned(256 * b, 256), 256)],
        lambda b: gred.at[pl.ds(aligned(128 * b, 128), 128)],
        lambda b: gz.at[b],
    )
    RZ = (rz_in, rz_exp, rz_red, rz_out)
    COMB = ((0, 1, 3), (3, 2, 0))

    def zr_direct(dest):
        ok = d != dest
        if dest == 3:
            ok = ok & (d != 0) & (d != 1)
        if dest == 0:
            ok = ok & (d != 3) & (d != 2)
        return ok

    def zr_copy(a, src_block, dest, slot, sem):
        return rc(GVIEW[a](src_block), RZ[a].at[slot], zr_s.at[a], zr_r.at[a, slot], dest, s)

    def zr_first(a):
        for src, via, dest in COMB:
            @pl.when(d == src)
            def _():
                zr_copy(a, dest, via, via, dest).start()

    def zr_send(a):
        for dest in (3, 0, 2, 1):
            @pl.when(zr_direct(dest))
            def _():
                zr_copy(a, dest, dest, d, dest).start()

    def zr_join(a):
        for src, via, dest in COMB:
            @pl.when(d == via)
            def _():
                zr_copy(a, dest, dest, d, dest).wait_recv()
                ref = GVIEW[a](dest)
                ref[...] = (ref[...].astype(F32) + RZ[a][via].astype(F32)).astype(BF16)
                zr_copy(a, dest, dest, d, dest).start()

    def zr_total(a):
        ref = GVIEW[a](d)
        for src in range(NZ):
            came = d != src
            if src == 0:
                came = came & (d != 3)
            if src == 3:
                came = came & (d != 0)

            @pl.when(came)
            def _():
                zr_copy(a, d, d, src, src).wait_recv()
        use = []
        for src in range(NZ):
            came = d != src
            if src == 0:
                came = came & (d != 3)
            if src == 3:
                came = came & (d != 0)
            use.append(came)
        return ref, use

    def zr_sum(a, use, base, at, n):
        total = base
        for src in range(NZ):
            piece = RZ[a][src, pl.ds(at, n), :].astype(F32)
            total = total + jnp.where(use[src], piece, 0.0)
        return total

    def zr_sent(a):
        whole = (gin, gexp, gred, gz)[a]
        bundle(whole.at[pl.ds(0, whole.shape[0] // 4 * 3)], zr_s.at[a], zr_r.at[a, 0]).wait_send()

    def dest_send(a, dest):
        for src, via, to in COMB:
            if to == dest:
                @pl.when(d == src)
                def _():
                    zr_copy(a, to, via, via, to).start()

        @pl.when(zr_direct(dest))
        def _():
            zr_copy(a, dest, dest, d, dest).start()

    for i in (0, 3, 4, 7, 8):
        ag_arrived(1, i)
    wo_group = bundle(wz.at[pl.ds(1, 3)], wo_s.at[0], wo_r.at[0])
    wo_group.wait_recv()

    def loop(n, f):
        def step(i, carry):
            f(i)
            return carry
        lax.fori_loop(0, n, step, 0)

    def do_block(b):
        at = aligned(4 * rows * b, 4 * rows)
        do_s[pl.ds(at, 4 * rows), :] = dot_nt(dyg[pl.ds(at, 4 * rows), :], wout[...]).astype(BF16)

    loop(NP // 4, do_block)
    gout[...] = dot_tn(o_s[...], dyg[...]).astype(BF16)

    def go_copy(m, incoming):
        t4 = lax.rem(peer(m), 4)
        src = gout.at[pl.ds(aligned(32 * t4, 32), 32)]
        dst = gz.at[t4 if incoming else quad]
        return rc(src, dst, go_s.at[0], go_r.at[0], d, peer(m))

    for m in range(1, 4):
        go_copy(m, False).start()
    gz[quad] = gout[pl.ds(aligned(32 * quad, 32), 32), :]
    early = 1

    def back_early(step):
        attend_back(NP // 2 - 1 - step)

    loop(early, back_early)
    go_group = bundle(gz.at[pl.ds(1, 3)], go_s.at[0], go_r.at[0])
    go_group.wait_recv()
    for dest in (3, 0, 2, 1):
        dest_send(3, dest)
    z_arrived(1)
    z_arrived(2)

    for dd in range(NZ):
        ebs[:, 128 * dd : 128 * (dd + 1)] = jnp.broadcast_to(vt[s, dd, 3:4, :], (8, 128))
    geb[...] = jnp.zeros_like(geb)
    sums[...] = jnp.zeros_like(sums)
    sums[2:3, :] = jnp.sum(dyg[pl.ds(aligned(rows * s, rows), rows), :].astype(F32), axis=0, keepdims=True)

    def ffn_block(b):
        at = pl.ds(aligned(rows * b, rows), rows)
        e = dot(xn[at, :], wexp[...]) + ebs[0:1, :]
        up = dot_nt(dyg[at, :], wred[...])
        a, slope = gelu_pair(e)
        act_s[at, :] = a.astype(BF16)
        de = (up * slope).astype(BF16)
        de_s[at, :] = de
        geb[...] = geb[...] + jnp.sum(de.astype(F32).reshape(rows // 8, 8, 4 * 128), axis=0)

    loop(NP, ffn_block)

    def gexp_block(b):
        at = aligned(256 * b, 256)
        gexp[pl.ds(at, 256), :] = dot_tn(xn[:, pl.ds(at, 256)], de_s[...]).astype(BF16)

    def gred_pair(one, two):
        left = jnp.concatenate(
            [act_s[:, 128 * one : 128 * (one + 1)], act_s[:, 128 * two : 128 * (two + 1)]], axis=1
        )
        both = dot_tn(left, dyg[...]).astype(BF16)
        gred[128 * one : 128 * (one + 1), :] = both[:128]
        gred[128 * two : 128 * (two + 1), :] = both[128:]

    for pair in ((3, 0), (2, 1)):
        gred_pair(*pair)
        for dest in pair:
            dest_send(2, dest)

    ag_sent(0)

    def chip_rows(m):
        return aligned(2 * rows * lax.div(peer(m), 2), 2 * rows)

    def out_block(m):
        at = pl.ds(chip_rows(m), 2 * rows)
        for c in range(0, D, D // 2):
            cols = slice(c, c + D // 2)
            pout[at, cols] = (dot(o_s[at, :], wout[:, cols]) + dot(act_s[at, :], wred[:, cols])).astype(BF16)

    def dn_block(m):
        at = pl.ds(chip_rows(m), 2 * rows)
        for c in range(0, D, D // 2):
            cols = slice(c, c + D // 2)
            dn = dot_nt(de_s[at, :], wexp[cols, :]) + dot_nt(dfused[at, :], win[cols, :])
            pdn[at, cols] = dn.astype(BF16)
            sums[0:1, cols] = sums[0:1, cols] + jnp.sum(dn * xn[at, cols].astype(F32), axis=0, keepdims=True)
            sums[1:2, cols] = sums[1:2, cols] + jnp.sum(dn, axis=0, keepdims=True)

    RS = ((pout, sib_o, r1_o, r2_o), (pdn, sib_d, r1_d, r2_d))

    def part(which, m, lo, n):
        return RS[which][0].at[pl.ds(aligned(rows * peer(m) + lo, half), n)]

    RSM = (
        (1, 7, 0, rows, lambda w: RS[w][1].at[0]),
        (1, 3, 0, rows, lambda w: RS[w][1].at[1]),
        (1, 5, 0, rows, lambda w: RS[w][1].at[2]),
        (1, 1, 0, rows, lambda w: RS[w][1].at[3]),
        (2, 6, 0, half, lambda w: RS[w][2].at[0]),
        (4, 6, half, half, lambda w: RS[w][2].at[1]),
        (2, 2, 0, half, lambda w: RS[w][3].at[0, pl.ds(0, half)]),
        (4, 4, half, half, lambda w: RS[w][3].at[1, pl.ds(half, half)]),
        (2, 2, half, half, lambda w: RS[w][3].at[0, pl.ds(half, half)]),
        (4, 4, 0, half, lambda w: RS[w][3].at[1, pl.ds(0, half)]),
    )

    def rs_copy(w, i):
        to, blk, lo, n, land = RSM[i]
        return rc(part(w, blk, lo, n), land(w), rs_s.at[w], rs_r.at[w, i], d, peer(to))

    def add_into(w, m, lo, n, came):
        def step(c):
            ref = RS[w][0].at[pl.ds(aligned(rows * peer(m) + lo + 64 * c, 64), 64)]
            ref[...] = (ref[...].astype(F32) + came[pl.ds(aligned(64 * c, 64), 64), :].astype(F32)).astype(BF16)
        loop(n // 64, step)

    def rs_across(w):
        rs_copy(w, 0).wait_recv()
        add_into(w, 6, 0, rows, RS[w][1].at[0])
        rs_copy(w, 4).start()
        rs_copy(w, 5).start()

    def rs_pair(w, which):
        rs_copy(w, 1 + which).wait_recv()
        add_into(w, (2, 4)[which], 0, rows, RS[w][1].at[1 + which])
        rs_copy(w, 6 + which).start()

    def rs_near(w, which):
        rs_copy(w, 5 - which).wait_recv()
        add_into(w, (2, 4)[which], (half, 0)[which], half, RS[w][2].at[1 - which])
        rs_copy(w, 8 + which).start()

    def rs_last(w):
        for i in (3, 6, 7, 8, 9):
            rs_copy(w, i).wait_recv()

    for i, m in enumerate((7, 3)):
        out_block(m)
        rs_copy(0, i).start()
    for dest in (3, 0, 2, 1):
        gexp_block(dest)
        dest_send(1, dest)
    for i, m in ((2, 5), (3, 1)):
        out_block(m)
        rs_copy(0, i).start()

    def back_step(step):
        attend_back(NP // 2 - 1 - early - step)

        @pl.when(step == 0)
        def _():
            rs_across(0)
            zr_join(2)
            rs_pair(0, 0)
            rs_pair(0, 1)

        @pl.when(step == 1)
        def _():
            zr_join(3)
            rs_near(0, 0)
            rs_near(0, 1)

        @pl.when(step == 2)
        def _():
            zr_join(1)

    loop(NP // 2 - early, back_step)

    def kv_block(b):
        at = aligned(rows * b, rows)
        dk = jnp.transpose(dkt[:, pl.ds(at, rows)])
        dv = jnp.transpose(dvt[:, pl.ds(at, rows)].astype(BF16))
        dfused[pl.ds(at, rows), 128:256] = turn(dk, angles(b), True).astype(BF16)
        dfused[pl.ds(at, rows), 256:] = dv

    loop(NP, kv_block)

    def gin_block(b):
        at = aligned(256 * b, 256)
        gin[pl.ds(at, 256), :] = dot_tn(xn[:, pl.ds(at, 256)], dfused[...]).astype(BF16)

    for i, m in enumerate((7, 3, 5)):
        dn_block(m)
        rs_copy(1, i).start()
    rs_across(1)
    for dest in (3, 0):
        gin_block(dest)
        dest_send(0, dest)
    dn_block(1)
    rs_copy(1, 3).start()
    for yy in range(2):
        for dd in range(NZ):
            group = 2 * dd + yy
            sv[yy, dd] = sums[:, 128 * group : 128 * (group + 1)]

    def sp_copy(m):
        return rc(sv.at[lax.div(peer(m), 4)], rv.at[m], sp_s.at[0], sp_r.at[0], d, peer(m))

    for m in range(1, NP):
        sp_copy(m).start()
    rs_pair(1, 0)
    rs_pair(1, 1)
    for dest in (2, 1):
        gin_block(dest)
        dest_send(0, dest)
    zr_join(0)
    rs_near(1, 0)
    rs_near(1, 1)
    geb_row = jnp.sum(geb[...], axis=0, keepdims=True)
    sp_group = bundle(rv.at[pl.ds(1, NP - 1)], sp_s.at[0], sp_r.at[0])
    sp_group.wait_recv()
    tiles = sv[ybit]
    for m in range(1, NP):
        tiles = tiles + rv[m]
    for dd in range(NZ):
        ebt = jnp.broadcast_to(geb_row[:, 128 * dd : 128 * (dd + 1)], (8, 128))
        zt[dd] = jnp.where(rows8 == 3, ebt, tiles[dd])

    def sz_copy(i, incoming):
        return rc(zt.at[other(i)], rzv.at[i], sz_s.at[0], sz_r.at[0], other(i), s)

    for i in range(1, NZ):
        sz_copy(i, False).start()

    def total_rows(a, n):
        ref, use = zr_total(a)

        def step(c):
            at = aligned(32 * c, 32)
            block = ref.at[pl.ds(at, 32)]
            block[...] = zr_sum(a, use, block[...].astype(F32), at, 32).astype(BF16)
        loop(n // 32, step)

    def back_copy(which, m, incoming):
        src = (gin, gexp)[which].at[pl.ds(aligned(256 * d + 32 * peer(m), 32), 32)]
        dst = (rb_in, rb_exp)[which].at[m]
        return rc(src, dst, b_s.at[which], b_r.at[which], d, peer(m))

    def back_group(which):
        return bundle((rb_in, rb_exp)[which].at[pl.ds(1, NP - 1)], b_s.at[which], b_r.at[which])

    total_rows(1, 256)
    for m in range(1, NP):
        back_copy(1, m, False).start()

    ref_r, use_r = zr_total(2)

    def red_total(c):
        at = aligned(32 * c, 32)
        tred_ref[pl.ds(at, 32), :] = zr_sum(2, use_r, ref_r[pl.ds(at, 32), :].astype(F32), at, 32)
    loop(4, red_total)
    mine = pl.ds(aligned(256 * d + 32 * s, 32), 32)
    leaving = []

    def leave(src, dst):
        out = pltpu.make_async_copy(src, dst, out_sem.at[len(leaving)])
        out.start()
        leaving.append(out)

    leave(tred_ref, tred_out)
    leave(gexp.at[mine], exp_out.at[0])
    rs_last(0)

    def out_final(c):
        at = aligned(32 * c, 32)
        hout_ref[pl.ds(at, 32), :] = (
            x_ref[pl.ds(at, 32), :].astype(F32) + rs_total32(0, c) + vecs[2:3, :]
        ).astype(BF16)

    def rs_total32(w, c):
        at = aligned(32 * c, 32)
        own = RS[w][0][pl.ds(aligned(rows * s + 32 * c, 32), 32), :].astype(F32)
        own = own + RS[w][1][3, pl.ds(at, 32), :].astype(F32)
        own = own + RS[w][3][0, pl.ds(at, 32), :].astype(F32)
        return own + RS[w][3][1, pl.ds(at, 32), :].astype(F32)

    loop(rows // 32, out_final)
    leave(hout_ref, hout_out)
    def grad_final(c):
        at = aligned(32 * c, 32)
        dn = rs_total32(1, c)
        unit, inv = unit_of(x_ref[pl.ds(at, 32), :])
        dyf = dyg[pl.ds(aligned(rows * s + 32 * c, 32), 32), :].astype(F32)
        g = dn * vecs[0:1, :]
        hg = inv * (
            g - jnp.mean(g, axis=1, keepdims=True) - unit * jnp.mean(g * unit, axis=1, keepdims=True)
        ) + dyf
        hgrad_ref[pl.ds(at, 32), :] = hg.astype(BF16)

    total_rows(0, 256)
    for m in range(1, NP):
        back_copy(0, m, False).start()
    rs_last(1)
    leave(gin.at[mine], in_out.at[0])
    loop(rows // 32, grad_final)
    leave(hgrad_ref, hgrad_out)
    ref_o, use_o = zr_total(3)
    tout_ref[...] = zr_sum(3, use_o, ref_o[...].astype(F32), 0, 32)

    leave(tout_ref, tout_out)
    back_group(1).wait_recv()
    leave(rb_exp.at[pl.ds(1, NP - 1)], exp_out.at[pl.ds(1, NP - 1)])
    back_group(0).wait_recv()
    leave(rb_in.at[pl.ds(1, NP - 1)], in_out.at[pl.ds(1, NP - 1)])
    sz_group = bundle(rzv.at[pl.ds(1, NZ - 1)], sz_s.at[0], sz_r.at[0])
    sz_group.wait_recv()
    tile = zt[d]
    for i in range(1, NZ):
        tile = tile + rzv[i]
    tile_ref[...] = jnp.where(rows8 == 3, tile, pltpu.roll(tile, lax.rem(128 - 32 * quad, 128), 1))

    for out in leaving:
        out.wait()
    for w in range(2):
        a2a_group(w).wait_send()
        back_group(w).wait_send()
    for g in (vz_group, vp_group, wo_group, go_group, sp_group, sz_group):
        g.wait_send()
    ag_sent(1)
    for w in range(2):
        bundle(RS[w][0].at[pl.ds(0, 7 * rows)], rs_s.at[w], rs_r.at[w, 0]).wait_send()
    for a in range(4):
        z_sent(a)
        zr_sent(a)


def update_kernel(*refs):
    weights, moments = refs[0:8], refs[8:16]
    rate_ref, decay_ref, hout_in, hgrad_in, gin, gexp, gred, gout, tile = refs[16:25]
    hout, hgrad = refs[25:27]
    new_moments, new_weights = refs[27:35], refs[35:43]
    s = lax.axis_index("seq")
    keep = 1.0 - decay_ref[0]
    rate = rate_ref[0]

    def update(k, index, grad):
        moment = 0.5 * moments[k][index] + grad * (0.5 / NZ)
        new_moments[k][index] = moment
        new_weights[k][index] = keep * weights[k][index] - rate * moment

    hout[...] = hout_in[...]
    hgrad[...] = hgrad_in[...]
    gain = weights[0][...].astype(BF16).astype(F32)
    shift = weights[1][...].astype(BF16).astype(F32)
    shift_grad = tile[1:2, :32]
    update(0, ..., (tile[0:1, :32] - shift * shift_grad) / gain)
    update(1, ..., shift_grad)
    update(7, ..., tile[2:3, :32])
    update(5, ..., tile[3:4, :])
    update(6, ..., gred[...])
    update(3, ..., gout[...])
    core = lax.rem(s, 2)
    xbit = lax.rem(lax.div(s, 2), 2)
    ybit = lax.div(s, 4)
    for m in range(NP):
        t = s
        if m & 1:
            t = t + (1 - 2 * core)
        if m & 2:
            t = t + 2 * (1 - 2 * xbit)
        if m & 4:
            t = t + 4 * (1 - 2 * ybit)
        pair = 2 * lax.rem(t, 4) + lax.div(t, 4)
        for part in range(3):
            cols = pl.ds(aligned(128 * pair + 1024 * part, 128), 128)
            update(2, (slice(None), cols), gin[m, :, 128 * part : 128 * (part + 1)].astype(F32))
        for e in range(NZ):
            cols = pl.ds(aligned(128 * (8 * e + t), 128), 128)
            update(4, (slice(None), cols), gexp[m, :, 128 * e : 128 * (e + 1)].astype(F32))


def fused_shards(*args):
    (hidden_in, out_cotangent), weights, moments = args[:2], args[2:10], args[10:18]
    rows = hidden_in.shape[1]
    seq = rows * NP
    freq = 10000.0 ** (-2.0 * np.arange(ROT // 2) / ROT)
    lane_freq = np.tile(freq, 128 // (ROT // 2))[None, :]
    near = np.arange(rows)[:, None] * lane_freq
    far = (rows * np.arange(NP))[:, None] * lane_freq
    tables = [jnp.asarray(f(a), F32) for a in (near, far) for f in (np.cos, np.sin)]

    def flat(v):
        return v.reshape(1, -1) if v.ndim == 1 else v

    shards_in = [flat(w) for w in weights]
    ff = weights[6].shape[0] * NZ
    moments_in = [flat(m) for m in moments]
    shard_shapes = [jax.ShapeDtypeStruct(w.shape, F32) for w in shards_in]
    vm = pltpu.VMEM
    dma = pltpu.SemaphoreType.DMA
    scratch = [
        vm((seq, D), BF16), vm((seq, D), BF16), vm((seq, D), BF16),
        vm((D, 384), BF16), vm((D, ff), BF16), vm((ff, D), BF16), vm((128, D), BF16), vm((NZ, 32, D), BF16),
        vm((NP, 32, 384), BF16), vm((NP, 32, ff), BF16),
        vm((seq, 128), BF16), vm((seq, 128), BF16),
        vm((128, seq), F32), vm((128, seq), F32), vm((seq, 384), BF16),
        vm((2, NP // 2, 2 * rows, 2 * rows), F32), vm((seq, 128), F32),
        vm((2, 2 * rows, 128), F32), vm((2, 2 * rows, 256), F32),
        vm((seq, ff), BF16), vm((seq, ff), BF16), vm((seq, D), BF16),
        vm((4, rows, D), BF16), vm((4, rows, D), BF16),
        vm((2, rows // 2, D), BF16), vm((2, rows, D), BF16), vm((2, rows // 2, D), BF16), vm((2, rows, D), BF16),
        vm((D, 384), BF16), vm((D, ff), BF16), vm((ff, D), BF16), vm((128, D), BF16), vm((NZ, 32, D), BF16),
        vm((NZ, 256, 384), BF16), vm((NZ, 256, ff), BF16), vm((NZ, 128, D), BF16), vm((NZ, 32, D), BF16),
        vm((NP, 32, 384), BF16), vm((NP, 32, ff), BF16),
        vm((NP, NZ, 8, 128), F32), vm((8, D), F32), vm((8, ff), F32), vm((8, ff), F32), vm((8, D), F32),
        vm((2, NZ, 8, 128), F32), vm((NP, NZ, 8, 128), F32), vm((NZ, 8, 128), F32), vm((NZ, 8, 128), F32),
        dma((2,)), dma((2,)), dma((2,)), dma((2, 9)), dma((4,)), dma((4, 4)),
        dma((1,)), dma((1,)), dma((1,)), dma((1,)), dma((1,)), dma((1,)),
        dma((2,)), dma((2, 10)), dma((4,)), dma((4, 4)), dma((1,)), dma((1,)),
        dma((2,)), dma((2,)), dma((1,)), dma((1,)), dma((1,)), dma((1,)), dma,
        vm((rows, D), BF16), vm((rows, D), BF16), vm((128, D), F32), vm((32, D), F32), dma((8,)),
    ]
    in_vmem = pl.BlockSpec(memory_space=pltpu.VMEM)
    in_smem = pl.BlockSpec(memory_space=pltpu.SMEM)

    def body(*refs):
        block_kernel(rows, *refs)

    rows_shape = jax.ShapeDtypeStruct((rows, D), BF16)
    grads = pl.pallas_call(
        body,
        out_shape=[
            rows_shape, rows_shape,
            jax.ShapeDtypeStruct((NP, 32, 384), BF16), jax.ShapeDtypeStruct((NP, 32, ff), BF16),
            jax.ShapeDtypeStruct((128, D), F32), jax.ShapeDtypeStruct((32, D), F32),
            jax.ShapeDtypeStruct((8, 128), F32),
        ],
        in_specs=[in_vmem, pl.BlockSpec(memory_space=pl.ANY)] + [in_vmem] * 12,
        out_specs=[pl.BlockSpec(memory_space=pl.ANY)] * 6 + [in_vmem],
        scratch_shapes=scratch,
        compiler_params=pltpu.CompilerParams(
            collective_id=0, has_side_effects=True, vmem_limit_bytes=63 * 2**20
        ),
        name="block_step",
    )(
        hidden_in.reshape(rows, D), out_cotangent.reshape(rows, D), *shards_in, *tables,
    )
    outs = pl.pallas_call(
        update_kernel,
        out_shape=[rows_shape, rows_shape] + shard_shapes + shard_shapes,
        in_specs=[in_vmem] * 16 + [in_smem] * 2 + [in_vmem] * 7,
        out_specs=[in_vmem] * 18,
        compiler_params=pltpu.CompilerParams(vmem_limit_bytes=63 * 2**20),
        name="block_update",
    )(*shards_in, *moments_in, args[18], args[19], *grads)
    small = [w.shape for w in weights]
    return (
        outs[0].reshape(hidden_in.shape),
        outs[1].reshape(hidden_in.shape),
        *[o.reshape(sh) for o, sh in zip(outs[2:], small + small)],
    )


def fits(mesh):
    return mesh.shape["dp"] == NZ and mesh.shape["seq"] == NP


def solution(mesh):
    placed = (
        P("dp", "seq", None),
        P("dp", "seq", None),
        P(("dp", "seq")),
        P(("dp", "seq")),
        P(("dp", "seq"), None),
        P(("dp", "seq"), None),
        P(("dp", "seq"), None),
        P(("dp", "seq")),
        P(("dp", "seq"), None),
        P(("dp", "seq")),
        P(("dp", "seq")),
        P(("dp", "seq")),
        P(("dp", "seq"), None),
        P(("dp", "seq"), None),
        P(("dp", "seq"), None),
        P(("dp", "seq")),
        P(("dp", "seq"), None),
        P(("dp", "seq")),
        P(),
        P(),
    )
    return jax.shard_map(
        fused_shards if fits(mesh) else shards,
        mesh=mesh,
        in_specs=placed,
        out_specs=(
            P("dp", "seq", None),
            P("dp", "seq", None),
            P(("dp", "seq")),
            P(("dp", "seq")),
            P(("dp", "seq"), None),
            P(("dp", "seq"), None),
            P(("dp", "seq"), None),
            P(("dp", "seq")),
            P(("dp", "seq"), None),
            P(("dp", "seq")),
            P(("dp", "seq")),
            P(("dp", "seq")),
            P(("dp", "seq"), None),
            P(("dp", "seq"), None),
            P(("dp", "seq"), None),
            P(("dp", "seq")),
            P(("dp", "seq"), None),
            P(("dp", "seq")),
        ),
        check_vma=False,
    )
```

```python
import jax
import jax.numpy as jnp
import numpy as np
from jax import lax
from jax.experimental import pallas as pl
from jax.experimental.pallas import tpu as pltpu
from jax.sharding import PartitionSpec as P

D = 1024
H = 16
HD = 64
ROT = 32


epsilon = 1e-05
masked_score = -1e30


def rotary(block, positions, direction):
    half_rot = ROT // 2
    frequency = 10000.0 ** (-2.0 * jnp.arange(half_rot, dtype=jnp.float32) / ROT)
    angles = direction * positions[:, None] * frequency[None, :]
    cosine = jnp.cos(angles)[:, None, :]
    sine_part = jnp.sin(angles)[:, None, :]
    first_half = block[..., :half_rot]
    second = block[..., half_rot:ROT]
    return jnp.concatenate(
        [
            first_half * cosine - second * sine_part,
            second * cosine + first_half * sine_part,
            block[..., ROT:],
        ],
        axis=-1,
    )


def gelu_tanh(values):
    return jax.nn.gelu(values, approximate=True)


def gelu_back(expanded, upstream):
    unused_out, pullback = jax.vjp(gelu_tanh, expanded)
    return pullback(upstream)[0]


def heads_of(rows):
    return rows.reshape(rows.shape[0], H, HD)


def scores_of(query_rows, key_rows):
    score_scale = HD ** (-0.5)
    return (
        jnp.einsum(
            "qhd,khd->hqk",
            heads_of(query_rows),
            heads_of(key_rows),
            preferred_element_type=jnp.float32,
        )
        * score_scale
    )


def shards(
    hidden_in,
    out_cotangent,
    norm_gain,
    norm_shift,
    attend_in,
    attend_out,
    expand_weight,
    expand_bias,
    reduce_weight,
    reduce_bias,
    gain_moment,
    shift_moment,
    inward_moment,
    outward_moment,
    expand_moment,
    expbias_moment,
    reduce_moment,
    redbias_moment,
    learn_rate,
    decay_rate,
):
    score_scale = HD ** (-0.5)
    gain_low, shift_low, inward_mat, outward_mat, expand_mat, expand_vec, reduce_mat, reduce_vec = (
        lax.all_gather(norm_gain.astype(jnp.bfloat16), ("dp", "seq"), axis=0, tiled=True),
        lax.all_gather(norm_shift.astype(jnp.bfloat16), ("dp", "seq"), axis=0, tiled=True),
        lax.all_gather(attend_in.astype(jnp.bfloat16), ("dp", "seq"), axis=0, tiled=True),
        lax.all_gather(attend_out.astype(jnp.bfloat16), ("dp", "seq"), axis=0, tiled=True),
        lax.all_gather(expand_weight.astype(jnp.bfloat16), ("dp", "seq"), axis=0, tiled=True),
        lax.all_gather(expand_bias.astype(jnp.bfloat16), ("dp", "seq"), axis=0, tiled=True),
        lax.all_gather(reduce_weight.astype(jnp.bfloat16), ("dp", "seq"), axis=0, tiled=True),
        lax.all_gather(reduce_bias.astype(jnp.bfloat16), ("dp", "seq"), axis=0, tiled=True),
    )
    seq_count, block_len, model_width = hidden_in.shape
    row_count = seq_count * block_len
    full_len = block_len * lax.axis_size("seq")
    seq_start = lax.axis_index("seq") * block_len
    query_index = seq_start + jnp.arange(block_len, dtype=jnp.int32)
    key_index = jnp.arange(full_len, dtype=jnp.int32)
    causal = key_index[None, :] <= query_index[:, None]
    positions = query_index.astype(jnp.float32)
    inputs = hidden_in.astype(jnp.float32).reshape(row_count, model_width)
    row_mean = jnp.mean(inputs, axis=-1, keepdims=True)
    centred = inputs - row_mean
    row_var = jnp.mean(centred * centred, axis=-1, keepdims=True)
    inverse = lax.rsqrt(row_var + epsilon)
    unit_rows = centred * inverse
    gain_full = gain_low.astype(jnp.float32)
    normed = (unit_rows * gain_full + shift_low.astype(jnp.float32)).astype(jnp.bfloat16)
    joined = jnp.dot(normed, inward_mat, preferred_element_type=jnp.float32).reshape(
        seq_count, block_len, 3 * D
    )
    query = (
        rotary(joined[..., :D].reshape(seq_count, block_len, H, HD), positions, 1.0)
        .astype(jnp.bfloat16)
        .reshape(seq_count, block_len, D)
    )
    keyed = (
        rotary(joined[..., D : 2 * D].reshape(seq_count, block_len, H, HD), positions, 1.0)
        .astype(jnp.bfloat16)
        .reshape(seq_count, block_len, D)
    )
    valued = joined[..., 2 * D :].astype(jnp.bfloat16)
    key_all, value_all = (
        lax.all_gather(keyed, "seq", axis=1, tiled=True),
        lax.all_gather(valued, "seq", axis=1, tiled=True),
    )

    def attend(operands):
        query_seq, key_seq, value_seq = operands
        scores = jnp.where(causal[None], scores_of(query_seq, key_seq), masked_score)
        row_max = jnp.max(scores, axis=-1, keepdims=True)
        log_total = row_max + jnp.log(jnp.sum(jnp.exp(scores - row_max), axis=-1, keepdims=True))
        weights = jnp.exp(scores - log_total).astype(jnp.bfloat16)
        mixed = jnp.einsum(
            "hqk,khd->qhd", weights, heads_of(value_seq), preferred_element_type=jnp.float32
        )
        return (mixed.reshape(-1, D).astype(jnp.bfloat16), jnp.transpose(log_total[..., 0]))

    attended, log_totals = lax.map(attend, (query, key_all, value_all))
    expanded = jnp.dot(normed, expand_mat, preferred_element_type=jnp.float32) + expand_vec.astype(
        jnp.float32
    )
    activated = gelu_tanh(expanded).astype(jnp.bfloat16)
    flat_attn = attended.reshape(row_count, D)
    result = (
        inputs
        + jnp.dot(flat_attn, outward_mat, preferred_element_type=jnp.float32)
        + jnp.dot(activated, reduce_mat, preferred_element_type=jnp.float32)
        + reduce_vec.astype(jnp.float32)
    )
    hidden_out = result.astype(jnp.bfloat16).reshape(seq_count, block_len, D)
    upstream = out_cotangent.reshape(row_count, D)
    grad_outward = jnp.einsum("rd,re->de", flat_attn, upstream, preferred_element_type=jnp.float32)
    grad_reduce = jnp.einsum("rf,re->fe", activated, upstream, preferred_element_type=jnp.float32)
    grad_redbias = jnp.sum(upstream.astype(jnp.float32), axis=0)
    attn_back = (
        jnp.einsum("re,de->rd", upstream, outward_mat, preferred_element_type=jnp.float32)
        .astype(jnp.bfloat16)
        .reshape(seq_count, block_len, D)
    )
    act_back = jnp.einsum("re,fe->rf", upstream, reduce_mat, preferred_element_type=jnp.float32)
    expand_back = gelu_back(expanded, act_back).astype(jnp.bfloat16)
    grad_expbias = jnp.sum(expand_back.astype(jnp.float32), axis=0)
    grad_expand = jnp.einsum("rd,rf->df", normed, expand_back, preferred_element_type=jnp.float32)
    norm_back = jnp.einsum("rf,df->rd", expand_back, expand_mat, preferred_element_type=jnp.float32)

    def query_side(query_seq, key_seq, value_seq, back_seq, total_seq):
        scores = jnp.where(causal[None], scores_of(query_seq, key_seq), masked_score)
        probs = jnp.exp(scores - jnp.transpose(total_seq)[:, :, None])
        prob_grad = jnp.einsum(
            "qhd,khd->hqk",
            heads_of(back_seq),
            heads_of(value_seq),
            preferred_element_type=jnp.float32,
        )
        row_delta = jnp.sum(probs * prob_grad, axis=-1, keepdims=True)
        score_grad = (probs * (prob_grad - row_delta)).astype(jnp.bfloat16)
        query_grad = (
            jnp.einsum(
                "hqk,khd->qhd", score_grad, heads_of(key_seq), preferred_element_type=jnp.float32
            )
            * score_scale
        )
        return (probs, score_grad, query_grad, row_delta)

    def attend_back(operands):
        query_seq, key_seq, value_seq, back_seq, total_seq = operands
        probs, score_grad, query_grad, row_delta = query_side(
            query_seq, key_seq, value_seq, back_seq, total_seq
        )
        key_grad = (
            jnp.einsum(
                "hqk,qhd->khd", score_grad, heads_of(query_seq), preferred_element_type=jnp.float32
            )
            * score_scale
        )
        value_grad = jnp.einsum(
            "hqk,qhd->khd",
            probs.astype(jnp.bfloat16),
            heads_of(back_seq),
            preferred_element_type=jnp.float32,
        )
        return (query_grad, key_grad.reshape(-1, D), value_grad.reshape(-1, D))

    query_grads, key_terms, value_terms = lax.map(
        attend_back, (query, key_all, value_all, attn_back, log_totals)
    )
    key_grads, value_grads = (
        lax.psum_scatter(key_terms, "seq", scatter_dimension=1, tiled=True),
        lax.psum_scatter(value_terms, "seq", scatter_dimension=1, tiled=True),
    )
    query_turned = rotary(query_grads, positions, -1.0).reshape(seq_count, block_len, D)
    key_turned = rotary(key_grads.reshape(seq_count, block_len, H, HD), positions, -1.0).reshape(
        seq_count, block_len, D
    )
    joined_back = (
        jnp.concatenate([query_turned, key_turned, value_grads], axis=-1)
        .astype(jnp.bfloat16)
        .reshape(row_count, 3 * D)
    )
    grad_inward = jnp.einsum("rd,re->de", normed, joined_back, preferred_element_type=jnp.float32)
    norm_back = norm_back + jnp.einsum(
        "re,de->rd", joined_back, inward_mat, preferred_element_type=jnp.float32
    )
    grad_gain = jnp.sum(norm_back * unit_rows, axis=0)
    grad_shift = jnp.sum(norm_back, axis=0)
    unit_back = norm_back * gain_full
    input_back = inverse * (
        unit_back
        - jnp.mean(unit_back, axis=-1, keepdims=True)
        - unit_rows * jnp.mean(unit_back * unit_rows, axis=-1, keepdims=True)
    ) + upstream.astype(jnp.float32)
    hidden_grad = input_back.astype(jnp.bfloat16).reshape(seq_count, block_len, D)
    totals = (
        lax.psum_scatter(grad_gain, ("dp", "seq"), scatter_dimension=0, tiled=True),
        lax.psum_scatter(grad_shift, ("dp", "seq"), scatter_dimension=0, tiled=True),
        lax.psum_scatter(grad_inward, ("dp", "seq"), scatter_dimension=0, tiled=True),
        lax.psum_scatter(grad_outward, ("dp", "seq"), scatter_dimension=0, tiled=True),
        lax.psum_scatter(grad_expand, ("dp", "seq"), scatter_dimension=0, tiled=True),
        lax.psum_scatter(grad_expbias, ("dp", "seq"), scatter_dimension=0, tiled=True),
        lax.psum_scatter(grad_reduce, ("dp", "seq"), scatter_dimension=0, tiled=True),
        lax.psum_scatter(grad_redbias, ("dp", "seq"), scatter_dimension=0, tiled=True),
    )
    seq_total = seq_count * lax.axis_size("dp")
    step_rate = learn_rate[0]
    decay_now = decay_rate[0]
    params = (
        norm_gain,
        norm_shift,
        attend_in,
        attend_out,
        expand_weight,
        expand_bias,
        reduce_weight,
        reduce_bias,
    )
    moments = (
        gain_moment,
        shift_moment,
        inward_moment,
        outward_moment,
        expand_moment,
        expbias_moment,
        reduce_moment,
        redbias_moment,
    )
    momenta = [
        0.5 * moment + 0.5 * (summed_grad / seq_total)
        for moment, summed_grad in zip(moments, totals)
    ]
    updated = [
        (1.0 - decay_now) * weight_now - step_rate * momentum
        for weight_now, momentum in zip(params, momenta)
    ]
    return (
        hidden_out,
        hidden_grad,
        momenta[0],
        momenta[1],
        momenta[2],
        momenta[3],
        momenta[4],
        momenta[5],
        momenta[6],
        momenta[7],
        updated[0],
        updated[1],
        updated[2],
        updated[3],
        updated[4],
        updated[5],
        updated[6],
        updated[7],
    )


F32 = jnp.float32
BF16 = jnp.bfloat16
MESH = pl.DeviceIdType.MESH
NZ = 4
NP = 8
NT = (((1,), (1,)), ((), ()))
TN = (((0,), (0,)), ((), ()))


def dot(a, b):
    return jnp.dot(a, b, preferred_element_type=F32)


def dot_nt(a, b):
    return lax.dot_general(a, b, NT, preferred_element_type=F32)


def dot_tn(a, b):
    return lax.dot_general(a, b, TN, preferred_element_type=F32)


def aligned(value, unit):
    return pl.multiple_of(value, unit)


def gelu_pair(e):
    square = e * e
    t = jnp.tanh(e * (GELU_C + (GELU_C * GELU_A) * square))
    half = 0.5 + 0.5 * t
    slope = half + (0.5 * e) * (1.0 - t * t) * (GELU_C + (3.0 * GELU_C * GELU_A) * square)
    return e * half, slope


GELU_C = 0.7978845608028654
GELU_A = 0.044715


def block_kernel(rows, *refs):
    (
        x_ref, dy_ref, gain_ref, shift_ref, win_ref, wout_ref, wexp_ref, ebias_ref, wred_ref, rbias_ref,
        cosr_ref, sinr_ref, cosb_ref, sinb_ref,
        hout_out, hgrad_out, in_out, exp_out, tred_out, tout_out, tile_ref,
        xg, dyg, xn, win, wexp, wred, wout, wz, pin, pexp,
        o_s, do_s, dkt, dvt, dfused, sbuf, lse, mref, acc,
        act_s, de_s, pdn, sib_o, sib_d, r1_o, r2_o, r1_d, r2_d,
        gin, gexp, gred, gout, gz, rz_in, rz_exp, rz_red, rz_out, rb_in, rb_exp,
        vt, vecs, ebs, geb, sums, sv, rv, zt, rzv,
        a2a_s, a2a_r, ag_s, ag_r, z_s, z_r, vz_s, vz_r, vp_s, vp_r, wo_s, wo_r,
        rs_s, rs_r, zr_s, zr_r, go_s, go_r, b_s, b_r, sp_s, sp_r, sz_s, sz_r, dy_sem,
        hout_ref, hgrad_ref, tred_ref, tout_ref, out_sem,
    ) = refs
    pout = xg
    d = lax.axis_index("dp")
    s = lax.axis_index("seq")
    core = lax.rem(s, 2)
    xbit = lax.rem(lax.div(s, 2), 2)
    ybit = lax.div(s, 4)
    chip = lax.div(s, 2)
    quad = lax.rem(s, 4)

    def peer(m):
        out = s
        if m & 1:
            out = out + (1 - 2 * core)
        if m & 2:
            out = out + 2 * (1 - 2 * xbit)
        if m & 4:
            out = out + 4 * (1 - 2 * ybit)
        return out

    def pair_of(t):
        return 2 * lax.rem(t, 4) + lax.div(t, 4)

    def rc(src, dst, ssem, rsem, dd, ss):
        return pltpu.make_async_remote_copy(
            src_ref=src, dst_ref=dst, send_sem=ssem, recv_sem=rsem,
            device_id=(dd, ss), device_id_type=MESH,
        )

    barrier = pltpu.get_barrier_semaphore()
    for m in range(1, NP):
        pl.semaphore_signal(barrier, inc=1, device_id=(d, peer(m)), device_id_type=MESH)
    for dz in range(1, NZ):
        pl.semaphore_signal(barrier, inc=1, device_id=(lax.rem(d + dz, NZ), s), device_id_type=MESH)

    zrow = jnp.zeros((1, 96), F32)
    small = jnp.concatenate(
        [
            jnp.concatenate([r[...].astype(BF16).astype(F32), zrow], axis=1)
            for r in (gain_ref, shift_ref, rbias_ref)
        ]
        + [jnp.zeros((5, 128), F32)],
        axis=0,
    )
    small = pltpu.roll(small, 32 * quad, 1)
    rows8 = lax.broadcasted_iota(jnp.int32, (8, 128), 0)
    ebias_row = jnp.broadcast_to(ebias_ref[...].astype(BF16).astype(F32), (8, 128))
    vt[s, d] = jnp.where(rows8 == 3, ebias_row, small)
    wz[d] = wout_ref[...].astype(BF16)
    own_dy = pltpu.make_async_copy(dy_ref, dyg.at[pl.ds(aligned(rows * s, rows), rows)], dy_sem)
    own_dy.start()
    xg[pl.ds(aligned(rows * s, rows), rows), :] = x_ref[...]
    own_rows = aligned(32 * (8 * d + s), 32)

    def pack_in():
        for m in range(NP):
            j = pair_of(peer(m))
            for part in range(3):
                piece = win_ref[:, pl.ds(aligned(128 * j + 1024 * part, 128), 128)].astype(BF16)
                if m == 0:
                    win[pl.ds(own_rows, 32), 128 * part : 128 * (part + 1)] = piece
                else:
                    pin[m, :, 128 * part : 128 * (part + 1)] = piece

    def pack_exp():
        for m in range(NP):
            t = peer(m)
            for e in range(NZ):
                piece = wexp_ref[:, pl.ds(aligned(128 * (8 * e + t), 128), 128)].astype(BF16)
                if m == 0:
                    wexp[pl.ds(own_rows, 32), 128 * e : 128 * (e + 1)] = piece
                else:
                    pexp[m, :, 128 * e : 128 * (e + 1)] = piece

    pack_in()
    pl.semaphore_wait(barrier, NP - 1 + NZ - 1)

    def bundle(ref, ssem, rsem):
        return rc(ref, ref, ssem, rsem, d, peer(1))

    def a2a_msg(which, m):
        src = (pin, pexp)[which].at[m]
        dst = (win, wexp)[which].at[pl.ds(own_rows, 32)]
        return rc(src, dst, a2a_s.at[which], a2a_r.at[which], d, peer(m))

    def a2a_group(which):
        return bundle((pin, pexp)[which].at[pl.ds(1, NP - 1)], a2a_s.at[which], a2a_r.at[which])

    half = rows // 2
    AG = (
        (1, 0, 0, rows), (2, 0, 0, rows), (4, 0, 0, rows),
        (1, 2, 0, rows), (1, 4, 0, rows), (4, 2, half, half), (2, 4, 0, half),
        (1, 6, 0, half), (1, 6, half, half),
    )

    def ag_copy(which, i, incoming):
        to, blk, lo, n = AG[i]
        buf = (xg, dyg)[which]
        at = rows * peer(blk ^ (to if incoming else 0)) + lo
        ref = buf.at[pl.ds(aligned(at, half), n)]
        return rc(ref, ref, ag_s.at[which], ag_r.at[which, i], d, peer(to))

    def ag_sent(which):
        bundle((xg, dyg)[which].at[pl.ds(0, 7 * rows)], ag_s.at[which], ag_r.at[which, 0]).wait_send()

    def ag_start(which, i):
        ag_copy(which, i, False).start()

    def ag_arrived(which, i):
        ag_copy(which, i, True).wait_recv()

    ZVIEW = (
        lambda b: win.at[pl.ds(aligned(256 * b, 256), 256)],
        lambda b: wexp.at[pl.ds(aligned(256 * b, 256), 256)],
        lambda b: wred.at[pl.ds(aligned(128 * b, 128), 128)],
        lambda b: wz.at[b],
    )

    def z_direct(dest):
        ok = d != dest
        if dest == NZ - 1:
            ok = ok & (d != 0)
        if dest == 0:
            ok = ok & (d != NZ - 1)
        return ok

    def z_send(a):
        for dest in (3, 0, 2, 1):
            @pl.when(z_direct(dest))
            def _():
                rc(ZVIEW[a](d), ZVIEW[a](d), z_s.at[a], z_r.at[a, d], dest, s).start()

    FWD = ((2, 0, 3), (1, 3, 0))

    def z_wait_block(a, b):
        rc(ZVIEW[a](b), ZVIEW[a](b), z_s.at[a], z_r.at[a, b], d, s).wait_recv()

    def z_forward(a):
        for at, blk, dest in FWD:
            @pl.when(d == at)
            def _():
                z_wait_block(a, blk)
                rc(ZVIEW[a](blk), ZVIEW[a](blk), z_s.at[a], z_r.at[a, blk], dest, s).start()

    PACE = ((0, 1), (3, 2))

    def z_pace(a):
        for at, blk in PACE:
            @pl.when(d == at)
            def _():
                z_wait_block(a, blk)

    def z_arrived(a, paced=False):
        for b in range(NZ):
            need = d != b
            for at, blk, dest in FWD:
                if blk == b:
                    need = need & (d != at)
            for at, blk in PACE:
                if paced and blk == b:
                    need = need & (d != at)

            @pl.when(need)
            def _():
                z_wait_block(a, b)

    def z_sent(a):
        whole = (win, wexp, wred, wz)[a]
        inner = (d == 1) | (d == 2)

        @pl.when(inner)
        def _():
            bundle(whole, z_s.at[a], z_r.at[a, 0]).wait_send()

        @pl.when(jnp.logical_not(inner))
        def _():
            bundle(whole.at[pl.ds(0, whole.shape[0] // 2)], z_s.at[a], z_r.at[a, 0]).wait_send()

    def other(i):
        return lax.rem(d + i, NZ)

    def vz_copy(i, incoming):
        b = lax.rem(d + NZ - i, NZ) if incoming else d
        return rc(vt.at[s, b], vt.at[s, b], vz_s.at[0], vz_r.at[0], other(i), s)

    def vp_copy(m, incoming):
        b = peer(m) if incoming else s
        return rc(vt.at[b], vt.at[b], vp_s.at[0], vp_r.at[0], d, peer(m))

    for i in range(1, NZ):
        vz_copy(i, False).start()
    for m in range(1, NP):
        a2a_msg(0, m).start()
    z_send(3)
    for i in (1, 2, 0):
        ag_start(0, i)
    pack_exp()
    wred[pl.ds(aligned(128 * d, 128), 128), :] = wred_ref[...].astype(BF16)
    vz_group = bundle(zt.at[pl.ds(1, NZ - 1)], vz_s.at[0], vz_r.at[0])
    vz_group.wait_recv()
    for m in range(1, NP):
        vp_copy(m, False).start()
    a2a_group(0).wait_recv()
    z_send(0)
    for m in range(1, NP):
        a2a_msg(1, m).start()
    z_forward(3)
    z_pace(0)
    z_forward(0)
    z_send(2)
    ag_arrived(0, 1)
    ag_start(0, 5)
    ag_start(0, 3)
    ag_arrived(0, 2)
    ag_start(0, 6)
    ag_start(0, 4)
    a2a_group(1).wait_recv()
    z_send(1)

    def wo_copy(m, incoming):
        src = wz.at[lax.rem(peer(m), 4)]
        r = lax.rem(peer(m), 4) if incoming else quad
        dst = wout.at[pl.ds(aligned(32 * r, 32), 32)]
        return rc(src, dst, wo_s.at[0], wo_r.at[0], d, peer(m))

    vp_group = bundle(rv.at[pl.ds(1, NP - 1)], vp_s.at[0], vp_r.at[0])
    vp_group.wait_recv()
    for dd in range(NZ):
        for yy in range(2):
            group = 2 * dd + yy
            total = vt[4 * yy, dd]
            for jj in range(1, 4):
                total = total + vt[4 * yy + jj, dd]
            vecs[:, 128 * group : 128 * (group + 1)] = total

    def unit_of(xb):
        xf = xb.astype(F32)
        mu = jnp.mean(xf, axis=1, keepdims=True)
        cen = xf - mu
        var = jnp.mean(cen * cen, axis=1, keepdims=True)
        inv = lax.rsqrt(var + epsilon)
        return cen * inv, inv

    def norm_block(b):
        def step(c, carry):
            at = aligned(rows * b + 128 * c, 128)
            unit, _ = unit_of(xg[pl.ds(at, 128), :])
            xn[pl.ds(at, 128), :] = (unit * vecs[0:1, :] + vecs[1:2, :]).astype(BF16)
            return carry
        lax.fori_loop(0, rows // 128, step, 0)

    lane_b = lax.broadcasted_iota(jnp.int32, (rows, 128), 1)
    low_head = lane_b < HD
    in_head = lax.rem(lane_b, HD)
    first_rot = in_head < ROT // 2
    second_rot = (in_head >= ROT // 2) & (in_head < ROT)

    def angles(b):
        cb, sb = cosb_ref[pl.ds(b, 1), :], sinb_ref[pl.ds(b, 1), :]
        cr, sr = cosr_ref[...], sinr_ref[...]
        co = jnp.where(in_head < ROT, cr * cb - sr * sb, 1.0)
        si = sr * cb + cr * sb
        return co, jnp.where(first_rot, -si, 0.0), jnp.where(second_rot, si, 0.0)

    def turn(block, table, back=False):
        co, up, down = table
        moved = pltpu.roll(block, 128 - ROT // 2, 1) * up + pltpu.roll(block, ROT // 2, 1) * down
        return block * co - moved if back else block * co + moved

    norm_block(s)
    ag_arrived(0, 0)
    norm_block(peer(1))
    own_dy.wait()
    for i in (1, 2, 0):
        ag_start(1, i)
    norm_block(peer(2))
    norm_block(peer(4))
    ag_arrived(0, 3)
    norm_block(peer(3))
    ag_arrived(0, 4)
    norm_block(peer(5))
    ag_arrived(0, 6)
    ag_start(0, 7)
    ag_arrived(0, 5)
    ag_start(0, 8)
    norm_block(peer(6))
    ag_arrived(0, 7)
    ag_arrived(0, 8)
    norm_block(peer(7))
    z_arrived(3)
    for m in range(1, 4):
        wo_copy(m, False).start()
    wout[pl.ds(aligned(32 * quad, 32), 32), :] = wz[quad]
    z_arrived(0, paced=True)

    def qkv_step(n, carry):
        joined = dot(xn[pl.ds(aligned(2 * rows * n, 2 * rows), 2 * rows), :], win[...])
        for part in range(2):
            b = 2 * n + part
            at = pl.ds(aligned(rows * b, rows), rows)
            piece = joined[rows * part : rows * (part + 1)]
            table = angles(b)
            dfused[at, :128] = (turn(piece[:, :128], table) * HD**-0.5).astype(BF16)
            dfused[at, 128:256] = turn(piece[:, 128:256], table).astype(BF16)
            dfused[at, 256:] = piece[:, 256:].astype(BF16)
        return carry

    lax.fori_loop(0, NP // 2, qkv_step, 0)
    QB = 2 * rows
    lane_q = lax.broadcasted_iota(jnp.int32, (QB, 128), 1) < HD

    def wide(tile):
        return jnp.concatenate([tile] * (QB // 128), axis=1)

    def fold(v):
        out = v[:, :128]
        for c in range(1, QB // 128):
            out = jnp.maximum(out, v[:, 128 * c : 128 * (c + 1)])
        return out

    def by_head(block):
        zero = jnp.zeros_like(block)
        return jnp.where(lane_q, block, zero), jnp.where(lane_q, zero, block)

    def hidden():
        return lax.broadcasted_iota(jnp.int32, (QB, QB), 1) > lax.broadcasted_iota(jnp.int32, (QB, QB), 0)

    ones = jnp.ones((QB, 128), BF16)

    def attend_step(i, carry):
        at = aligned(QB * i, QB)
        qh = by_head(dfused[pl.ds(at, QB), :128])
        kj = dfused[pl.ds(at, QB), 128:256]
        mask = hidden()
        for h in range(2):
            sc = jnp.where(mask, masked_score, dot_nt(qh[h], kj))
            sbuf[h, i] = sc
            mref[h] = fold(sc)

        def scores(j, c2):
            kk = dfused[pl.ds(aligned(QB * j, QB), QB), 128:256]
            for h in range(2):
                sc = dot_nt(qh[h], kk)
                sbuf[h, j] = sc
                mref[h] = jnp.maximum(mref[h], fold(sc))
            return c2

        lax.fori_loop(0, i, scores, 0)
        for h in range(2):
            mref[h] = jnp.broadcast_to(jnp.max(mref[h], axis=1, keepdims=True), (QB, 128))
            acc[h] = jnp.zeros((QB, 256), F32)

        def weigh(j, c2):
            vj = jnp.concatenate([dfused[pl.ds(aligned(QB * j, QB), QB), 256:], ones], axis=1)
            for h in range(2):
                pj = jnp.exp(sbuf[h, j] - wide(mref[h])).astype(BF16)
                acc[h] = acc[h] + dot(pj, vj)
            return c2

        lax.fori_loop(0, i + 1, weigh, 0)
        o_s[pl.ds(at, QB), :] = jnp.where(
            lane_q, acc[0][:, :128] / acc[0][:, 128:], acc[1][:, :128] / acc[1][:, 128:]
        ).astype(BF16)
        lse[pl.ds(at, QB), :] = jnp.where(
            lane_q, mref[0] + jnp.log(acc[0][:, 128:]), mref[1] + jnp.log(acc[1][:, 128:])
        )

        @pl.when(i == 1)
        def _():
            z_forward(2)

        @pl.when(i == 1)
        def _():
            ag_arrived(1, 1)
            ag_start(1, 5)
            ag_start(1, 3)
            ag_arrived(1, 2)
            ag_start(1, 6)
            ag_start(1, 4)
        return carry

    lax.fori_loop(0, NP // 2, attend_step, 0)
    z_forward(1)
    ag_arrived(1, 6)
    ag_start(1, 7)
    ag_arrived(1, 5)
    ag_start(1, 8)

    dkt[...] = jnp.zeros_like(dkt)
    dvt[...] = jnp.zeros_like(dvt)

    def attend_back(i):
        at = aligned(QB * i, QB)
        qi = dfused[pl.ds(at, QB), :128]
        doi = do_s[pl.ds(at, QB), :]
        dof = doi.astype(F32)
        qh = by_head(qi)
        doh = by_head(doi)
        qt = jnp.transpose(qi.astype(F32)).astype(BF16)
        dot_t = jnp.transpose(dof).astype(BF16)
        parts = by_head(dof * o_s[pl.ds(at, QB), :].astype(F32))
        for h in range(2):
            mref[h] = jnp.broadcast_to(jnp.sum(parts[h], axis=1, keepdims=True), (QB, 128))
            acc[h, :, :128] = jnp.broadcast_to(lse[pl.ds(at, QB), HD * h : HD * h + 1], (QB, 128))
            acc[h, :, 128:] = jnp.zeros((QB, 128), F32)

        def unit(j, mask):
            ja = aligned(QB * j, QB)
            kk = dfused[pl.ds(ja, QB), 128:256]
            vj = dfused[pl.ds(ja, QB), 256:]
            for h in range(2):
                hs = slice(HD * h, HD * (h + 1))
                p = jnp.exp(dot_nt(qh[h], kk) - wide(acc[h, :, :128]))
                if mask is not None:
                    p = jnp.where(mask, 0.0, p)
                ds = (p * (dot_nt(doh[h], vj) - wide(mref[h]))).astype(BF16)
                acc[h, :, 128:] = acc[h, :, 128:] + dot(ds, kk)
                dkt[hs, pl.ds(ja, QB)] = dkt[hs, pl.ds(ja, QB)] + dot(qt[hs, :], ds)
                dvt[hs, pl.ds(ja, QB)] = dvt[hs, pl.ds(ja, QB)] + dot(dot_t[hs, :], p.astype(BF16))

        def free(j, c2):
            unit(j, None)
            return c2

        lax.fori_loop(0, i, free, 0)
        unit(i, hidden())
        for part in range(2):
            piece = slice(rows * part, rows * (part + 1))
            dq = jnp.where(low_head, acc[0, piece, 128:], acc[1, piece, 128:]) * HD**-0.5
            dfused[pl.ds(aligned(at + rows * part, rows), rows), :128] = turn(dq, angles(2 * i + part), True).astype(BF16)

    GVIEW = (
        lambda b: gin.at[pl.ds(aligned(256 * b, 256), 256)],
        lambda b: gexp.at[pl.ds(aligned(256 * b, 256), 256)],
        lambda b: gred.at[pl.ds(aligned(128 * b, 128), 128)],
        lambda b: gz.at[b],
    )
    RZ = (rz_in, rz_exp, rz_red, rz_out)
    COMB = ((0, 1, 3), (3, 2, 0))

    def zr_direct(dest):
        ok = d != dest
        if dest == 3:
            ok = ok & (d != 0) & (d != 1)
        if dest == 0:
            ok = ok & (d != 3) & (d != 2)
        return ok

    def zr_copy(a, src_block, dest, slot, sem):
        return rc(GVIEW[a](src_block), RZ[a].at[slot], zr_s.at[a], zr_r.at[a, slot], dest, s)

    def zr_first(a):
        for src, via, dest in COMB:
            @pl.when(d == src)
            def _():
                zr_copy(a, dest, via, via, dest).start()

    def zr_send(a):
        for dest in (3, 0, 2, 1):
            @pl.when(zr_direct(dest))
            def _():
                zr_copy(a, dest, dest, d, dest).start()

    def zr_join(a):
        for src, via, dest in COMB:
            @pl.when(d == via)
            def _():
                zr_copy(a, dest, dest, d, dest).wait_recv()
                ref = GVIEW[a](dest)
                ref[...] = (ref[...].astype(F32) + RZ[a][via].astype(F32)).astype(BF16)
                zr_copy(a, dest, dest, d, dest).start()

    def zr_total(a):
        ref = GVIEW[a](d)
        for src in range(NZ):
            came = d != src
            if src == 0:
                came = came & (d != 3)
            if src == 3:
                came = came & (d != 0)

            @pl.when(came)
            def _():
                zr_copy(a, d, d, src, src).wait_recv()
        use = []
        for src in range(NZ):
            came = d != src
            if src == 0:
                came = came & (d != 3)
            if src == 3:
                came = came & (d != 0)
            use.append(came)
        return ref, use

    def zr_sum(a, use, base, at, n):
        total = base
        for src in range(NZ):
            piece = RZ[a][src, pl.ds(at, n), :].astype(F32)
            total = total + jnp.where(use[src], piece, 0.0)
        return total

    def zr_sent(a):
        whole = (gin, gexp, gred, gz)[a]
        bundle(whole.at[pl.ds(0, whole.shape[0] // 4 * 3)], zr_s.at[a], zr_r.at[a, 0]).wait_send()

    def dest_send(a, dest):
        for src, via, to in COMB:
            if to == dest:
                @pl.when(d == src)
                def _():
                    zr_copy(a, to, via, via, to).start()

        @pl.when(zr_direct(dest))
        def _():
            zr_copy(a, dest, dest, d, dest).start()

    for i in (0, 3, 4, 7, 8):
        ag_arrived(1, i)
    wo_group = bundle(wz.at[pl.ds(1, 3)], wo_s.at[0], wo_r.at[0])
    wo_group.wait_recv()

    def loop(n, f):
        def step(i, carry):
            f(i)
            return carry
        lax.fori_loop(0, n, step, 0)

    def do_block(b):
        at = aligned(4 * rows * b, 4 * rows)
        do_s[pl.ds(at, 4 * rows), :] = dot_nt(dyg[pl.ds(at, 4 * rows), :], wout[...]).astype(BF16)

    loop(NP // 4, do_block)
    gout[...] = dot_tn(o_s[...], dyg[...]).astype(BF16)

    def go_copy(m, incoming):
        t4 = lax.rem(peer(m), 4)
        src = gout.at[pl.ds(aligned(32 * t4, 32), 32)]
        dst = gz.at[t4 if incoming else quad]
        return rc(src, dst, go_s.at[0], go_r.at[0], d, peer(m))

    for m in range(1, 4):
        go_copy(m, False).start()
    gz[quad] = gout[pl.ds(aligned(32 * quad, 32), 32), :]
    early = 1

    def back_early(step):
        attend_back(NP // 2 - 1 - step)

    loop(early, back_early)
    go_group = bundle(gz.at[pl.ds(1, 3)], go_s.at[0], go_r.at[0])
    go_group.wait_recv()
    for dest in (3, 0, 2, 1):
        dest_send(3, dest)
    z_arrived(1)
    z_arrived(2)

    for dd in range(NZ):
        ebs[:, 128 * dd : 128 * (dd + 1)] = jnp.broadcast_to(vt[s, dd, 3:4, :], (8, 128))
    geb[...] = jnp.zeros_like(geb)
    sums[...] = jnp.zeros_like(sums)
    sums[2:3, :] = jnp.sum(dyg[pl.ds(aligned(rows * s, rows), rows), :].astype(F32), axis=0, keepdims=True)

    def ffn_block(b):
        at = pl.ds(aligned(rows * b, rows), rows)
        e = dot(xn[at, :], wexp[...]) + ebs[0:1, :]
        up = dot_nt(dyg[at, :], wred[...])
        a, slope = gelu_pair(e)
        act_s[at, :] = a.astype(BF16)
        de = (up * slope).astype(BF16)
        de_s[at, :] = de
        geb[...] = geb[...] + jnp.sum(de.astype(F32).reshape(rows // 8, 8, 4 * 128), axis=0)

    loop(NP, ffn_block)

    def gexp_block(b):
        at = aligned(256 * b, 256)
        gexp[pl.ds(at, 256), :] = dot_tn(xn[:, pl.ds(at, 256)], de_s[...]).astype(BF16)

    def gred_pair(one, two):
        left = jnp.concatenate(
            [act_s[:, 128 * one : 128 * (one + 1)], act_s[:, 128 * two : 128 * (two + 1)]], axis=1
        )
        both = dot_tn(left, dyg[...]).astype(BF16)
        gred[128 * one : 128 * (one + 1), :] = both[:128]
        gred[128 * two : 128 * (two + 1), :] = both[128:]

    for pair in ((3, 0), (2, 1)):
        gred_pair(*pair)
        for dest in pair:
            dest_send(2, dest)

    ag_sent(0)

    def chip_rows(m):
        return aligned(2 * rows * lax.div(peer(m), 2), 2 * rows)

    def out_block(m):
        at = pl.ds(chip_rows(m), 2 * rows)
        for c in range(0, D, D // 2):
            cols = slice(c, c + D // 2)
            pout[at, cols] = (dot(o_s[at, :], wout[:, cols]) + dot(act_s[at, :], wred[:, cols])).astype(BF16)

    def dn_block(m):
        at = pl.ds(chip_rows(m), 2 * rows)
        for c in range(0, D, D // 2):
            cols = slice(c, c + D // 2)
            dn = dot_nt(de_s[at, :], wexp[cols, :]) + dot_nt(dfused[at, :], win[cols, :])
            pdn[at, cols] = dn.astype(BF16)
            sums[0:1, cols] = sums[0:1, cols] + jnp.sum(dn * xn[at, cols].astype(F32), axis=0, keepdims=True)
            sums[1:2, cols] = sums[1:2, cols] + jnp.sum(dn, axis=0, keepdims=True)

    RS = ((pout, sib_o, r1_o, r2_o), (pdn, sib_d, r1_d, r2_d))

    def part(which, m, lo, n):
        return RS[which][0].at[pl.ds(aligned(rows * peer(m) + lo, half), n)]

    RSM = (
        (1, 7, 0, rows, lambda w: RS[w][1].at[0]),
        (1, 3, 0, rows, lambda w: RS[w][1].at[1]),
        (1, 5, 0, rows, lambda w: RS[w][1].at[2]),
        (1, 1, 0, rows, lambda w: RS[w][1].at[3]),
        (2, 6, 0, half, lambda w: RS[w][2].at[0]),
        (4, 6, half, half, lambda w: RS[w][2].at[1]),
        (2, 2, 0, half, lambda w: RS[w][3].at[0, pl.ds(0, half)]),
        (4, 4, half, half, lambda w: RS[w][3].at[1, pl.ds(half, half)]),
        (2, 2, half, half, lambda w: RS[w][3].at[0, pl.ds(half, half)]),
        (4, 4, 0, half, lambda w: RS[w][3].at[1, pl.ds(0, half)]),
    )

    def rs_copy(w, i):
        to, blk, lo, n, land = RSM[i]
        return rc(part(w, blk, lo, n), land(w), rs_s.at[w], rs_r.at[w, i], d, peer(to))

    def add_into(w, m, lo, n, came):
        def step(c):
            ref = RS[w][0].at[pl.ds(aligned(rows * peer(m) + lo + 64 * c, 64), 64)]
            ref[...] = (ref[...].astype(F32) + came[pl.ds(aligned(64 * c, 64), 64), :].astype(F32)).astype(BF16)
        loop(n // 64, step)

    def rs_across(w):
        rs_copy(w, 0).wait_recv()
        add_into(w, 6, 0, rows, RS[w][1].at[0])
        rs_copy(w, 4).start()
        rs_copy(w, 5).start()

    def rs_pair(w, which):
        rs_copy(w, 1 + which).wait_recv()
        add_into(w, (2, 4)[which], 0, rows, RS[w][1].at[1 + which])
        rs_copy(w, 6 + which).start()

    def rs_near(w, which):
        rs_copy(w, 5 - which).wait_recv()
        add_into(w, (2, 4)[which], (half, 0)[which], half, RS[w][2].at[1 - which])
        rs_copy(w, 8 + which).start()

    def rs_last(w):
        for i in (3, 6, 7, 8, 9):
            rs_copy(w, i).wait_recv()

    for i, m in enumerate((7, 3)):
        out_block(m)
        rs_copy(0, i).start()
    for dest in (3, 0, 2, 1):
        gexp_block(dest)
        dest_send(1, dest)
    for i, m in ((2, 5), (3, 1)):
        out_block(m)
        rs_copy(0, i).start()

    def back_step(step):
        attend_back(NP // 2 - 1 - early - step)

        @pl.when(step == 0)
        def _():
            rs_across(0)
            zr_join(2)
            rs_pair(0, 0)
            rs_pair(0, 1)

        @pl.when(step == 1)
        def _():
            zr_join(3)
            rs_near(0, 0)
            rs_near(0, 1)

        @pl.when(step == 2)
        def _():
            zr_join(1)

    loop(NP // 2 - early, back_step)

    def kv_block(b):
        at = aligned(rows * b, rows)
        dk = jnp.transpose(dkt[:, pl.ds(at, rows)])
        dv = jnp.transpose(dvt[:, pl.ds(at, rows)].astype(BF16))
        dfused[pl.ds(at, rows), 128:256] = turn(dk, angles(b), True).astype(BF16)
        dfused[pl.ds(at, rows), 256:] = dv

    loop(NP, kv_block)

    def gin_block(b):
        at = aligned(256 * b, 256)
        gin[pl.ds(at, 256), :] = dot_tn(xn[:, pl.ds(at, 256)], dfused[...]).astype(BF16)

    for i, m in enumerate((7, 3, 5)):
        dn_block(m)
        rs_copy(1, i).start()
    rs_across(1)
    for dest in (3, 0):
        gin_block(dest)
        dest_send(0, dest)
    dn_block(1)
    rs_copy(1, 3).start()
    for yy in range(2):
        for dd in range(NZ):
            group = 2 * dd + yy
            sv[yy, dd] = sums[:, 128 * group : 128 * (group + 1)]

    def sp_copy(m):
        return rc(sv.at[lax.div(peer(m), 4)], rv.at[m], sp_s.at[0], sp_r.at[0], d, peer(m))

    for m in range(1, NP):
        sp_copy(m).start()
    rs_pair(1, 0)
    rs_pair(1, 1)
    for dest in (2, 1):
        gin_block(dest)
        dest_send(0, dest)
    zr_join(0)
    rs_near(1, 0)
    rs_near(1, 1)
    geb_row = jnp.sum(geb[...], axis=0, keepdims=True)
    sp_group = bundle(rv.at[pl.ds(1, NP - 1)], sp_s.at[0], sp_r.at[0])
    sp_group.wait_recv()
    tiles = sv[ybit]
    for m in range(1, NP):
        tiles = tiles + rv[m]
    for dd in range(NZ):
        ebt = jnp.broadcast_to(geb_row[:, 128 * dd : 128 * (dd + 1)], (8, 128))
        zt[dd] = jnp.where(rows8 == 3, ebt, tiles[dd])

    def sz_copy(i, incoming):
        return rc(zt.at[other(i)], rzv.at[i], sz_s.at[0], sz_r.at[0], other(i), s)

    for i in range(1, NZ):
        sz_copy(i, False).start()

    def total_rows(a, n):
        ref, use = zr_total(a)

        def step(c):
            at = aligned(32 * c, 32)
            block = ref.at[pl.ds(at, 32)]
            block[...] = zr_sum(a, use, block[...].astype(F32), at, 32).astype(BF16)
        loop(n // 32, step)

    def back_copy(which, m, incoming):
        src = (gin, gexp)[which].at[pl.ds(aligned(256 * d + 32 * peer(m), 32), 32)]
        dst = (rb_in, rb_exp)[which].at[m]
        return rc(src, dst, b_s.at[which], b_r.at[which], d, peer(m))

    def back_group(which):
        return bundle((rb_in, rb_exp)[which].at[pl.ds(1, NP - 1)], b_s.at[which], b_r.at[which])

    total_rows(1, 256)
    for m in range(1, NP):
        back_copy(1, m, False).start()

    ref_r, use_r = zr_total(2)

    def red_total(c):
        at = aligned(32 * c, 32)
        tred_ref[pl.ds(at, 32), :] = zr_sum(2, use_r, ref_r[pl.ds(at, 32), :].astype(F32), at, 32)
    loop(4, red_total)
    mine = pl.ds(aligned(256 * d + 32 * s, 32), 32)
    leaving = []

    def leave(src, dst):
        out = pltpu.make_async_copy(src, dst, out_sem.at[len(leaving)])
        out.start()
        leaving.append(out)

    leave(tred_ref, tred_out)
    leave(gexp.at[mine], exp_out.at[0])
    rs_last(0)

    def out_final(c):
        at = aligned(32 * c, 32)
        hout_ref[pl.ds(at, 32), :] = (
            x_ref[pl.ds(at, 32), :].astype(F32) + rs_total32(0, c) + vecs[2:3, :]
        ).astype(BF16)

    def rs_total32(w, c):
        at = aligned(32 * c, 32)
        own = RS[w][0][pl.ds(aligned(rows * s + 32 * c, 32), 32), :].astype(F32)
        own = own + RS[w][1][3, pl.ds(at, 32), :].astype(F32)
        own = own + RS[w][3][0, pl.ds(at, 32), :].astype(F32)
        return own + RS[w][3][1, pl.ds(at, 32), :].astype(F32)

    loop(rows // 32, out_final)
    leave(hout_ref, hout_out)
    def grad_final(c):
        at = aligned(32 * c, 32)
        dn = rs_total32(1, c)
        unit, inv = unit_of(x_ref[pl.ds(at, 32), :])
        dyf = dyg[pl.ds(aligned(rows * s + 32 * c, 32), 32), :].astype(F32)
        g = dn * vecs[0:1, :]
        hg = inv * (
            g - jnp.mean(g, axis=1, keepdims=True) - unit * jnp.mean(g * unit, axis=1, keepdims=True)
        ) + dyf
        hgrad_ref[pl.ds(at, 32), :] = hg.astype(BF16)

    total_rows(0, 256)
    for m in range(1, NP):
        back_copy(0, m, False).start()
    rs_last(1)
    leave(gin.at[mine], in_out.at[0])
    loop(rows // 32, grad_final)
    leave(hgrad_ref, hgrad_out)
    ref_o, use_o = zr_total(3)
    tout_ref[...] = zr_sum(3, use_o, ref_o[...].astype(F32), 0, 32)

    leave(tout_ref, tout_out)
    back_group(1).wait_recv()
    leave(rb_exp.at[pl.ds(1, NP - 1)], exp_out.at[pl.ds(1, NP - 1)])
    back_group(0).wait_recv()
    leave(rb_in.at[pl.ds(1, NP - 1)], in_out.at[pl.ds(1, NP - 1)])
    sz_group = bundle(rzv.at[pl.ds(1, NZ - 1)], sz_s.at[0], sz_r.at[0])
    sz_group.wait_recv()
    tile = zt[d]
    for i in range(1, NZ):
        tile = tile + rzv[i]
    tile_ref[...] = jnp.where(rows8 == 3, tile, pltpu.roll(tile, lax.rem(128 - 32 * quad, 128), 1))

    for out in leaving:
        out.wait()
    for w in range(2):
        a2a_group(w).wait_send()
        back_group(w).wait_send()
    for g in (vz_group, vp_group, wo_group, go_group, sp_group, sz_group):
        g.wait_send()
    ag_sent(1)
    for w in range(2):
        bundle(RS[w][0].at[pl.ds(0, 7 * rows)], rs_s.at[w], rs_r.at[w, 0]).wait_send()
    for a in range(4):
        z_sent(a)
        zr_sent(a)


def update_kernel(*refs):
    weights, moments = refs[0:8], refs[8:16]
    rate_ref, decay_ref, hout_in, hgrad_in, gin, gexp, gred, gout, tile = refs[16:25]
    hout, hgrad = refs[25:27]
    new_moments, new_weights = refs[27:35], refs[35:43]
    s = lax.axis_index("seq")
    keep = 1.0 - decay_ref[0]
    rate = rate_ref[0]

    def update(k, index, grad):
        moment = 0.5 * moments[k][index] + grad * (0.5 / NZ)
        new_moments[k][index] = moment
        new_weights[k][index] = keep * weights[k][index] - rate * moment

    hout[...] = hout_in[...]
    hgrad[...] = hgrad_in[...]
    gain = weights[0][...].astype(BF16).astype(F32)
    shift = weights[1][...].astype(BF16).astype(F32)
    shift_grad = tile[1:2, :32]
    update(0, ..., (tile[0:1, :32] - shift * shift_grad) / gain)
    update(1, ..., shift_grad)
    update(7, ..., tile[2:3, :32])
    update(5, ..., tile[3:4, :])
    update(6, ..., gred[...])
    update(3, ..., gout[...])
    core = lax.rem(s, 2)
    xbit = lax.rem(lax.div(s, 2), 2)
    ybit = lax.div(s, 4)
    for m in range(NP):
        t = s
        if m & 1:
            t = t + (1 - 2 * core)
        if m & 2:
            t = t + 2 * (1 - 2 * xbit)
        if m & 4:
            t = t + 4 * (1 - 2 * ybit)
        pair = 2 * lax.rem(t, 4) + lax.div(t, 4)
        for part in range(3):
            cols = pl.ds(aligned(128 * pair + 1024 * part, 128), 128)
            update(2, (slice(None), cols), gin[m, :, 128 * part : 128 * (part + 1)].astype(F32))
        for e in range(NZ):
            cols = pl.ds(aligned(128 * (8 * e + t), 128), 128)
            update(4, (slice(None), cols), gexp[m, :, 128 * e : 128 * (e + 1)].astype(F32))


def fused_shards(*args):
    (hidden_in, out_cotangent), weights, moments = args[:2], args[2:10], args[10:18]
    rows = hidden_in.shape[1]
    seq = rows * NP
    freq = 10000.0 ** (-2.0 * np.arange(ROT // 2) / ROT)
    lane_freq = np.tile(freq, 128 // (ROT // 2))[None, :]
    near = np.arange(rows)[:, None] * lane_freq
    far = (rows * np.arange(NP))[:, None] * lane_freq
    tables = [jnp.asarray(f(a), F32) for a in (near, far) for f in (np.cos, np.sin)]

    def flat(v):
        return v.reshape(1, -1) if v.ndim == 1 else v

    shards_in = [flat(w) for w in weights]
    ff = weights[6].shape[0] * NZ
    moments_in = [flat(m) for m in moments]
    shard_shapes = [jax.ShapeDtypeStruct(w.shape, F32) for w in shards_in]
    vm = pltpu.VMEM
    dma = pltpu.SemaphoreType.DMA
    scratch = [
        vm((seq, D), BF16), vm((seq, D), BF16), vm((seq, D), BF16),
        vm((D, 384), BF16), vm((D, ff), BF16), vm((ff, D), BF16), vm((128, D), BF16), vm((NZ, 32, D), BF16),
        vm((NP, 32, 384), BF16), vm((NP, 32, ff), BF16),
        vm((seq, 128), BF16), vm((seq, 128), BF16),
        vm((128, seq), F32), vm((128, seq), F32), vm((seq, 384), BF16),
        vm((2, NP // 2, 2 * rows, 2 * rows), F32), vm((seq, 128), F32),
        vm((2, 2 * rows, 128), F32), vm((2, 2 * rows, 256), F32),
        vm((seq, ff), BF16), vm((seq, ff), BF16), vm((seq, D), BF16),
        vm((4, rows, D), BF16), vm((4, rows, D), BF16),
        vm((2, rows // 2, D), BF16), vm((2, rows, D), BF16), vm((2, rows // 2, D), BF16), vm((2, rows, D), BF16),
        vm((D, 384), BF16), vm((D, ff), BF16), vm((ff, D), BF16), vm((128, D), BF16), vm((NZ, 32, D), BF16),
        vm((NZ, 256, 384), BF16), vm((NZ, 256, ff), BF16), vm((NZ, 128, D), BF16), vm((NZ, 32, D), BF16),
        vm((NP, 32, 384), BF16), vm((NP, 32, ff), BF16),
        vm((NP, NZ, 8, 128), F32), vm((8, D), F32), vm((8, ff), F32), vm((8, ff), F32), vm((8, D), F32),
        vm((2, NZ, 8, 128), F32), vm((NP, NZ, 8, 128), F32), vm((NZ, 8, 128), F32), vm((NZ, 8, 128), F32),
        dma((2,)), dma((2,)), dma((2,)), dma((2, 9)), dma((4,)), dma((4, 4)),
        dma((1,)), dma((1,)), dma((1,)), dma((1,)), dma((1,)), dma((1,)),
        dma((2,)), dma((2, 10)), dma((4,)), dma((4, 4)), dma((1,)), dma((1,)),
        dma((2,)), dma((2,)), dma((1,)), dma((1,)), dma((1,)), dma((1,)), dma,
        vm((rows, D), BF16), vm((rows, D), BF16), vm((128, D), F32), vm((32, D), F32), dma((8,)),
    ]
    in_vmem = pl.BlockSpec(memory_space=pltpu.VMEM)
    in_smem = pl.BlockSpec(memory_space=pltpu.SMEM)

    def body(*refs):
        block_kernel(rows, *refs)

    rows_shape = jax.ShapeDtypeStruct((rows, D), BF16)
    grads = pl.pallas_call(
        body,
        out_shape=[
            rows_shape, rows_shape,
            jax.ShapeDtypeStruct((NP, 32, 384), BF16), jax.ShapeDtypeStruct((NP, 32, ff), BF16),
            jax.ShapeDtypeStruct((128, D), F32), jax.ShapeDtypeStruct((32, D), F32),
            jax.ShapeDtypeStruct((8, 128), F32),
        ],
        in_specs=[in_vmem, pl.BlockSpec(memory_space=pl.ANY)] + [in_vmem] * 12,
        out_specs=[pl.BlockSpec(memory_space=pl.ANY)] * 6 + [in_vmem],
        scratch_shapes=scratch,
        compiler_params=pltpu.CompilerParams(
            collective_id=0, has_side_effects=True, vmem_limit_bytes=63 * 2**20
        ),
        name="block_step",
    )(
        hidden_in.reshape(rows, D), out_cotangent.reshape(rows, D), *shards_in, *tables,
    )
    outs = pl.pallas_call(
        update_kernel,
        out_shape=[rows_shape, rows_shape] + shard_shapes + shard_shapes,
        in_specs=[in_vmem] * 16 + [in_smem] * 2 + [in_vmem] * 7,
        out_specs=[in_vmem] * 18,
        compiler_params=pltpu.CompilerParams(vmem_limit_bytes=63 * 2**20),
        name="block_update",
    )(*shards_in, *moments_in, args[18], args[19], *grads)
    small = [w.shape for w in weights]
    return (
        outs[0].reshape(hidden_in.shape),
        outs[1].reshape(hidden_in.shape),
        *[o.reshape(sh) for o, sh in zip(outs[2:], small + small)],
    )


def fits(mesh):
    return mesh.shape["dp"] == NZ and mesh.shape["seq"] == NP


def solution(mesh):
    placed = (
        P("dp", "seq", None),
        P("dp", "seq", None),
        P(("dp", "seq")),
        P(("dp", "seq")),
        P(("dp", "seq"), None),
        P(("dp", "seq"), None),
        P(("dp", "seq"), None),
        P(("dp", "seq")),
        P(("dp", "seq"), None),
        P(("dp", "seq")),
        P(("dp", "seq")),
        P(("dp", "seq")),
        P(("dp", "seq"), None),
        P(("dp", "seq"), None),
        P(("dp", "seq"), None),
        P(("dp", "seq")),
        P(("dp", "seq"), None),
        P(("dp", "seq")),
        P(),
        P(),
    )
    return jax.shard_map(
        fused_shards if fits(mesh) else shards,
        mesh=mesh,
        in_specs=placed,
        out_specs=(
            P("dp", "seq", None),
            P("dp", "seq", None),
            P(("dp", "seq")),
            P(("dp", "seq")),
            P(("dp", "seq"), None),
            P(("dp", "seq"), None),
            P(("dp", "seq"), None),
            P(("dp", "seq")),
            P(("dp", "seq"), None),
            P(("dp", "seq")),
            P(("dp", "seq")),
            P(("dp", "seq")),
            P(("dp", "seq"), None),
            P(("dp", "seq"), None),
            P(("dp", "seq"), None),
            P(("dp", "seq")),
            P(("dp", "seq"), None),
            P(("dp", "seq")),
        ),
        check_vma=False,
    )
```
